256 devices in a mesh: img: 16 (over z, core), txt: 16 (over x, y).
Axes of the slice: x: 4, y: 4, z: 8, core: 2. Of those that a mesh axis runs over, the one named last changes fastest.
Arguments:
- teacher_img: bfloat16 [16384, 1280], P('img'), may hold values from -40 to 40
- teacher_txt: bfloat16 [16384, 1280], P('txt'), may hold values from -40 to 40
- student_img: bfloat16 [16384, 512], P('img'), may hold values from -40 to 40
- student_txt: bfloat16 [16384, 512], P('txt'), may hold values from -40 to 40
Outputs:
- loss: float32 [], replicated
- grad_img: float32 [16384, 512], P(('img', 'txt'))
- grad_txt: float32 [16384, 512], P(('txt', 'img'))
The draws below stay inside these ranges and needn't reach their ends.
All inputs are finite; a program needn't handle non-finite values.
Results may differ from the reference program's by a relative error of at most 0.0033.
Values sent between devices are 32-bit elements; how exact they have to be, the bound alone decides.
No kernel may reach another device: no remote copies, remote signals or barrier semaphores. Data moves between devices by JAX's collectives and lax.ppermute only.
A program may use at most 64 MiB of HBM per device.

```python
import math
import jax
import jax.numpy as jnp
from jax import lax

DT = 1280
DS = 512
ROWS = 1024
IMAGES = 16384
TEXTS = 16384


def embed_pair(key, width, marker):
    base = jax.random.fold_in(key, marker)
    keys = jax.random.split(base, 2)
    images = jnp.clip(jax.random.normal(keys[0], (IMAGES, width), jnp.float32), -5.0, 5.0)
    texts = jnp.clip(jax.random.normal(keys[1], (TEXTS, width), jnp.float32), -5.0, 5.0)
    return (images.astype(jnp.bfloat16), texts.astype(jnp.bfloat16))


def draw_teacher_img(key, part):
    return embed_pair(key, DT, 11)[0]


def draw_teacher_txt(key, part):
    return embed_pair(key, DT, 11)[1]


def draw_student_img(key, part):
    return embed_pair(key, DS, 23)[0]


def draw_student_txt(key, part):
    return embed_pair(key, DS, 23)[1]


def setup_inputs(seed: int = 0) -> dict:
    streams_of = jax.random.split(jax.random.key(seed), 5)
    return {
        "teacher_img": draw_teacher_img(jax.random.fold_in(streams_of[4], 71), 0),
        "teacher_txt": draw_teacher_txt(jax.random.fold_in(streams_of[4], 71), 0),
        "student_img": draw_student_img(jax.random.fold_in(streams_of[4], 71), 0),
        "student_txt": draw_student_txt(jax.random.fold_in(streams_of[4], 71), 0),
    }


def logits(left, right, width):
    return 3.0 / math.sqrt(width) * jnp.dot(left, right.T, preferred_element_type=jnp.float32)

def join_pair(peak_one, mass_one, peak_two, mass_two):
    highest = jnp.maximum(peak_one, peak_two)
    return (highest, mass_one * jnp.exp(peak_one - highest) + mass_two * jnp.exp(peak_two - highest))

def reference(teacher_img, teacher_txt, student_img, student_txt):
    blocks = IMAGES // ROWS
    scale_learn = 3.0 / math.sqrt(DS)
    teach_rows = teacher_img.reshape(blocks, ROWS, DT)
    learn_rows = student_img.reshape(blocks, ROWS, DS)

    def first_pass(carry, pieces):
        teach_peak, teach_mass, learn_peak, learn_mass = carry
        teach_block = logits(pieces[0], teacher_txt, DT)
        learn_block = logits(pieces[1], student_txt, DS)
        row_teach = jax.scipy.special.logsumexp(teach_block, axis=1)
        row_learn = jax.scipy.special.logsumexp(learn_block, axis=1)
        block_peak = lax.optimization_barrier(jnp.max(teach_block, axis=0))
        block_mass = lax.optimization_barrier(jnp.sum(jnp.exp(teach_block - block_peak[None, :]), axis=0))
        teach_peak, teach_mass = join_pair(teach_peak, teach_mass, block_peak, block_mass)
        block_peak = lax.optimization_barrier(jnp.max(learn_block, axis=0))
        block_mass = lax.optimization_barrier(jnp.sum(jnp.exp(learn_block - block_peak[None, :]), axis=0))
        learn_peak, learn_mass = join_pair(learn_peak, learn_mass, block_peak, block_mass)
        return ((teach_peak, teach_mass, learn_peak, learn_mass), (row_teach, row_learn))
    lowest = jnp.full((TEXTS,), -jnp.inf, jnp.float32)
    nothing = jnp.zeros((TEXTS,), jnp.float32)
    carry, (row_teach, row_learn) = lax.scan(first_pass, (lowest, nothing, lowest, nothing), (teach_rows, learn_rows))
    col_teach = carry[0] + jnp.log(carry[1])
    col_learn = carry[2] + jnp.log(carry[3])

    def second_pass(carry, pieces):
        grad_text, row_total, col_total = carry
        teach_part, learn_part, teach_norm, learn_norm = pieces
        teach_block = logits(teach_part, teacher_txt, DT)
        learn_block = logits(learn_part, student_txt, DS)
        p_row = jnp.exp(teach_block - teach_norm[:, None])
        q_row = jnp.exp(learn_block - learn_norm[:, None])
        p_col = jnp.exp(teach_block - col_teach[None, :])
        q_col = jnp.exp(learn_block - col_learn[None, :])
        gap = teach_block - learn_block
        row_total = row_total + jnp.sum(p_row * gap) + jnp.sum(learn_norm - teach_norm)
        col_total = col_total + jnp.sum(p_col * gap)
        delta = (8.0 * (q_row - p_row + q_col - p_col)).astype(jnp.bfloat16)
        grad_block = scale_learn * jnp.dot(delta, student_txt, preferred_element_type=jnp.float32)
        grad_text = grad_text + scale_learn * jnp.dot(delta.T, learn_part, preferred_element_type=jnp.float32)
        return ((grad_text, row_total, col_total), grad_block)
    start = (jnp.zeros((TEXTS, DS), jnp.float32), jnp.zeros((), jnp.float32), jnp.zeros((), jnp.float32))
    (grad_txt, row_total, col_total), grad_blocks = lax.scan(second_pass, start, (teach_rows, learn_rows, row_teach, row_learn))
    col_total = col_total + jnp.sum(col_learn - col_teach)
    loss = 0.5 * (row_total / IMAGES + col_total / TEXTS)
    grad_img = grad_blocks.reshape(IMAGES, DS)
    return (loss, grad_img, grad_txt)
```

```python
import math

import jax
import jax.numpy as jnp
from jax import lax
from jax.sharding import Mesh
from jax.sharding import PartitionSpec as P

IMG = ("img_0", "img_1")
TXT = ("txt_0", "txt_1")
IMG_TXT = ("img_0", "img_1", "txt_0", "txt_1")
TXT_IMG = ("txt_0", "txt_1", "img_0", "img_1")


def from_everyone(shard, axis):
    copies = jnp.broadcast_to(shard, (lax.axis_size(axis), *shard.shape))
    return lax.all_to_all(copies, axis, split_axis=0, concat_axis=0, tiled=True)


def local_stats(teacher, student, gap, along):
    teach_peak = jnp.max(teacher, axis=along, keepdims=True)
    learn_peak = jnp.max(student, axis=along, keepdims=True)
    weight = jnp.exp(teacher - teach_peak)
    teach_mass = jnp.sum(weight, axis=along)
    learn_mass = jnp.sum(jnp.exp(student - learn_peak), axis=along)
    gap_sum = jnp.sum(weight * gap, axis=along)
    return jnp.stack(
        [
            jnp.squeeze(teach_peak, along) + jnp.log(teach_mass),
            jnp.squeeze(learn_peak, along) + jnp.log(learn_mass),
            gap_sum / teach_mass,
        ]
    ).reshape(-1, 128)


def joined(parts):
    parts = parts.reshape(parts.shape[0], 3, -1)
    teach, learn, gap = parts[:, 0], parts[:, 1], parts[:, 2]
    teach_peak = jnp.max(teach, axis=0)
    learn_peak = jnp.max(learn, axis=0)
    weight = jnp.exp(teach - teach_peak)
    mass = jnp.sum(weight, axis=0)
    teach_norm = teach_peak + jnp.log(mass)
    learn_norm = learn_peak + jnp.log(jnp.sum(jnp.exp(learn - learn_peak), axis=0))
    gap_mean = jnp.sum(weight * gap, axis=0) / mass
    return teach_norm, learn_norm, jnp.sum(gap_mean + learn_norm - teach_norm)


def step_perm(size, shift):
    return [(k, (k + shift) % size) for k in range(size)]


def body(teacher_img, teacher_txt, student_img, student_txt):
    scale_teach = 3.0 / math.sqrt(teacher_img.shape[1])
    scale_learn = 3.0 / math.sqrt(student_img.shape[1])
    rows = teacher_img.shape[0]
    cols = teacher_txt.shape[0]
    img_count = lax.axis_size(IMG)
    txt_count = lax.axis_size(TXT)
    width = student_img.shape[1]
    teacher = scale_teach * jnp.einsum(
        "id,jd->ij", teacher_img, teacher_txt, preferred_element_type=jnp.float32
    )
    student = scale_learn * jnp.einsum(
        "id,jd->ij", student_img, student_txt, preferred_element_type=jnp.float32
    )
    gap = teacher - student
    row_teach, row_learn, row_loss = joined(
        from_everyone(local_stats(teacher, student, gap, 1), TXT)
    )
    col_teach, col_learn, col_loss = joined(
        from_everyone(local_stats(teacher, student, gap, 0), IMG)
    )
    q_row = jnp.exp(student - row_learn[:, None])
    p_row = jnp.exp(teacher - row_teach[:, None])
    q_col = jnp.exp(student - col_learn[None, :])
    p_col = jnp.exp(teacher - col_teach[None, :])
    delta = (8.0 * (q_row - p_row + q_col - p_col)).astype(jnp.bfloat16)

    def with_note(grad, pieces, note):
        grad = grad.reshape(pieces, -1, width)
        note = jnp.broadcast_to(note, (pieces, 8, width))
        return jnp.concatenate([grad, note], axis=1)

    to_txt = scale_learn * jnp.einsum(
        "ij,id->jd", delta, student_img, preferred_element_type=jnp.float32
    )
    to_txt = with_note(to_txt, img_count, row_loss)
    chips, cores = lax.axis_size("img_0"), lax.axis_size("img_1")
    to_txt = to_txt.reshape(chips, cores, -1, width)
    core = lax.axis_index("img_1")
    kept = lax.dynamic_index_in_dim(to_txt, core, 1, keepdims=False)
    sent = lax.dynamic_index_in_dim(to_txt, 1 - core, 1, keepdims=False)
    both = kept + lax.ppermute(sent, "img_1", step_perm(cores, 1))

    to_img = scale_learn * jnp.dot(delta, student_txt, preferred_element_type=jnp.float32)
    to_img = with_note(to_img, txt_count, col_loss)
    got_img = lax.all_to_all(to_img, TXT, 0, 0, tiled=True)

    place = lax.axis_index("img_0")

    def piece(shift):
        return lax.dynamic_index_in_dim(both, (place + shift) % chips, 0, keepdims=False)

    up, down = piece(chips // 2), piece(1 - chips // 2 + chips)
    for k in range(chips // 2 - 1, -1, -1):
        up = lax.ppermute(up, "img_0", step_perm(chips, 1))
        if k:
            up = up + piece(k)
    for k in range(chips // 2 - 2, -1, -1):
        down = lax.ppermute(down, "img_0", step_perm(chips, -1))
        if k:
            down = down + piece(chips - k)
    got_txt = up + down + piece(0)
    got_img = jnp.sum(got_img, axis=0)
    own = rows // txt_count
    loss = 0.5 * (got_txt[-1, 0] / (rows * img_count) + got_img[-1, 0] / (cols * txt_count))
    return (loss, got_img[:own], got_txt[: cols // img_count])


def solution(mesh):
    torus = Mesh(mesh.devices.reshape(8, 2, 4, 4), ("img_0", "img_1", "txt_0", "txt_1"))
    in_specs = (P(IMG, None), P(TXT, None), P(IMG, None), P(TXT, None))
    out_specs = (P(), P(IMG_TXT, None), P(TXT_IMG, None))
    return jax.shard_map(body, mesh=torus, in_specs=in_specs, out_specs=out_specs, check_vma=False)
```

```python
import functools
import math

import jax
import jax.numpy as jnp
from jax import lax
from jax.experimental import pallas as pl
from jax.experimental.pallas import tpu as pltpu
from jax.sharding import Mesh
from jax.sharding import PartitionSpec as P

IMG = ("img_0", "img_1")
TXT = ("txt_0", "txt_1")
IMG_TXT = ("img_0", "img_1", "txt_0", "txt_1")
TXT_IMG = ("txt_0", "txt_1", "img_0", "img_1")
LANES = 128
NOTE = 8
VMEM_LIMIT = 48 * 1024 * 1024
LN2 = math.log(2.0)
F32 = jnp.float32
WHOLE = pl.BlockSpec(memory_space=pltpu.VMEM)
ANYWHERE = pl.BlockSpec(memory_space=pl.ANY)


def cost(flops, size, transcendentals=0):
    return pl.CostEstimate(flops=flops, bytes_accessed=size, transcendentals=transcendentals)


def stats_kernel(scale_teach, scale_learn, ti_hbm, tt_hbm, si_hbm, st_hbm, t_hbm, s_hbm,
                 row_out, col_out, ti, tt, si, st, t, s, peaks, sums, col_peaks, col_sums, sems):
    loads = [
        pltpu.make_async_copy(src, dst, sems.at[k])
        for k, (src, dst) in enumerate(((st_hbm, st), (si_hbm, si), (tt_hbm, tt), (ti_hbm, ti)))
    ]
    for load in loads:
        load.start()
    rows, cols = t.shape
    wide = 256

    def logits(left, right, out, scale, which):
        @pl.loop(0, cols // wide)
        def _(n):
            at = pl.multiple_of(n * wide, wide)
            block = scale * lax.dot_general(
                left[...], right[pl.ds(at, wide), :], (((1,), (1,)), ((), ())),
                preferred_element_type=F32,
            )
            out[:, pl.ds(at, wide)] = block
            col_peaks[which, :, pl.ds(at, wide)] = jnp.max(
                block.reshape(rows // 8, 8, wide), axis=0
            )
            top = jnp.maximum(block[:, :LANES], block[:, LANES:])

            @pl.when(n == 0)
            def _():
                peaks[which] = top

            @pl.when(n > 0)
            def _():
                peaks[which] = jnp.maximum(peaks[which], top)

        peaks[which] = jnp.broadcast_to(
            jnp.max(peaks[which], axis=1, keepdims=True), (rows, LANES)
        )
        col_peaks[which] = jnp.broadcast_to(
            jnp.max(col_peaks[which], axis=0, keepdims=True), (8, cols)
        )

    loads[0].wait()
    loads[1].wait()
    logits(si, st, s, scale_learn, 1)
    save_s = pltpu.make_async_copy(s, s_hbm, sems.at[4])
    save_s.start()
    loads[2].wait()
    loads[3].wait()
    logits(ti, tt, t, scale_teach, 0)
    save_t = pltpu.make_async_copy(t, t_hbm, sems.at[5])
    save_t.start()

    group = 4 * LANES
    for h in range(cols // group):
        def strip(r, carry):
            at = pl.multiple_of(r * 8, 8)
            down = pl.ds(at, 8)
            row_peak_t, row_peak_s = peaks[0, down, :], peaks[1, down, :]
            row_t = row_s = row_g = None
            new = []
            for k in range(group // LANES):
                across = slice(h * group + k * LANES, h * group + (k + 1) * LANES)
                tv, sv = t[down, across], s[down, across]
                gap = tv - sv
                wr = jnp.exp2(tv - row_peak_t)
                vr = jnp.exp2(sv - row_peak_s)
                wc = jnp.exp2(tv - col_peaks[0, :, across])
                vc = jnp.exp2(sv - col_peaks[1, :, across])
                row_t = wr if row_t is None else row_t + wr
                row_s = vr if row_s is None else row_s + vr
                row_g = wr * gap if row_g is None else row_g + wr * gap
                ct, cs, cg = carry[3 * k : 3 * k + 3]
                new += [ct + wc, cs + vc, cg + wc * gap]
            for q, value in enumerate((row_t, row_s, row_g)):
                if h:
                    value = value + sums[q, down, :]
                sums[q, down, :] = value
            return tuple(new)

        zeros = tuple(jnp.zeros((8, LANES), F32) for _ in range(3 * group // LANES))
        found = lax.fori_loop(0, rows // 8, strip, zeros, unroll=4)
        for k in range(group // LANES):
            across = slice(h * group + k * LANES, h * group + (k + 1) * LANES)
            for q in range(3):
                col_sums[q, :, across] = found[3 * k + q]

    def publish(out, peak_t, peak_s, mass_t, mass_s, gap):
        lse_t = peak_t + jnp.log2(mass_t)
        lse_s = peak_s + jnp.log2(mass_s)
        mean = gap / mass_t
        for q, value in enumerate((lse_t, lse_s, mean)):
            for b in range(value.shape[1] // LANES):
                line = value[:, b * LANES : (b + 1) * LANES]
                for k in range(out.shape[0]):
                    out[k, q * 8 + b : q * 8 + b + 1, :] = line

    publish(
        col_out, col_peaks[0, :1, :], col_peaks[1, :1, :],
        *(jnp.sum(col_sums[q], axis=0, keepdims=True) for q in range(3)),
    )

    def across_lanes(value, weight):
        found = lax.dot_general(
            jnp.full((8, LANES), weight, F32), value, (((1,), (1,)), ((), ())),
            preferred_element_type=F32, precision=lax.Precision.HIGHEST,
        )
        return found[:1]

    publish(
        row_out,
        across_lanes(peaks[0], 1.0 / LANES), across_lanes(peaks[1], 1.0 / LANES),
        *(across_lanes(sums[q], 1.0) for q in range(3)),
    )
    save_s.wait()
    save_t.wait()


def local_stats(teacher_img, teacher_txt, student_img, student_txt, copies):
    rows, deep = teacher_img.shape
    cols, thin = student_txt.shape
    logit = jax.ShapeDtypeStruct((rows, cols), F32)
    kernel = functools.partial(
        stats_kernel, 3.0 / math.sqrt(deep) / LN2, 3.0 / math.sqrt(thin) / LN2
    )
    return pl.pallas_call(
        kernel,
        name="logits_and_statistics",
        out_shape=(
            logit, logit,
            jax.ShapeDtypeStruct((copies[0], 3 * 8, LANES), F32),
            jax.ShapeDtypeStruct((copies[1], 3 * 8, LANES), F32),
        ),
        in_specs=[ANYWHERE] * 4,
        out_specs=(ANYWHERE, ANYWHERE, WHOLE, WHOLE),
        scratch_shapes=[
            pltpu.VMEM((rows, deep), jnp.bfloat16), pltpu.VMEM((cols, deep), jnp.bfloat16),
            pltpu.VMEM((rows, thin), jnp.bfloat16), pltpu.VMEM((cols, thin), jnp.bfloat16),
            pltpu.VMEM((rows, cols), F32), pltpu.VMEM((rows, cols), F32),
            pltpu.VMEM((2, rows, LANES), F32), pltpu.VMEM((3, rows, LANES), F32),
            pltpu.VMEM((2, 8, cols), F32), pltpu.VMEM((3, 8, cols), F32),
            pltpu.SemaphoreType.DMA((6,)),
        ],
        compiler_params=pltpu.CompilerParams(vmem_limit_bytes=VMEM_LIMIT),
        cost_estimate=cost(2 * rows * cols * (deep + thin), 8 * rows * cols, 4 * rows * cols),
    )(teacher_img, teacher_txt, student_img, student_txt)


def joined(stats):
    teach, learn, gap = (stats[:, 8 * q : 8 * q + 8, :] for q in range(3))
    teach_peak = jnp.max(teach, axis=0)
    learn_peak = jnp.max(learn, axis=0)
    weight = jnp.exp2(teach - teach_peak[None])
    mass = jnp.sum(weight, axis=0)
    teach_norm = teach_peak + jnp.log2(mass)
    learn_norm = learn_peak + jnp.log2(jnp.sum(jnp.exp2(learn - learn_peak[None]), axis=0))
    mean = jnp.sum(weight * gap, axis=0) / mass
    return teach_norm, learn_norm, jnp.sum(mean + learn_norm - teach_norm)


def delta_kernel(scale, row_stats, col_stats, t, s, st, delta_out, img_out, note_out,
                 row_norms, col_norms, col_note):
    step = pl.program_id(0)
    tall = t.shape[0]

    @pl.when(step == 0)
    def _():
        for stats, norms, by_row in ((row_stats, row_norms, True), (col_stats, col_norms, False)):
            teach, learn, total = joined(stats[...])
            if by_row:
                note_out[...] = jnp.full(note_out.shape, total, F32)
            else:
                col_note[...] = jnp.full(col_note.shape, total, F32)
            for which, value in enumerate((teach, learn)):
                value = value - 3.0
                if by_row:
                    turned = jnp.concatenate([value] * (LANES // 8), axis=0).T
                for b in range(8):
                    if by_row:
                        norms[which, b * LANES : (b + 1) * LANES, :] = jnp.broadcast_to(
                            turned[:, b : b + 1], (LANES, LANES)
                        )
                    else:
                        norms[which, :, b * LANES : (b + 1) * LANES] = jnp.broadcast_to(
                            value[b : b + 1, :], (16, LANES)
                        )

    base = step * tall

    @pl.loop(0, tall // 16)
    def _(r):
        at = pl.multiple_of(r * 16, 16)
        down = pl.ds(at, 16)
        there = pl.ds(pl.multiple_of(base + at, 16), 16)
        row_t, row_s = row_norms[0, there, :], row_norms[1, there, :]
        for k in range(t.shape[1] // LANES):
            across = slice(k * LANES, (k + 1) * LANES)
            tv, sv = t[down, across], s[down, across]
            value = (
                jnp.exp2(sv - row_s) - jnp.exp2(tv - row_t)
                + jnp.exp2(sv - col_norms[1, :, across]) - jnp.exp2(tv - col_norms[0, :, across])
            )
            delta_out[down, across] = value.astype(jnp.bfloat16)

    grad = scale * jnp.dot(delta_out[...], st[...], preferred_element_type=F32)
    own = (img_out.shape[1] - NOTE) * LANES // st.shape[1]
    for k in range(img_out.shape[0]):
        for b in range(st.shape[1] // LANES):
            img_out[k, b * own : (b + 1) * own, :] = grad[
                k * own : (k + 1) * own, b * LANES : (b + 1) * LANES
            ]
        img_out[k, img_out.shape[1] - NOTE :, :] = col_note[...]


def delta_and_img(row_stats, col_stats, t, s, student_txt):
    rows, cols = t.shape
    thin = student_txt.shape[1]
    pieces = row_stats.shape[0]
    steps = 4
    tall = rows // steps
    lines = rows // pieces * thin // LANES + NOTE
    fixed = lambda shape: pl.BlockSpec(shape, lambda i: (0,) * len(shape))
    return pl.pallas_call(
        functools.partial(delta_kernel, 3.0 / math.sqrt(thin)),
        name="delta_and_image_gradient",
        grid=(steps,),
        out_shape=(
            jax.ShapeDtypeStruct((rows, cols), jnp.bfloat16),
            jax.ShapeDtypeStruct((pieces, lines, LANES), F32),
            jax.ShapeDtypeStruct((NOTE, thin), F32),
        ),
        in_specs=[
            fixed(row_stats.shape), fixed(col_stats.shape),
            pl.BlockSpec((tall, cols), lambda i: (i, 0)),
            pl.BlockSpec((tall, cols), lambda i: (i, 0)),
            fixed(student_txt.shape),
        ],
        out_specs=(
            pl.BlockSpec((tall, cols), lambda i: (i, 0)),
            pl.BlockSpec((pieces // steps, lines, LANES), lambda i: (i, 0, 0)),
            fixed((NOTE, thin)),
        ),
        scratch_shapes=[
            pltpu.VMEM((2, rows, LANES), F32), pltpu.VMEM((2, 16, cols), F32),
            pltpu.VMEM((NOTE, LANES), F32),
        ],
        compiler_params=pltpu.CompilerParams(vmem_limit_bytes=VMEM_LIMIT),
        cost_estimate=cost(2 * rows * cols * thin, 10 * rows * cols, 4 * rows * cols),
    )(row_stats, col_stats, t, s, student_txt)


def txt_kernel(scale, place, delta, si, note, out):
    tall = delta.shape[1]
    out[0, :tall, :] = scale * lax.dot_general(
        delta[...], si[...], (((0,), (0,)), ((), ())), preferred_element_type=F32
    )
    out[0, tall:, :] = note[...]


def txt_gradient(delta, student_img, note, upward, chips):
    rows, cols = delta.shape
    thin = student_img.shape[1]
    tall = cols // chips
    slots = chips // 2

    def dest(g, where):
        flow = where[1]
        up = where[0] + slots - g
        down = where[0] + slots + 1 + g
        return (0, lax.rem(jnp.where(flow == 0, up, down) + chips, chips))

    return pl.pallas_call(
        functools.partial(txt_kernel, 3.0 / math.sqrt(thin)),
        name="text_gradient",
        out_shape=jax.ShapeDtypeStruct((slots, tall + NOTE, thin), F32),
        grid_spec=pltpu.PrefetchScalarGridSpec(
            num_scalar_prefetch=1,
            grid=(slots,),
            in_specs=[
                pl.BlockSpec((rows, tall), dest),
                pl.BlockSpec((rows, thin), lambda g, where: (0, 0)),
                pl.BlockSpec((NOTE, thin), lambda g, where: (0, 0)),
            ],
            out_specs=pl.BlockSpec((1, tall + NOTE, thin), lambda g, where: (g, 0, 0)),
        ),
        compiler_params=pltpu.CompilerParams(vmem_limit_bytes=VMEM_LIMIT),
        cost_estimate=cost(rows * cols * thin, rows * cols * 2 + cols * thin * 2),
    )(upward, delta, student_img, note)


def sum_kernel(parts, out, note):
    own = out.shape[0]
    for b in range(out.shape[1] // LANES):
        total = parts[0, b * own : (b + 1) * own, :]
        for k in range(1, parts.shape[0]):
            total = total + parts[k, b * own : (b + 1) * own, :]
        out[:, b * LANES : (b + 1) * LANES] = total
    last = slice(parts.shape[1] - NOTE, parts.shape[1])
    total = parts[0, last, :]
    for k in range(1, parts.shape[0]):
        total = total + parts[k, last, :]
    note[...] = total


def summed(parts, thin):
    own = (parts.shape[1] - NOTE) * LANES // thin
    return pl.pallas_call(
        sum_kernel,
        name="sum_of_image_parts",
        out_shape=(jax.ShapeDtypeStruct((own, thin), F32), jax.ShapeDtypeStruct((NOTE, LANES), F32)),
        in_specs=[WHOLE],
        out_specs=(WHOLE, WHOLE),
        cost_estimate=cost(parts.size, 4 * parts.size),
    )(parts)


def body(teacher_img, teacher_txt, student_img, student_txt):
    rows, thin = student_img.shape
    cols = student_txt.shape[0]
    chips, cores = lax.axis_size("img_0"), lax.axis_size("img_1")
    img_count, txt_count = chips * cores, lax.axis_size(TXT)
    place, core = lax.axis_index("img_0"), lax.axis_index("img_1")

    t, s, row_stats, col_stats = local_stats(
        teacher_img, teacher_txt, student_img, student_txt, (txt_count, img_count)
    )
    row_stats = lax.all_to_all(row_stats, TXT, 0, 0, tiled=True)
    col_stats = lax.all_to_all(col_stats, IMG, 0, 0, tiled=True)
    delta, to_img, row_note = delta_and_img(row_stats, col_stats, t, s, student_txt)
    got_img = lax.all_to_all(to_img, TXT, 0, 0, tiled=True)

    theirs = txt_gradient(delta, student_img, row_note, jnp.stack([place, 1 - core]), chips)
    mine = txt_gradient(delta, student_img, row_note, jnp.stack([place, core]), chips)
    swap = [(k, 1 - k) for k in range(cores)]
    theirs = lax.ppermute(theirs, "img_1", swap)
    around = [
        (cores * z + c, cores * ((z + 1 - 2 * c) % chips) + c)
        for z in range(chips) for c in range(cores)
    ]
    flow = mine[0] + theirs[0]
    for k in range(1, chips // 2):
        flow = lax.ppermute(flow, IMG, around) + mine[k] + theirs[k]
    last = lax.ppermute(flow, IMG, [pair for pair in around if pair[0] % cores == 0])
    flow = jnp.where(core == 0, last, flow)
    halves = flow[:-NOTE].reshape(cores, -1, thin)
    note = flow[-NOTE:]
    keep = lax.dynamic_index_in_dim(halves, core, 0, keepdims=False)
    give = lax.dynamic_index_in_dim(halves, 1 - core, 0, keepdims=False)
    got = lax.ppermute(jnp.concatenate([give, note], axis=0), "img_1", swap)
    grad_txt = keep + got[:-NOTE]
    row_loss = note[0, 0] + got[-1, 0]

    grad_img, col_note = summed(got_img, thin)
    loss = (0.5 * LN2) * (
        row_loss / (rows * img_count) + col_note[0, 0] / (cols * txt_count)
    )
    return (loss, grad_img, grad_txt)


def solution(mesh):
    torus = Mesh(mesh.devices.reshape(8, 2, 4, 4), ("img_0", "img_1", "txt_0", "txt_1"))
    in_specs = (P(IMG, None), P(TXT, None), P(IMG, None), P(TXT, None))
    out_specs = (P(), P(IMG_TXT, None), P(TXT_IMG, None))
    return jax.shard_map(body, mesh=torus, in_specs=in_specs, out_specs=out_specs, check_vma=False)
```

```python
import functools
import math

import jax
import jax.numpy as jnp
from jax import lax
from jax.experimental import pallas as pl
from jax.experimental.pallas import tpu as pltpu
from jax.sharding import Mesh
from jax.sharding import PartitionSpec as P

IMG = ("img_0", "img_1")
TXT = ("txt_0", "txt_1")
IMG_TXT = ("img_0", "img_1", "txt_0", "txt_1")
TXT_IMG = ("txt_0", "txt_1", "img_0", "img_1")
LANES = 128
NOTE = 8
VMEM_LIMIT = 40 * 1024 * 1024
STATS_LIMIT = 54 * 1024 * 1024
LN2 = math.log(2.0)
F32 = jnp.float32
WHOLE = pl.BlockSpec(memory_space=pltpu.VMEM)
ANYWHERE = pl.BlockSpec(memory_space=pl.ANY)


def cost(flops, size, transcendentals=0):
    return pl.CostEstimate(flops=flops, bytes_accessed=size, transcendentals=transcendentals)


def stats_kernel(scale_teach, scale_learn, ti_hbm, tt_hbm, si_hbm, st_hbm, t, s, row_out, col_out,
                 ti, tt, si, st, peaks, sums, col_peaks, col_sums, sems):
    rows, cols = t.shape
    tall = 256
    chunks = rows // tall

    def load(src, dst, at, size, which):
        copy = pltpu.make_async_copy(
            src.at[pl.ds(at, size), :], dst.at[pl.ds(at, size), :], sems.at[which]
        )
        copy.start()
        return copy

    tt_load = load(tt_hbm, tt, 0, cols, 0)
    ti_loads = [load(ti_hbm, ti, n * tall, tall, 1 + n) for n in range(chunks)]
    st_load = load(st_hbm, st, 0, cols, 1 + chunks)
    si_load = load(si_hbm, si, 0, rows, 2 + chunks)

    def logits(left, right, out, scale, which, arrivals):
        for n in range(chunks):
            if arrivals:
                arrivals[n].wait()
            down = slice(n * tall, (n + 1) * tall)
            block = scale * lax.dot_general(
                left[down, :], right[...], (((1,), (1,)), ((), ())), preferred_element_type=F32
            )
            out[down, :] = block
            top = jnp.max(block.reshape(tall // 8, 8, cols), axis=0)
            col_peaks[which] = jnp.maximum(col_peaks[which], top) if n else top
            side = block[:, :LANES]
            for k in range(1, cols // LANES):
                side = jnp.maximum(side, block[:, k * LANES : (k + 1) * LANES])
            peaks[which, down, :] = jnp.broadcast_to(
                jnp.max(side, axis=1, keepdims=True), (tall, LANES)
            )
        col_peaks[which] = jnp.broadcast_to(
            jnp.max(col_peaks[which], axis=0, keepdims=True), (8, cols)
        )

    tt_load.wait()
    logits(ti, tt, t, scale_teach, 0, ti_loads)
    st_load.wait()
    si_load.wait()
    logits(si, st, s, scale_learn, 1, None)

    group = 4 * LANES
    for h in range(cols // group):
        def strip(r, carry):
            at = pl.multiple_of(r * 8, 8)
            down = pl.ds(at, 8)
            row_peak_t, row_peak_s = peaks[0, down, :], peaks[1, down, :]
            row_t = row_s = row_g = None
            new = []
            for k in range(group // LANES):
                across = slice(h * group + k * LANES, h * group + (k + 1) * LANES)
                tv, sv = t[down, across], s[down, across]
                gap = tv - sv
                wr = jnp.exp2(tv - row_peak_t)
                vr = jnp.exp2(sv - row_peak_s)
                wc = jnp.exp2(tv - col_peaks[0, :, across])
                vc = jnp.exp2(sv - col_peaks[1, :, across])
                row_t = wr if row_t is None else row_t + wr
                row_s = vr if row_s is None else row_s + vr
                row_g = wr * gap if row_g is None else row_g + wr * gap
                ct, cs, cg = carry[3 * k : 3 * k + 3]
                new += [ct + wc, cs + vc, cg + wc * gap]
            for q, value in enumerate((row_t, row_s, row_g)):
                if h:
                    value = value + sums[q, down, :]
                sums[q, down, :] = value
            return tuple(new)

        zeros = tuple(jnp.zeros((8, LANES), F32) for _ in range(3 * group // LANES))
        found = lax.fori_loop(0, rows // 8, strip, zeros, unroll=4)
        for k in range(group // LANES):
            across = slice(h * group + k * LANES, h * group + (k + 1) * LANES)
            for q in range(3):
                col_sums[q, :, across] = found[3 * k + q]

    def publish(out, peak_t, peak_s, mass_t, mass_s, gap):
        lse_t = peak_t + jnp.log2(mass_t)
        lse_s = peak_s + jnp.log2(mass_s)
        mean = gap / mass_t
        for q, value in enumerate((lse_t, lse_s, mean)):
            for b in range(value.shape[1] // LANES):
                line = value[:, b * LANES : (b + 1) * LANES]
                out[q * 8 + b : q * 8 + b + 1, :] = line

    publish(
        col_out, col_peaks[0, :1, :], col_peaks[1, :1, :],
        *(jnp.sum(col_sums[q], axis=0, keepdims=True) for q in range(3)),
    )

    def across_lanes(value, weight):
        found = lax.dot_general(
            jnp.full((8, LANES), weight, F32), value, (((1,), (1,)), ((), ())),
            preferred_element_type=F32, precision=lax.Precision.HIGHEST,
        )
        return found[:1]

    publish(
        row_out,
        across_lanes(peaks[0], 1.0 / LANES), across_lanes(peaks[1], 1.0 / LANES),
        *(across_lanes(sums[q], 1.0) for q in range(3)),
    )


def local_stats(teacher_img, teacher_txt, student_img, student_txt):
    rows, deep = teacher_img.shape
    cols, thin = student_txt.shape
    kernel = functools.partial(
        stats_kernel, 3.0 / math.sqrt(deep) / LN2, 3.0 / math.sqrt(thin) / LN2
    )
    return pl.pallas_call(
        kernel,
        name="logits_and_statistics",
        out_shape=(
            pltpu.VMEM((rows, cols), F32), pltpu.VMEM((rows, cols), F32),
            jax.ShapeDtypeStruct((3 * rows // LANES, LANES), F32),
            jax.ShapeDtypeStruct((3 * cols // LANES, LANES), F32),
        ),
        in_specs=[ANYWHERE] * 4,
        out_specs=(WHOLE,) * 4,
        scratch_shapes=[
            pltpu.VMEM((rows, deep), jnp.bfloat16), pltpu.VMEM((cols, deep), jnp.bfloat16),
            pltpu.VMEM((rows, thin), jnp.bfloat16), pltpu.VMEM((cols, thin), jnp.bfloat16),
            pltpu.VMEM((2, rows, LANES), F32), pltpu.VMEM((3, rows, LANES), F32),
            pltpu.VMEM((2, 8, cols), F32), pltpu.VMEM((3, 8, cols), F32),
            pltpu.SemaphoreType.DMA((8,)),
        ],
        compiler_params=pltpu.CompilerParams(vmem_limit_bytes=STATS_LIMIT),
        cost_estimate=cost(2 * rows * cols * (deep + thin), 8 * rows * cols, 4 * rows * cols),
    )(teacher_img, teacher_txt, student_img, student_txt)


def joined(parts):
    teach, learn, gap = ([part[8 * q : 8 * q + 8, :] for part in parts] for q in range(3))
    teach_peak = functools.reduce(jnp.maximum, teach)
    learn_peak = functools.reduce(jnp.maximum, learn)
    weights = [jnp.exp2(part - teach_peak) for part in teach]
    mass = sum(weights[1:], weights[0])
    shares = [jnp.exp2(part - learn_peak) for part in learn]
    gaps = [weight * part for weight, part in zip(weights, gap)]
    return (
        teach_peak + jnp.log2(mass),
        learn_peak + jnp.log2(sum(shares[1:], shares[0])),
        sum(gaps[1:], gaps[0]) / mass,
    )


def join_kernel(groups, *refs):
    sources, outs = refs[: len(refs) - len(groups)], refs[len(refs) - len(groups) :]
    for group, out in zip(groups, outs):
        for q, value in enumerate(joined([sources[k][...] for k in group])):
            out[8 * q : 8 * q + 8, :] = value


def join(groups, *parts):
    return pl.pallas_call(
        functools.partial(join_kernel, groups),
        name="joined_statistics",
        out_shape=[jax.ShapeDtypeStruct(parts[group[0]].shape, F32) for group in groups],
        in_specs=[WHOLE] * len(parts),
        out_specs=[WHOLE] * len(groups),
        cost_estimate=cost(parts[0].size * 20, parts[0].size * 4 * len(parts), parts[0].size * 4),
    )(*parts)


def gradient_kernel(scale, *refs):
    row_parts, col_parts = refs[:4], refs[4:6]
    t, s, st, si, img_out, theirs, mine, delta, row_norms, col_norms = refs[6:]
    rows, cols = t.shape
    thin = st.shape[1]
    row_teach, row_learn, row_mean = joined([part[...] for part in row_parts])
    col_teach, col_learn, col_mean = joined([part[...] for part in col_parts])
    row_total = jnp.sum(row_mean + row_learn - row_teach)
    col_total = jnp.sum(col_mean + col_learn - col_teach)
    for which, (down, across) in enumerate(((row_teach, col_teach), (row_learn, col_learn))):
        turned = jnp.concatenate([down - 3.0] * (LANES // 8), axis=0).T
        for b in range(8):
            row_norms[which, b * LANES : (b + 1) * LANES, :] = jnp.broadcast_to(
                turned[:, b : b + 1], (LANES, LANES)
            )
            col_norms[which, :, b * LANES : (b + 1) * LANES] = jnp.broadcast_to(
                across[b : b + 1, :] - 3.0, (16, LANES)
            )

    def strip(r, carry):
        down = pl.ds(pl.multiple_of(r * 16, 16), 16)
        row_t, row_s = row_norms[0, down, :], row_norms[1, down, :]
        for k in range(cols // LANES):
            across = slice(k * LANES, (k + 1) * LANES)
            tv, sv = t[down, across], s[down, across]
            value = (
                jnp.exp2(sv - row_s) - jnp.exp2(tv - row_t)
                + jnp.exp2(sv - col_norms[1, :, across]) - jnp.exp2(tv - col_norms[0, :, across])
            )
            delta[down, across] = value.astype(jnp.bfloat16)
        return carry

    lax.fori_loop(0, rows // 16, strip, 0, unroll=2)

    place, core = lax.axis_index("img_0"), lax.axis_index("img_1")
    chips = lax.axis_size("img_0")
    tall = cols // chips
    half = tall // 2
    full_note = jnp.full((NOTE, thin), row_total, F32)

    def text_block(out, top, far, part, note):
        size = tall if part is None else half
        at = lax.rem(place + far + chips, chips) * tall
        across = pl.ds(pl.multiple_of(at, tall), tall)
        grad = scale * lax.dot_general(
            delta[:, across], si[...], (((0,), (0,)), ((), ())), preferred_element_type=F32
        )
        if part is not None:
            grad = jnp.where(part == 0, grad[:half], grad[half:])
        out[top : top + size, :] = grad
        out[top + size : top + size + NOTE, :] = note

    for out, flow in ((theirs, 1 - core), (mine, core)):
        sign = 1 - 2 * flow
        top = 0
        for far, part, note in (
            (2 * sign, None, full_note), (3 * sign, None, full_note), (sign, None, full_note),
            (chips // 2, flow, 0.5 * full_note), (0, flow, full_note),
        ):
            text_block(out, top, far, part, note)
            top += (tall if part is None else half) + NOTE

    pieces, lines, _ = img_out.shape
    own = rows // pieces
    some = 4
    for n in range(pieces // some):
        grad = scale * jnp.dot(
            delta[n * some * own : (n + 1) * some * own, :], st[...], preferred_element_type=F32
        )
        for k in range(some):
            for b in range(thin // LANES):
                img_out[n * some + k, b * own : (b + 1) * own, :] = grad[
                    k * own : (k + 1) * own, b * LANES : (b + 1) * LANES
                ]
    for k in range(pieces):
        img_out[k, lines - NOTE :, :] = jnp.full((NOTE, LANES), col_total, F32)


def flow_rows(tall):
    full, part = tall + NOTE, tall // 2 + NOTE
    return (full, full, full, part, part)


def gradients(row_parts, col_parts, t, s, student_txt, student_img, pieces, chips):
    rows, cols = t.shape
    thin = student_txt.shape[1]
    lines = rows // pieces * thin // LANES + NOTE
    flow = jax.ShapeDtypeStruct((sum(flow_rows(cols // chips)), thin), F32)
    return pl.pallas_call(
        functools.partial(gradient_kernel, 3.0 / math.sqrt(thin)),
        name="delta_and_gradients",
        out_shape=(jax.ShapeDtypeStruct((pieces, lines, LANES), F32), flow, flow),
        in_specs=[WHOLE] * (len(row_parts) + len(col_parts) + 4),
        out_specs=(WHOLE,) * 3,
        scratch_shapes=[
            pltpu.VMEM((rows, cols), jnp.bfloat16),
            pltpu.VMEM((2, rows, LANES), F32), pltpu.VMEM((2, 16, cols), F32),
        ],
        compiler_params=pltpu.CompilerParams(vmem_limit_bytes=VMEM_LIMIT),
        cost_estimate=cost(4 * rows * cols * thin, 8 * rows * cols, 4 * rows * cols),
    )(*row_parts, *col_parts, t, s, student_txt, student_img)


def add_kernel(mine, theirs, *outs):
    top = 0
    for out in outs:
        down = slice(top, top + out.shape[0])
        out[...] = mine[down, :] + theirs[down, :]
        top += out.shape[0]


def added(mine, theirs, chips):
    thin = mine.shape[1]
    sizes = flow_rows(2 * (mine.shape[0] - 5 * NOTE) // chips)
    return pl.pallas_call(
        add_kernel,
        name="both_cores_text_terms",
        out_shape=[jax.ShapeDtypeStruct((size, thin), F32) for size in sizes],
        in_specs=[WHOLE] * 2,
        out_specs=[WHOLE] * len(sizes),
        cost_estimate=cost(mine.size, 12 * mine.size),
    )(mine, theirs)


def relay_kernel(near, next_one, far, farthest, out):
    core = lax.axis_index("img_1")
    full = out.shape[0]
    half = (full - NOTE) // 2
    out[...] = near[...] + next_one[...] + far[...]
    down = pl.ds(pl.multiple_of(core * half, half), half)
    out[down, :] = out[down, :] + farthest[:half, :]
    out[full - NOTE :, :] = out[full - NOTE :, :] + farthest[half:, :]


def relayed(*parts):
    return pl.pallas_call(
        relay_kernel,
        name="relayed_text_terms",
        out_shape=jax.ShapeDtypeStruct(parts[0].shape, F32),
        in_specs=[WHOLE] * 4,
        out_specs=WHOLE,
        cost_estimate=cost(parts[0].size * 3, 16 * parts[0].size),
    )(*parts)


def sum_kernel(parts, out, note):
    own = out.shape[0]
    for b in range(out.shape[1] // LANES):
        total = parts[0, b * own : (b + 1) * own, :]
        for k in range(1, parts.shape[0]):
            total = total + parts[k, b * own : (b + 1) * own, :]
        out[:, b * LANES : (b + 1) * LANES] = total
    last = slice(parts.shape[1] - NOTE, parts.shape[1])
    total = parts[0, last, :]
    for k in range(1, parts.shape[0]):
        total = total + parts[k, last, :]
    note[...] = total


def summed(parts, thin):
    own = (parts.shape[1] - NOTE) * LANES // thin
    return pl.pallas_call(
        sum_kernel,
        name="sum_of_image_parts",
        out_shape=(jax.ShapeDtypeStruct((own, thin), F32), jax.ShapeDtypeStruct((NOTE, LANES), F32)),
        in_specs=[WHOLE],
        out_specs=(WHOLE, WHOLE),
        cost_estimate=cost(parts.size, 4 * parts.size),
    )(parts)


def finish_kernel(row_share, col_share, flow, other, own, col_note, out, loss):
    half = out.shape[0]
    core = lax.axis_index("img_1")
    down = pl.ds(pl.multiple_of(core * half, half), half)
    out[...] = flow[down, :] + other[down, :] + own[:half, :]
    row_note = flow[2 * half :, :LANES] + other[2 * half :, :LANES] + own[half:, :LANES]
    loss[...] = (0.5 * LN2) * (row_note * row_share + col_note[...] * col_share)


def finished(row_share, col_share, flow, other, own, col_note):
    thin = flow.shape[1]
    return pl.pallas_call(
        functools.partial(finish_kernel, row_share, col_share),
        name="text_gradient_and_loss",
        out_shape=(
            jax.ShapeDtypeStruct((own.shape[0] - NOTE, thin), F32),
            jax.ShapeDtypeStruct((NOTE, LANES), F32),
        ),
        in_specs=[WHOLE] * 4,
        out_specs=(WHOLE, WHOLE),
        cost_estimate=cost(own.size * 3, 16 * own.size),
    )(flow, other, own, col_note)


def turn(size, step):
    return [(k, (k + step) % size) for k in range(size)]


def body(teacher_img, teacher_txt, student_img, student_txt):
    rows = student_img.shape[0]
    cols, thin = student_txt.shape
    chips, cores = lax.axis_size("img_0"), lax.axis_size("img_1")
    img_count, txt_count = chips * cores, lax.axis_size(TXT)
    side = lax.axis_size("txt_0")

    t, s, row, col = local_stats(teacher_img, teacher_txt, student_img, student_txt)
    xs = [lax.ppermute(row, "txt_0", turn(side, k)) for k in (1, 3, 2)]
    below = lax.ppermute(col, "img_0", turn(chips, 1))
    above = lax.ppermute(col, "img_0", turn(chips, -1))
    row, three, two = join(((0, 1, 2, 3), (4, 5, 6), (4, 5)), row, *xs, col, below, above)
    ys = [lax.ppermute(row, "txt_1", turn(side, k)) for k in (1, 3, 2)]
    below = lax.ppermute(three, "img_0", turn(chips, 3))
    above = lax.ppermute(two, "img_0", turn(chips, -3))
    (col,) = join(((0, 1, 2),), three, below, above)
    swap = turn(cores, 1)
    other = lax.ppermute(col, "img_1", swap)

    to_img, theirs, mine = gradients(
        (row, *ys), (col, other), t, s, student_txt, student_img, txt_count, chips
    )
    theirs = lax.ppermute(theirs, "img_1", swap)
    got_img = lax.all_to_all(to_img, TXT, 0, 0, tiled=True)
    one, two, near, three, own = added(mine, theirs, chips)

    def outward(value, step):
        pairs = [
            (cores * z + c, cores * ((z + step * (1 - 2 * c)) % chips) + c)
            for z in range(chips) for c in range(cores)
        ]
        return lax.ppermute(value, IMG, pairs)

    flow = relayed(near, outward(one, 1), outward(two, 2), outward(three, 3))
    flow = outward(flow, 1)
    across = lax.ppermute(flow, "img_1", swap)
    grad_img, col_note = summed(got_img, thin)
    grad_txt, loss = finished(
        1.0 / (rows * img_count), 1.0 / (cols * txt_count), flow, across, own, col_note
    )
    return (loss[0, 0], grad_img, grad_txt)


def solution(mesh):
    torus = Mesh(mesh.devices.reshape(8, 2, 4, 4), ("img_0", "img_1", "txt_0", "txt_1"))
    in_specs = (P(IMG, None), P(TXT, None), P(IMG, None), P(TXT, None))
    out_specs = (P(), P(IMG_TXT, None), P(TXT_IMG, None))
    return jax.shard_map(body, mesh=torus, in_specs=in_specs, out_specs=out_specs, check_vma=False)
```

```python
import functools
import math

import jax
import jax.numpy as jnp
from jax import lax
from jax.experimental import pallas as pl
from jax.experimental.pallas import tpu as pltpu
from jax.sharding import Mesh
from jax.sharding import PartitionSpec as P

IMG = ("img_0", "img_1")
TXT = ("txt_0", "txt_1")
IMG_TXT = ("img_0", "img_1", "txt_0", "txt_1")
TXT_IMG = ("txt_0", "txt_1", "img_0", "img_1")
LANES = 128
NOTE = 8
VMEM_LIMIT = 20 * 1024 * 1024
STATS_LIMIT = 24 * 1024 * 1024
LN2 = math.log(2.0)
F32 = jnp.float32
MIB = 1024 * 1024
WHOLE = pl.BlockSpec(memory_space=pltpu.VMEM)
FAR = pl.BlockSpec(memory_space=pltpu.HBM)


def cost(flops, size, transcendentals=0):
    return pl.CostEstimate(flops=flops, bytes_accessed=size, transcendentals=transcendentals)


def stats_kernel(scale_teach, scale_learn, ti_hbm, tt_hbm, si_hbm, st_hbm, t, s, row_out, col_out,
                 ti, tt, si, st, peaks, sums, col_peaks, col_sums, sems):
    rows, cols = t.shape
    tall = 256
    chunks = rows // tall

    def load(src, dst, at, size, which):
        copy = pltpu.make_async_copy(
            src.at[pl.ds(at, size), :], dst.at[pl.ds(at, size), :], sems.at[which]
        )
        copy.start()
        return copy

    tt_load = load(tt_hbm, tt, 0, cols, 0)
    ti_loads = [load(ti_hbm, ti, n * tall, tall, 1 + n) for n in range(2)]

    def logits(left, right, out, scale, which, arrivals):
        for n in range(chunks):
            if arrivals:
                arrivals[n].wait()
            down = slice(n * tall, (n + 1) * tall)
            block = scale * lax.dot_general(
                left[down, :], right[...], (((1,), (1,)), ((), ())), preferred_element_type=F32
            )
            out[down, :] = block
            top = jnp.max(block.reshape(tall // 8, 8, cols), axis=0)
            col_peaks[which] = jnp.maximum(col_peaks[which], top) if n else top
            side = block[:, :LANES]
            for k in range(1, cols // LANES):
                side = jnp.maximum(side, block[:, k * LANES : (k + 1) * LANES])
            peaks[which, down, :] = jnp.broadcast_to(
                jnp.max(side, axis=1, keepdims=True), (tall, LANES)
            )
        col_peaks[which] = jnp.broadcast_to(
            jnp.max(col_peaks[which], axis=0, keepdims=True), (8, cols)
        )

    tt_load.wait()
    ti_loads += [load(ti_hbm, ti, n * tall, tall, 1 + n) for n in range(2, chunks)]
    st_load = load(st_hbm, st, 0, cols, 1 + chunks)
    si_load = load(si_hbm, si, 0, rows, 2 + chunks)
    logits(ti, tt, t, scale_teach, 0, ti_loads)
    st_load.wait()
    si_load.wait()
    logits(si, st, s, scale_learn, 1, None)
    lane = lax.broadcasted_iota(jnp.int32, (8, LANES), 1)

    group = 4 * LANES
    for h in range(cols // group):
        def strip(r, carry):
            at = pl.multiple_of(r * 8, 8)
            down = pl.ds(at, 8)
            row_peak_t, row_peak_s = peaks[0, down, :], peaks[1, down, :]
            row_t = row_s = row_g = None
            new = []
            for k in range(group // LANES):
                across = slice(h * group + k * LANES, h * group + (k + 1) * LANES)
                tv, sv = t[down, across], s[down, across]
                gap = tv - sv
                wr = jnp.exp2(tv - row_peak_t)
                vr = jnp.exp2(sv - row_peak_s)
                wc = jnp.exp2(tv - col_peaks[0, :, across])
                vc = jnp.exp2(sv - col_peaks[1, :, across])
                row_t = wr if row_t is None else row_t + wr
                row_s = vr if row_s is None else row_s + vr
                row_g = wr * gap if row_g is None else row_g + wr * gap
                ct, cs, cg = carry[3 * k : 3 * k + 3]
                new += [ct + wc, cs + vc, cg + wc * gap]
            if h < cols // group - 1:
                for q, value in enumerate((row_t, row_s, row_g)):
                    sums[q, down, :] = value + sums[q, down, :] if h else value
            else:
                packed = jnp.where(lane == 0, row_peak_t, row_peak_s)
                for q, value in enumerate((row_t, row_s, row_g)):
                    total = value + sums[q, down, :] if h else value
                    total = jnp.sum(total, axis=1, keepdims=True)
                    packed = jnp.where(lane == 2 + q, total, packed)
                sums[0, down, :] = packed
            return tuple(new)

        zeros = tuple(jnp.zeros((8, LANES), F32) for _ in range(3 * group // LANES))
        found = lax.fori_loop(0, rows // 8, strip, zeros, unroll=4)
        for k in range(group // LANES):
            across = slice(h * group + k * LANES, h * group + (k + 1) * LANES)
            for q in range(3):
                col_sums[q, :, across] = found[3 * k + q]

    def publish(out, peak_t, peak_s, mass_t, mass_s, gap):
        found = (peak_t + jnp.log2(mass_t), peak_s + jnp.log2(mass_s), gap / mass_t)
        for q, value in enumerate(found):
            out[8 * q : 8 * q + 8, :] = value

    def stacked(lines):
        return jnp.concatenate(lines, axis=0)

    def by_column(value):
        return stacked([value[:, b * LANES : (b + 1) * LANES] for b in range(cols // LANES)])

    publish(
        col_out, by_column(col_peaks[0, :1, :]), by_column(col_peaks[1, :1, :]),
        *(by_column(jnp.sum(col_sums[q], axis=0, keepdims=True)) for q in range(3)),
    )
    turned = [sums[0, b * LANES : (b + 1) * LANES, :].T for b in range(rows // LANES)]
    publish(row_out, *(stacked([block[q : q + 1, :] for block in turned]) for q in range(5)))


def local_stats(teacher_img, teacher_txt, student_img, student_txt):
    rows, deep = teacher_img.shape
    cols, thin = student_txt.shape
    kernel = functools.partial(
        stats_kernel, 3.0 / math.sqrt(deep) / LN2, 3.0 / math.sqrt(thin) / LN2
    )
    return pl.pallas_call(
        kernel,
        name="logits_and_statistics",
        out_shape=(
            pltpu.VMEM((rows, cols), F32), pltpu.VMEM((rows, cols), F32),
            jax.ShapeDtypeStruct((3 * rows // LANES, LANES), F32),
            jax.ShapeDtypeStruct((3 * cols // LANES, LANES), F32),
        ),
        in_specs=[FAR] * 4,
        out_specs=(WHOLE,) * 4,
        scratch_shapes=[
            pltpu.VMEM((rows, deep), jnp.bfloat16), pltpu.VMEM((cols, deep), jnp.bfloat16),
            pltpu.VMEM((rows, thin), jnp.bfloat16), pltpu.VMEM((cols, thin), jnp.bfloat16),
            pltpu.VMEM((2, rows, LANES), F32), pltpu.VMEM((3, rows, LANES), F32),
            pltpu.VMEM((2, 8, cols), F32), pltpu.VMEM((3, 8, cols), F32),
            pltpu.SemaphoreType.DMA((8,)),
        ],
        compiler_params=pltpu.CompilerParams(vmem_limit_bytes=STATS_LIMIT),
        cost_estimate=cost(2 * rows * cols * (deep + thin), 8 * rows * cols, 4 * rows * cols),
    )(*(
        pltpu.with_memory_space_constraint(x, pltpu.HBM)
        for x in (teacher_img, teacher_txt, student_img, student_txt)
    ))


def joined(parts):
    teach, learn, gap = ([part[8 * q : 8 * q + 8, :] for part in parts] for q in range(3))
    teach_peak = functools.reduce(jnp.maximum, teach)
    learn_peak = functools.reduce(jnp.maximum, learn)
    weights = [jnp.exp2(part - teach_peak) for part in teach]
    mass = sum(weights[1:], weights[0])
    shares = [jnp.exp2(part - learn_peak) for part in learn]
    gaps = [weight * part for weight, part in zip(weights, gap)]
    return (
        teach_peak + jnp.log2(mass),
        learn_peak + jnp.log2(sum(shares[1:], shares[0])),
        sum(gaps[1:], gaps[0]) / mass,
    )


def join_kernel(groups, *refs):
    sources, outs = refs[: len(refs) - len(groups)], refs[len(refs) - len(groups) :]
    for group, out in zip(groups, outs):
        for q, value in enumerate(joined([sources[k][...] for k in group])):
            out[8 * q : 8 * q + 8, :] = value


def join(groups, *parts):
    return pl.pallas_call(
        functools.partial(join_kernel, groups),
        name="joined_statistics",
        out_shape=[jax.ShapeDtypeStruct(parts[group[0]].shape, F32) for group in groups],
        in_specs=[WHOLE] * len(parts),
        out_specs=[WHOLE] * len(groups),
        compiler_params=pltpu.CompilerParams(vmem_limit_bytes=1 * MIB),
        cost_estimate=cost(parts[0].size * 20, parts[0].size * 4 * len(parts), parts[0].size * 4),
    )(*parts)


def gradient_kernel(scale, *refs):
    row_parts, col_parts = refs[:4], refs[4:6]
    t, s, st_far, si_far, img_out, theirs_out, mine = refs[6:13]
    delta, row_norms, col_norms, img_block, theirs, st, si, sems = refs[13:]
    loads = [
        pltpu.make_async_copy(src, dst, sems.at[sems.shape[0] - 1 - k])
        for k, (src, dst) in enumerate(((st_far, st), (si_far, si)))
    ]
    for load in loads:
        load.start()
    rows, cols = t.shape
    thin = st.shape[1]
    row_teach, row_learn, row_mean = joined([part[...] for part in row_parts])
    col_teach, col_learn, col_mean = joined([part[...] for part in col_parts])
    row_total = jnp.sum(row_mean + row_learn - row_teach)
    col_total = jnp.sum(col_mean + col_learn - col_teach)
    for which, (down, across) in enumerate(((row_teach, col_teach), (row_learn, col_learn))):
        turned = jnp.concatenate([down - 3.0] * (LANES // 8), axis=0).T
        for b in range(8):
            row_norms[which, b * LANES : (b + 1) * LANES, :] = jnp.broadcast_to(
                turned[:, b : b + 1], (LANES, LANES)
            )
            col_norms[which, :, b * LANES : (b + 1) * LANES] = jnp.broadcast_to(
                across[b : b + 1, :] - 3.0, (16, LANES)
            )

    def strip(r, carry):
        down = pl.ds(pl.multiple_of(r * 16, 16), 16)
        row_t, row_s = row_norms[0, down, :], row_norms[1, down, :]
        for k in range(cols // LANES):
            across = slice(k * LANES, (k + 1) * LANES)
            tv, sv = t[down, across], s[down, across]
            value = (
                jnp.exp2(sv - row_s) - jnp.exp2(tv - row_t)
                + jnp.exp2(sv - col_norms[1, :, across]) - jnp.exp2(tv - col_norms[0, :, across])
            )
            delta[down, across] = value.astype(jnp.bfloat16)
        return carry

    lax.fori_loop(0, rows // 16, strip, 0, unroll=2)
    for load in loads:
        load.wait()

    pieces, lines, _ = img_block.shape
    own = rows // pieces
    some = 4
    for k in range(pieces):
        img_block[k, lines - NOTE :, :] = jnp.full((NOTE, LANES), col_total, F32)
    saves = []
    for n in range(pieces // some):
        grad = scale * jnp.dot(
            delta[n * some * own : (n + 1) * some * own, :], st[...], preferred_element_type=F32
        )
        for k in range(some):
            for b in range(thin // LANES):
                img_block[n * some + k, b * own : (b + 1) * own, :] = grad[
                    k * own : (k + 1) * own, b * LANES : (b + 1) * LANES
                ]
        save = pltpu.make_async_copy(
            img_block.at[pl.ds(n * some, some)], img_out.at[pl.ds(n * some, some)], sems.at[n]
        )
        save.start()
        saves.append(save)

    place, core = lax.axis_index("img_0"), lax.axis_index("img_1")
    chips = lax.axis_size("img_0")
    tall = cols // chips
    half = tall // 2
    full_note = jnp.full((NOTE, thin), row_total, F32)

    def text_block(out, top, far, part, note):
        size = tall if part is None else half
        at = lax.rem(place + far + chips, chips) * tall
        across = pl.ds(pl.multiple_of(at, tall), tall)
        grad = scale * lax.dot_general(
            delta[:, across], si[...], (((0,), (0,)), ((), ())), preferred_element_type=F32
        )
        if part is not None:
            grad = jnp.where(part == 0, grad[:half], grad[half:])
        out[top : top + size, :] = grad
        out[top + size : top + size + NOTE, :] = note

    for out, flow in ((theirs, 1 - core), (mine, core)):
        sign = 1 - 2 * flow
        top = 0
        for far, part, note in (
            (2 * sign, None, full_note), (3 * sign, None, full_note), (sign, None, full_note),
            (chips // 2, flow, 0.5 * full_note), (0, flow, full_note),
        ):
            text_block(out, top, far, part, note)
            top += (tall if part is None else half) + NOTE
        if out is theirs:
            save = pltpu.make_async_copy(theirs, theirs_out, sems.at[len(saves)])
            save.start()
            saves.append(save)

    for save in saves:
        save.wait()


def flow_rows(tall):
    full, part = tall + NOTE, tall // 2 + NOTE
    return (full, full, full, part, part)


def gradients(row_parts, col_parts, t, s, student_txt, student_img, pieces, chips):
    rows, cols = t.shape
    thin = student_txt.shape[1]
    lines = rows // pieces * thin // LANES + NOTE
    flow = jax.ShapeDtypeStruct((sum(flow_rows(cols // chips)), thin), F32)
    return pl.pallas_call(
        functools.partial(gradient_kernel, 3.0 / math.sqrt(thin)),
        name="delta_and_gradients",
        out_shape=(
            pltpu.HBM((pieces, lines, LANES), F32), pltpu.HBM(flow.shape, F32), flow,
        ),
        in_specs=[WHOLE] * (len(row_parts) + len(col_parts) + 2) + [FAR] * 2,
        out_specs=(FAR, FAR, WHOLE),
        scratch_shapes=[
            pltpu.VMEM((rows, cols), jnp.bfloat16),
            pltpu.VMEM((2, rows, LANES), F32), pltpu.VMEM((2, 16, cols), F32),
            pltpu.VMEM((pieces, lines, LANES), F32), pltpu.VMEM(flow.shape, F32),
            pltpu.VMEM(student_txt.shape, jnp.bfloat16), pltpu.VMEM(student_img.shape, jnp.bfloat16),
            pltpu.SemaphoreType.DMA((pieces // 4 + 3,)),
        ],
        compiler_params=pltpu.CompilerParams(vmem_limit_bytes=VMEM_LIMIT),
        cost_estimate=cost(4 * rows * cols * thin, 8 * rows * cols, 4 * rows * cols),
    )(
        *row_parts, *col_parts, t, s,
        *(pltpu.with_memory_space_constraint(x, pltpu.HBM) for x in (student_txt, student_img)),
    )


def add_kernel(mine, theirs, *outs):
    top = 0
    for out in outs:
        down = slice(top, top + out.shape[0])
        out[...] = mine[down, :] + theirs[down, :]
        top += out.shape[0]


def added(mine, theirs, chips):
    thin = mine.shape[1]
    sizes = flow_rows(2 * (mine.shape[0] - 5 * NOTE) // chips)
    return pl.pallas_call(
        add_kernel,
        name="both_cores_text_terms",
        out_shape=[jax.ShapeDtypeStruct((size, thin), F32) for size in sizes],
        in_specs=[WHOLE] * 2,
        out_specs=[WHOLE] * len(sizes),
        compiler_params=pltpu.CompilerParams(vmem_limit_bytes=8 * MIB),
        cost_estimate=cost(mine.size, 12 * mine.size),
    )(mine, theirs)


def relay_kernel(near, next_one, far, farthest, out):
    core = lax.axis_index("img_1")
    full = out.shape[0]
    half = (full - NOTE) // 2
    out[...] = near[...] + next_one[...] + far[...]
    down = pl.ds(pl.multiple_of(core * half, half), half)
    out[down, :] = out[down, :] + farthest[:half, :]
    out[full - NOTE :, :] = out[full - NOTE :, :] + farthest[half:, :]


def relayed(*parts):
    return pl.pallas_call(
        relay_kernel,
        name="relayed_text_terms",
        out_shape=jax.ShapeDtypeStruct(parts[0].shape, F32),
        in_specs=[WHOLE] * 4,
        out_specs=WHOLE,
        compiler_params=pltpu.CompilerParams(vmem_limit_bytes=4 * MIB),
        cost_estimate=cost(parts[0].size * 3, 16 * parts[0].size),
    )(*parts)


def sum_kernel(parts, out, note):
    own = out.shape[0]
    for b in range(out.shape[1] // LANES):
        total = parts[0, b * own : (b + 1) * own, :]
        for k in range(1, parts.shape[0]):
            total = total + parts[k, b * own : (b + 1) * own, :]
        out[:, b * LANES : (b + 1) * LANES] = total
    last = slice(parts.shape[1] - NOTE, parts.shape[1])
    total = parts[0, last, :]
    for k in range(1, parts.shape[0]):
        total = total + parts[k, last, :]
    note[...] = total


def summed(parts, thin):
    own = (parts.shape[1] - NOTE) * LANES // thin
    return pl.pallas_call(
        sum_kernel,
        name="sum_of_image_parts",
        out_shape=(jax.ShapeDtypeStruct((own, thin), F32), jax.ShapeDtypeStruct((NOTE, LANES), F32)),
        in_specs=[WHOLE],
        out_specs=(WHOLE, WHOLE),
        compiler_params=pltpu.CompilerParams(vmem_limit_bytes=4 * MIB),
        cost_estimate=cost(parts.size, 4 * parts.size),
    )(parts)


def finish_kernel(row_share, col_share, flow, other, own, col_note, out, loss):
    half = out.shape[0]
    core = lax.axis_index("img_1")
    down = pl.ds(pl.multiple_of(core * half, half), half)
    out[...] = flow[down, :] + other[down, :] + own[:half, :]
    row_note = flow[2 * half :, :LANES] + other[2 * half :, :LANES] + own[half:, :LANES]
    total = (0.5 * LN2) * (row_note * row_share + col_note[...] * col_share)
    loss[0, 0] = total[0, 0]


def finished(row_share, col_share, flow, other, own, col_note):
    thin = flow.shape[1]
    return pl.pallas_call(
        functools.partial(finish_kernel, row_share, col_share),
        name="text_gradient_and_loss",
        out_shape=(
            jax.ShapeDtypeStruct((own.shape[0] - NOTE, thin), F32),
            jax.ShapeDtypeStruct((1, 1), F32),
        ),
        in_specs=[WHOLE] * 4,
        out_specs=(WHOLE, pl.BlockSpec(memory_space=pltpu.SMEM)),
        compiler_params=pltpu.CompilerParams(vmem_limit_bytes=4 * MIB),
        cost_estimate=cost(own.size * 3, 16 * own.size),
    )(flow, other, own, col_note)


def turn(size, step):
    return [(k, (k + step) % size) for k in range(size)]


def body(teacher_img, teacher_txt, student_img, student_txt):
    rows = student_img.shape[0]
    cols, thin = student_txt.shape
    chips, cores = lax.axis_size("img_0"), lax.axis_size("img_1")
    img_count, txt_count = chips * cores, lax.axis_size(TXT)
    side = lax.axis_size("txt_0")

    t, s, row, col = local_stats(teacher_img, teacher_txt, student_img, student_txt)
    xs = [lax.ppermute(row, "txt_0", turn(side, k)) for k in (1, 3, 2)]
    below = lax.ppermute(col, "img_0", turn(chips, 1))
    above = lax.ppermute(col, "img_0", turn(chips, -1))
    row, three, two = join(((0, 1, 2, 3), (4, 5, 6), (4, 5)), row, *xs, col, below, above)
    ys = [lax.ppermute(row, "txt_1", turn(side, k)) for k in (1, 3, 2)]
    below = lax.ppermute(three, "img_0", turn(chips, 3))
    above = lax.ppermute(two, "img_0", turn(chips, -3))
    (col,) = join(((0, 1, 2),), three, below, above)
    swap = turn(cores, 1)
    other = lax.ppermute(col, "img_1", swap)

    to_img, theirs, mine = gradients(
        (row, *ys), (col, other), t, s, student_txt, student_img, txt_count, chips
    )
    theirs = lax.ppermute(theirs, "img_1", swap)
    got_img = lax.all_to_all(to_img, TXT, 0, 0, tiled=True)
    one, two, near, three, own = added(mine, theirs, chips)

    def outward(value, step):
        pairs = [
            (cores * z + c, cores * ((z + step * (1 - 2 * c)) % chips) + c)
            for z in range(chips) for c in range(cores)
        ]
        return lax.ppermute(value, IMG, pairs)

    flow = relayed(near, outward(one, 1), outward(two, 2), outward(three, 3))
    flow = outward(flow, 1)
    across = lax.ppermute(flow, "img_1", swap)
    grad_img, col_note = summed(got_img, thin)
    grad_txt, loss = finished(
        1.0 / (rows * img_count), 1.0 / (cols * txt_count), flow, across, own, col_note
    )
    return (loss.reshape(()), grad_img, grad_txt)


def solution(mesh):
    torus = Mesh(mesh.devices.reshape(8, 2, 4, 4), ("img_0", "img_1", "txt_0", "txt_1"))
    in_specs = (P(IMG, None), P(TXT, None), P(IMG, None), P(TXT, None))
    out_specs = (P(), P(IMG_TXT, None), P(TXT_IMG, None))
    return jax.shard_map(body, mesh=torus, in_specs=in_specs, out_specs=out_specs, check_vma=False)
```

```python
import functools
import math

import jax
import jax.numpy as jnp
from jax import lax
from jax.experimental import pallas as pl
from jax.experimental.pallas import tpu as pltpu
from jax.sharding import Mesh
from jax.sharding import PartitionSpec as P

IMG = ("img_0", "img_1")
TXT = ("txt_0", "txt_1")
IMG_TXT = ("img_0", "img_1", "txt_0", "txt_1")
TXT_IMG = ("txt_0", "txt_1", "img_0", "img_1")
LANES = 128
NOTE = 8
VMEM_LIMIT = 28 * 1024 * 1024
STATS_LIMIT = 32 * 1024 * 1024
LN2 = math.log(2.0)
F32 = jnp.float32
MIB = 1024 * 1024
WHOLE = pl.BlockSpec(memory_space=pltpu.VMEM)
FAR = pl.BlockSpec(memory_space=pltpu.HBM)


def cost(flops, size, transcendentals=0):
    return pl.CostEstimate(flops=flops, bytes_accessed=size, transcendentals=transcendentals)


def stats_kernel(scale_teach, scale_learn, ti_hbm, tt_hbm, si_hbm, st_hbm, t_hbm, s_hbm,
                 row_out, col_out, ti, tt, si, st, t, s, peaks, sums, col_peaks, col_sums, sems):
    rows, cols = t.shape
    tall = 256
    chunks = rows // tall

    def load(src, dst, at, size, which):
        copy = pltpu.make_async_copy(
            src.at[pl.ds(at, size), :], dst.at[pl.ds(at, size), :], sems.at[which]
        )
        copy.start()
        return copy

    st_load = load(st_hbm, st, 0, cols, 1 + chunks)
    si_load = load(si_hbm, si, 0, rows, 2 + chunks)
    tt_load = load(tt_hbm, tt, 0, cols, 0)

    saves = []

    def logits(left, right, out, far, scale, which, arrivals):
        for n in range(chunks):
            if arrivals:
                arrivals[n].wait()
            down = slice(n * tall, (n + 1) * tall)
            block = scale * lax.dot_general(
                left[down, :], right[...], (((1,), (1,)), ((), ())), preferred_element_type=F32
            )
            out[down, :] = block
            saves.append(load(out, far, n * tall, tall, sems.shape[0] - 1 - len(saves)))
            top = jnp.max(block.reshape(tall // 8, 8, cols), axis=0)
            col_peaks[which] = jnp.maximum(col_peaks[which], top) if n else top
            side = block[:, :LANES]
            for k in range(1, cols // LANES):
                side = jnp.maximum(side, block[:, k * LANES : (k + 1) * LANES])
            peaks[which, down, :] = jnp.broadcast_to(
                jnp.max(side, axis=1, keepdims=True), (tall, LANES)
            )
        col_peaks[which] = jnp.broadcast_to(
            jnp.max(col_peaks[which], axis=0, keepdims=True), (8, cols)
        )

    st_load.wait()
    si_load.wait()
    ti_loads = [load(ti_hbm, ti, n * tall, tall, 1 + n) for n in range(chunks)]
    logits(si, st, s, s_hbm, scale_learn, 1, None)
    tt_load.wait()
    logits(ti, tt, t, t_hbm, scale_teach, 0, ti_loads)

    group = 4 * LANES
    for h in range(cols // group):
        def strip(r, carry):
            at = pl.multiple_of(r * 8, 8)
            down = pl.ds(at, 8)
            row_peak_t, row_peak_s = peaks[0, down, :], peaks[1, down, :]
            row_t = row_s = row_g = None
            new = []
            for k in range(group // LANES):
                across = slice(h * group + k * LANES, h * group + (k + 1) * LANES)
                tv, sv = t[down, across], s[down, across]
                gap = tv - sv
                wr = jnp.exp2(tv - row_peak_t)
                vr = jnp.exp2(sv - row_peak_s)
                wc = jnp.exp2(tv - col_peaks[0, :, across])
                vc = jnp.exp2(sv - col_peaks[1, :, across])
                row_t = wr if row_t is None else row_t + wr
                row_s = vr if row_s is None else row_s + vr
                row_g = wr * gap if row_g is None else row_g + wr * gap
                ct, cs, cg = carry[3 * k : 3 * k + 3]
                new += [ct + wc, cs + vc, cg + wc * gap]
            for q, value in enumerate((row_t, row_s, row_g)):
                sums[q, down, :] = value + sums[q, down, :] if h else value
            return tuple(new)

        zeros = tuple(jnp.zeros((8, LANES), F32) for _ in range(3 * group // LANES))
        found = lax.fori_loop(0, rows // 8, strip, zeros, unroll=8)
        for k in range(group // LANES):
            across = slice(h * group + k * LANES, h * group + (k + 1) * LANES)
            for q in range(3):
                col_sums[q, :, across] = found[3 * k + q]

    def publish(out, peak_t, peak_s, mass_t, mass_s, gap):
        found = (peak_t + jnp.log2(mass_t), peak_s + jnp.log2(mass_s), gap / mass_t)
        for q, value in enumerate(found):
            for k in range(out.shape[0]):
                out[k, 8 * q : 8 * q + 8, :] = value

    def stacked(lines):
        return jnp.concatenate(lines, axis=0)

    def by_column(value):
        return stacked([value[:, b * LANES : (b + 1) * LANES] for b in range(cols // LANES)])

    publish(
        col_out, by_column(col_peaks[0, :1, :]), by_column(col_peaks[1, :1, :]),
        *(by_column(jnp.sum(col_sums[q], axis=0, keepdims=True)) for q in range(3)),
    )
    lane = lax.broadcasted_iota(jnp.int32, (rows, LANES), 1)
    packed = jnp.where(lane == 0, peaks[0], peaks[1])
    for q in range(3):
        packed = jnp.where(lane == 2 + q, jnp.sum(sums[q], axis=1, keepdims=True), packed)
    turned = [packed[b * LANES : (b + 1) * LANES, :].T for b in range(rows // LANES)]
    publish(row_out, *(stacked([block[q : q + 1, :] for block in turned]) for q in range(5)))
    for save in saves:
        save.wait()


def local_stats(teacher_img, teacher_txt, student_img, student_txt, copies):
    rows, deep = teacher_img.shape
    cols, thin = student_txt.shape
    kernel = functools.partial(
        stats_kernel, 3.0 / math.sqrt(deep) / LN2, 3.0 / math.sqrt(thin) / LN2
    )
    return pl.pallas_call(
        kernel,
        name="logits_and_statistics",
        out_shape=(
            pltpu.HBM((rows, cols), F32), pltpu.HBM((rows, cols), F32),
            jax.ShapeDtypeStruct((1, 3 * rows // LANES, LANES), F32),
            jax.ShapeDtypeStruct((copies, 3 * cols // LANES, LANES), F32),
        ),
        in_specs=[FAR] * 4,
        out_specs=(FAR, FAR, WHOLE, WHOLE),
        scratch_shapes=[
            pltpu.VMEM((rows, deep), jnp.bfloat16), pltpu.VMEM((cols, deep), jnp.bfloat16),
            pltpu.VMEM((rows, thin), jnp.bfloat16), pltpu.VMEM((cols, thin), jnp.bfloat16),
            pltpu.VMEM((rows, cols), F32), pltpu.VMEM((rows, cols), F32),
            pltpu.VMEM((2, rows, LANES), F32), pltpu.VMEM((3, rows, LANES), F32),
            pltpu.VMEM((2, 8, cols), F32), pltpu.VMEM((3, 8, cols), F32),
            pltpu.SemaphoreType.DMA((16,)),
        ],
        compiler_params=pltpu.CompilerParams(vmem_limit_bytes=STATS_LIMIT),
        cost_estimate=cost(2 * rows * cols * (deep + thin), 8 * rows * cols, 4 * rows * cols),
    )(*(
        pltpu.with_memory_space_constraint(x, pltpu.HBM)
        for x in (teacher_img, teacher_txt, student_img, student_txt)
    ))


def joined(parts):
    teach, learn, gap = ([part[8 * q : 8 * q + 8, :] for part in parts] for q in range(3))
    teach_peak = functools.reduce(jnp.maximum, teach)
    learn_peak = functools.reduce(jnp.maximum, learn)
    weights = [jnp.exp2(part - teach_peak) for part in teach]
    mass = sum(weights[1:], weights[0])
    shares = [jnp.exp2(part - learn_peak) for part in learn]
    gaps = [weight * part for weight, part in zip(weights, gap)]
    return (
        teach_peak + jnp.log2(mass),
        learn_peak + jnp.log2(sum(shares[1:], shares[0])),
        sum(gaps[1:], gaps[0]) / mass,
    )


def join_kernel(groups, *refs):
    sources, outs = refs[: len(refs) - len(groups)], refs[len(refs) - len(groups) :]
    for group, out in zip(groups, outs):
        for q, value in enumerate(joined([sources[k][...] for k in group])):
            out[8 * q : 8 * q + 8, :] = value


def join(groups, *parts):
    return pl.pallas_call(
        functools.partial(join_kernel, groups),
        name="joined_statistics",
        out_shape=[jax.ShapeDtypeStruct(parts[group[0]].shape, F32) for group in groups],
        in_specs=[WHOLE] * len(parts),
        out_specs=[WHOLE] * len(groups),
        compiler_params=pltpu.CompilerParams(vmem_limit_bytes=1 * MIB),
        cost_estimate=cost(parts[0].size * 20, parts[0].size * 4 * len(parts), parts[0].size * 4),
    )(*parts)


def delta_kernel(scale, *refs):
    row_parts = refs[:4]
    col_stats, t_far, s_far, st_far, si_far, delta, theirs_out, mine, st, col_note = refs[4:14]
    row_norms, col_norms, t, s, theirs, si, sems = refs[14:]
    tall = 256
    arrivals = []
    for n in range(t.shape[0] // tall):
        down = pl.ds(n * tall, tall)
        arrivals.append([
            pltpu.make_async_copy(far.at[down, :], near.at[down, :], sems.at[3 + 2 * n + k])
            for k, (far, near) in enumerate(((t_far, t), (s_far, s)))
        ])
        for copy in arrivals[-1]:
            copy.start()
    loads = [
        pltpu.make_async_copy(src, dst, sems.at[1 + k])
        for k, (src, dst) in enumerate(((st_far, st), (si_far, si)))
    ]
    for load in loads:
        load.start()
    rows, cols = t.shape
    thin = st.shape[1]
    row_teach, row_learn, row_mean = joined([part[...] for part in row_parts])
    col_teach, col_learn, col_mean = joined(
        [col_stats[k] for k in range(col_stats.shape[0])]
    )
    row_total = jnp.sum(row_mean + row_learn - row_teach)
    col_total = jnp.sum(col_mean + col_learn - col_teach)
    col_note[...] = jnp.full(col_note.shape, col_total, F32)
    for which, (down, across) in enumerate(((row_teach, col_teach), (row_learn, col_learn))):
        turned = jnp.concatenate([down - 3.0] * (LANES // 8), axis=0).T
        for b in range(8):
            row_norms[which, b * LANES : (b + 1) * LANES, :] = jnp.broadcast_to(
                turned[:, b : b + 1], (LANES, LANES)
            )
            col_norms[which, :, b * LANES : (b + 1) * LANES] = jnp.broadcast_to(
                across[b : b + 1, :] - 3.0, (16, LANES)
            )

    def strip(r, carry):
        down = pl.ds(pl.multiple_of(r * 16, 16), 16)
        row_t, row_s = row_norms[0, down, :], row_norms[1, down, :]
        for k in range(cols // LANES):
            across = slice(k * LANES, (k + 1) * LANES)
            tv, sv = t[down, across], s[down, across]
            value = (
                jnp.exp2(sv - row_s) - jnp.exp2(tv - row_t)
                + jnp.exp2(sv - col_norms[1, :, across]) - jnp.exp2(tv - col_norms[0, :, across])
            )
            delta[down, across] = value.astype(jnp.bfloat16)
        return carry

    for n, copies in enumerate(arrivals):
        for copy in copies:
            copy.wait()
        lax.fori_loop(n * tall // 16, (n + 1) * tall // 16, strip, 0, unroll=2)
    for load in loads:
        load.wait()

    place, core = lax.axis_index("img_0"), lax.axis_index("img_1")
    chips = lax.axis_size("img_0")
    tall = cols // chips
    half = tall // 2
    full_note = jnp.full((NOTE, thin), row_total, F32)

    def text_block(out, top, far, part, note):
        size = tall if part is None else half
        at = lax.rem(place + far + chips, chips) * tall
        across = pl.ds(pl.multiple_of(at, tall), tall)
        grad = scale * lax.dot_general(
            delta[:, across], si[...], (((0,), (0,)), ((), ())), preferred_element_type=F32
        )
        if part is not None:
            grad = jnp.where(part == 0, grad[:half], grad[half:])
        out[top : top + size, :] = grad
        out[top + size : top + size + NOTE, :] = note

    for out, flow in ((theirs, 1 - core), (mine, core)):
        sign = 1 - 2 * flow
        top = 0
        for far, part, note in (
            (2 * sign, None, full_note), (3 * sign, None, full_note), (sign, None, full_note),
            (chips // 2, flow, 0.5 * full_note), (0, flow, full_note),
        ):
            text_block(out, top, far, part, note)
            top += (tall if part is None else half) + NOTE
        if out is theirs:
            save = pltpu.make_async_copy(theirs, theirs_out, sems.at[0])
            save.start()

    save.wait()


def image_kernel(scale, delta, st, col_note, img_out, img_block, sems):
    rows = delta.shape[0]
    thin = st.shape[1]
    pieces, lines, _ = img_block.shape
    own = rows // pieces
    some = 4
    for k in range(pieces):
        img_block[k, lines - NOTE :, :] = col_note[...]
    saves = []
    for n in range(pieces // some):
        grad = scale * jnp.dot(
            delta[n * some * own : (n + 1) * some * own, :], st[...], preferred_element_type=F32
        )
        for k in range(some):
            for b in range(thin // LANES):
                img_block[n * some + k, b * own : (b + 1) * own, :] = grad[
                    k * own : (k + 1) * own, b * LANES : (b + 1) * LANES
                ]
        save = pltpu.make_async_copy(
            img_block.at[pl.ds(n * some, some)], img_out.at[pl.ds(n * some, some)], sems.at[n]
        )
        save.start()
        saves.append(save)

    for save in saves:
        save.wait()


def flow_rows(tall):
    full, part = tall + NOTE, tall // 2 + NOTE
    return (full, full, full, part, part)


def delta_and_text(row_parts, col_stats, t, s, student_txt, student_img, chips):
    rows, cols = t.shape
    thin = student_txt.shape[1]
    flow = (sum(flow_rows(cols // chips)), thin)
    return pl.pallas_call(
        functools.partial(delta_kernel, 3.0 / math.sqrt(thin)),
        name="delta_and_text_gradient",
        out_shape=(
            pltpu.VMEM((rows, cols), jnp.bfloat16), pltpu.HBM(flow, F32),
            jax.ShapeDtypeStruct(flow, F32), pltpu.VMEM(student_txt.shape, jnp.bfloat16),
            jax.ShapeDtypeStruct((NOTE, LANES), F32),
        ),
        in_specs=[WHOLE] * (len(row_parts) + 1) + [FAR] * 4,
        out_specs=(WHOLE, FAR, WHOLE, WHOLE, WHOLE),
        scratch_shapes=[
            pltpu.VMEM((2, rows, LANES), F32), pltpu.VMEM((2, 16, cols), F32),
            pltpu.VMEM((rows, cols), F32), pltpu.VMEM((rows, cols), F32),
            pltpu.VMEM(flow, F32), pltpu.VMEM(student_img.shape, jnp.bfloat16),
            pltpu.SemaphoreType.DMA((11,)),
        ],
        compiler_params=pltpu.CompilerParams(vmem_limit_bytes=VMEM_LIMIT),
        cost_estimate=cost(2 * rows * cols * thin, 8 * rows * cols, 4 * rows * cols),
    )(
        *row_parts, col_stats,
        *(
            pltpu.with_memory_space_constraint(x, pltpu.HBM)
            for x in (t, s, student_txt, student_img)
        ),
    )


def image_gradient(delta, student_txt, col_note, pieces):
    rows, cols = delta.shape
    thin = student_txt.shape[1]
    shape = (pieces, rows // pieces * thin // LANES + NOTE, LANES)
    return pl.pallas_call(
        functools.partial(image_kernel, 3.0 / math.sqrt(thin)),
        name="image_gradient",
        out_shape=pltpu.HBM(shape, F32),
        in_specs=[WHOLE] * 3,
        out_specs=FAR,
        scratch_shapes=[pltpu.VMEM(shape, F32), pltpu.SemaphoreType.DMA((pieces // 4,))],
        compiler_params=pltpu.CompilerParams(vmem_limit_bytes=16 * MIB),
        cost_estimate=cost(2 * rows * cols * thin, 4 * rows * thin + 2 * rows * cols),
    )(delta, student_txt, col_note)


def add_kernel(mine, theirs, *outs):
    top = 0
    for out in outs:
        down = slice(top, top + out.shape[0])
        out[...] = mine[down, :] + theirs[down, :]
        top += out.shape[0]


def added(mine, theirs, chips):
    thin = mine.shape[1]
    sizes = flow_rows(2 * (mine.shape[0] - 5 * NOTE) // chips)
    return pl.pallas_call(
        add_kernel,
        name="both_cores_text_terms",
        out_shape=[jax.ShapeDtypeStruct((size, thin), F32) for size in sizes],
        in_specs=[WHOLE] * 2,
        out_specs=[WHOLE] * len(sizes),
        compiler_params=pltpu.CompilerParams(vmem_limit_bytes=8 * MIB),
        cost_estimate=cost(mine.size, 12 * mine.size),
    )(mine, theirs)


def relay_kernel(near, full, *refs):
    out = refs[-1]
    out[...] = near[...] + full[...]
    if len(refs) > 1:
        part = refs[0]
        size = out.shape[0] - NOTE
        half = size // 2
        down = pl.ds(pl.multiple_of(lax.axis_index("img_1") * half, half), half)
        out[down, :] = out[down, :] + part[:half, :]
        out[size:, :] = out[size:, :] + part[half:, :]


def relayed(*parts):
    return pl.pallas_call(
        relay_kernel,
        name="relayed_text_terms",
        out_shape=jax.ShapeDtypeStruct(parts[0].shape, F32),
        in_specs=[WHOLE] * len(parts),
        out_specs=WHOLE,
        compiler_params=pltpu.CompilerParams(vmem_limit_bytes=4 * MIB),
        cost_estimate=cost(parts[0].size * 3, 12 * parts[0].size),
    )(*parts)


def sum_kernel(parts, out, note):
    own = out.shape[0]
    for b in range(out.shape[1] // LANES):
        total = parts[0, b * own : (b + 1) * own, :]
        for k in range(1, parts.shape[0]):
            total = total + parts[k, b * own : (b + 1) * own, :]
        out[:, b * LANES : (b + 1) * LANES] = total
    last = slice(parts.shape[1] - NOTE, parts.shape[1])
    total = parts[0, last, :]
    for k in range(1, parts.shape[0]):
        total = total + parts[k, last, :]
    note[...] = total


def summed(parts, thin):
    own = (parts.shape[1] - NOTE) * LANES // thin
    return pl.pallas_call(
        sum_kernel,
        name="sum_of_image_parts",
        out_shape=(jax.ShapeDtypeStruct((own, thin), F32), jax.ShapeDtypeStruct((NOTE, LANES), F32)),
        in_specs=[WHOLE],
        out_specs=(WHOLE, WHOLE),
        compiler_params=pltpu.CompilerParams(vmem_limit_bytes=4 * MIB),
        cost_estimate=cost(parts.size, 4 * parts.size),
    )(parts)


def finish_kernel(row_share, col_share, flow, other, own, col_note, out, loss):
    half = out.shape[0]
    core = lax.axis_index("img_1")
    down = pl.ds(pl.multiple_of(core * half, half), half)
    out[...] = flow[down, :] + other[down, :] + own[:half, :]
    row_note = flow[2 * half :, :LANES] + other[2 * half :, :LANES] + own[half:, :LANES]
    total = (0.5 * LN2) * (row_note * row_share + col_note[...] * col_share)
    loss[0, 0] = total[0, 0]


def finished(row_share, col_share, flow, other, own, col_note):
    thin = flow.shape[1]
    return pl.pallas_call(
        functools.partial(finish_kernel, row_share, col_share),
        name="text_gradient_and_loss",
        out_shape=(
            jax.ShapeDtypeStruct((own.shape[0] - NOTE, thin), F32),
            jax.ShapeDtypeStruct((1, 1), F32),
        ),
        in_specs=[WHOLE] * 4,
        out_specs=(WHOLE, pl.BlockSpec(memory_space=pltpu.SMEM)),
        compiler_params=pltpu.CompilerParams(vmem_limit_bytes=4 * MIB),
        cost_estimate=cost(own.size * 3, 16 * own.size),
    )(flow, other, own, col_note)


def turn(size, step):
    return [(k, (k + step) % size) for k in range(size)]


def body(teacher_img, teacher_txt, student_img, student_txt):
    rows = student_img.shape[0]
    cols, thin = student_txt.shape
    chips, cores = lax.axis_size("img_0"), lax.axis_size("img_1")
    img_count, txt_count = chips * cores, lax.axis_size(TXT)
    side = lax.axis_size("txt_0")

    t, s, row, col = local_stats(
        teacher_img, teacher_txt, student_img, student_txt, img_count
    )
    col = lax.all_to_all(col, IMG, 0, 0, tiled=True)
    row = row[0]
    for axis in TXT:
        others = [lax.ppermute(row, axis, turn(side, k)) for k in (1, 3, 2)]
        if axis == TXT[0]:
            (row,) = join(((0, 1, 2, 3),), row, *others)
    swap = turn(cores, 1)

    delta, theirs, mine, near_txt, col_note = delta_and_text(
        (row, *others), col, t, s, student_txt, student_img, chips
    )
    theirs = lax.ppermute(theirs, "img_1", swap)
    to_img = image_gradient(delta, near_txt, col_note, txt_count)
    got_img = lax.all_to_all(to_img, TXT, 0, 0, tiled=True)
    two, three, one, four, own = added(mine, theirs, chips)

    def outward(value, step):
        pairs = [
            (cores * z + c, cores * ((z + step * (1 - 2 * c)) % chips) + c)
            for z in range(chips) for c in range(cores)
        ]
        return lax.ppermute(value, IMG, pairs)

    four = outward(four, 2)
    flow = relayed(two, outward(three, 1), four)
    flow = relayed(one, outward(flow, 1))
    flow = outward(flow, 1)
    across = lax.ppermute(flow, "img_1", swap)
    grad_img, col_note = summed(got_img, thin)
    grad_txt, loss = finished(
        1.0 / (rows * img_count), 1.0 / (cols * txt_count), flow, across, own, col_note
    )
    return (loss.reshape(()), grad_img, grad_txt)


def solution(mesh):
    torus = Mesh(mesh.devices.reshape(8, 2, 4, 4), ("img_0", "img_1", "txt_0", "txt_1"))
    in_specs = (P(IMG, None), P(TXT, None), P(IMG, None), P(TXT, None))
    out_specs = (P(), P(IMG_TXT, None), P(TXT_IMG, None))
    return jax.shard_map(body, mesh=torus, in_specs=in_specs, out_specs=out_specs, check_vma=False)
```

```python
import functools
import math

import jax
import jax.numpy as jnp
from jax import lax
from jax.experimental import pallas as pl
from jax.experimental.pallas import tpu as pltpu
from jax.sharding import Mesh
from jax.sharding import PartitionSpec as P

IMG = ("img_0", "img_1")
TXT = ("txt_0", "txt_1")
IMG_TXT = ("img_0", "img_1", "txt_0", "txt_1")
TXT_IMG = ("txt_0", "txt_1", "img_0", "img_1")
LANES = 128
NOTE = 8
VMEM_LIMIT = 28 * 1024 * 1024
STATS_LIMIT = 32 * 1024 * 1024
LN2 = math.log(2.0)
F32 = jnp.float32
MIB = 1024 * 1024
WHOLE = pl.BlockSpec(memory_space=pltpu.VMEM)
FAR = pl.BlockSpec(memory_space=pltpu.HBM)


def cost(flops, size, transcendentals=0):
    return pl.CostEstimate(flops=flops, bytes_accessed=size, transcendentals=transcendentals)


def stats_kernel(scale_teach, scale_learn, ti_hbm, tt_hbm, si_hbm, st_hbm, t_hbm, s_hbm,
                 row_out, col_out, ti, tt, si, st, t, s, peaks, sums, col_peaks, col_sums, sems):
    rows, cols = t.shape
    tall = 256
    chunks = rows // tall

    def load(src, dst, at, size, which):
        copy = pltpu.make_async_copy(
            src.at[pl.ds(at, size), :], dst.at[pl.ds(at, size), :], sems.at[which]
        )
        copy.start()
        return copy

    st_load = load(st_hbm, st, 0, cols, 1 + chunks)
    si_load = load(si_hbm, si, 0, rows, 2 + chunks)
    tt_load = load(tt_hbm, tt, 0, cols, 0)

    saves = []

    def logits(left, right, out, far, scale, which, arrivals):
        for n in range(chunks):
            if arrivals:
                arrivals[n].wait()
            down = slice(n * tall, (n + 1) * tall)
            block = scale * lax.dot_general(
                left[down, :], right[...], (((1,), (1,)), ((), ())), preferred_element_type=F32
            )
            out[down, :] = block
            saves.append(load(out, far, n * tall, tall, sems.shape[0] - 1 - len(saves)))
            top = jnp.max(block.reshape(tall // 8, 8, cols), axis=0)
            col_peaks[which] = jnp.maximum(col_peaks[which], top) if n else top
            side = block[:, :LANES]
            for k in range(1, cols // LANES):
                side = jnp.maximum(side, block[:, k * LANES : (k + 1) * LANES])
            peaks[which, down, :] = jnp.broadcast_to(
                jnp.max(side, axis=1, keepdims=True), (tall, LANES)
            )
        col_peaks[which] = jnp.broadcast_to(
            jnp.max(col_peaks[which], axis=0, keepdims=True), (8, cols)
        )

    st_load.wait()
    si_load.wait()
    ti_loads = [load(ti_hbm, ti, n * tall, tall, 1 + n) for n in range(chunks)]
    logits(si, st, s, s_hbm, scale_learn, 1, None)
    tt_load.wait()
    logits(ti, tt, t, t_hbm, scale_teach, 0, ti_loads)

    group = 4 * LANES
    for h in range(cols // group):
        def strip(r, carry):
            at = pl.multiple_of(r * 8, 8)
            down = pl.ds(at, 8)
            row_peak_t, row_peak_s = peaks[0, down, :], peaks[1, down, :]
            row_t = row_s = row_g = None
            new = []
            for k in range(group // LANES):
                across = slice(h * group + k * LANES, h * group + (k + 1) * LANES)
                tv, sv = t[down, across], s[down, across]
                gap = tv - sv
                wr = jnp.exp2(tv - row_peak_t)
                vr = jnp.exp2(sv - row_peak_s)
                wc = jnp.exp2(tv - col_peaks[0, :, across])
                vc = jnp.exp2(sv - col_peaks[1, :, across])
                row_t = wr if row_t is None else row_t + wr
                row_s = vr if row_s is None else row_s + vr
                row_g = wr * gap if row_g is None else row_g + wr * gap
                ct, cs, cg = carry[3 * k : 3 * k + 3]
                new += [ct + wc, cs + vc, cg + wc * gap]
            for q, value in enumerate((row_t, row_s, row_g)):
                sums[q, down, :] = value + sums[q, down, :] if h else value
            return tuple(new)

        zeros = tuple(jnp.zeros((8, LANES), F32) for _ in range(3 * group // LANES))
        found = lax.fori_loop(0, rows // 8, strip, zeros, unroll=8)
        for k in range(group // LANES):
            across = slice(h * group + k * LANES, h * group + (k + 1) * LANES)
            for q in range(3):
                col_sums[q, :, across] = found[3 * k + q]

    def publish(out, peak_t, peak_s, mass_t, mass_s, gap):
        found = (peak_t + jnp.log2(mass_t), peak_s + jnp.log2(mass_s), gap / mass_t)
        for q, value in enumerate(found):
            for k in range(out.shape[0]):
                out[k, 8 * q : 8 * q + 8, :] = value

    def stacked(lines):
        return jnp.concatenate(lines, axis=0)

    def by_column(value):
        return stacked([value[:, b * LANES : (b + 1) * LANES] for b in range(cols // LANES)])

    publish(
        col_out, by_column(col_peaks[0, :1, :]), by_column(col_peaks[1, :1, :]),
        *(by_column(jnp.sum(col_sums[q], axis=0, keepdims=True)) for q in range(3)),
    )
    lane = lax.broadcasted_iota(jnp.int32, (rows, LANES), 1)
    packed = jnp.where(lane == 0, peaks[0], peaks[1])
    for q in range(3):
        packed = jnp.where(lane == 2 + q, jnp.sum(sums[q], axis=1, keepdims=True), packed)
    turned = [packed[b * LANES : (b + 1) * LANES, :].T for b in range(rows // LANES)]
    publish(row_out, *(stacked([block[q : q + 1, :] for block in turned]) for q in range(5)))
    for save in saves:
        save.wait()


def local_stats(teacher_img, teacher_txt, student_img, student_txt, copies):
    rows, deep = teacher_img.shape
    cols, thin = student_txt.shape
    kernel = functools.partial(
        stats_kernel, 3.0 / math.sqrt(deep) / LN2, 3.0 / math.sqrt(thin) / LN2
    )
    return pl.pallas_call(
        kernel,
        name="logits_and_statistics",
        out_shape=(
            pltpu.HBM((rows, cols), F32), pltpu.HBM((rows, cols), F32),
            jax.ShapeDtypeStruct((1, 3 * rows // LANES, LANES), F32),
            jax.ShapeDtypeStruct((copies, 3 * cols // LANES, LANES), F32),
        ),
        in_specs=[FAR] * 4,
        out_specs=(FAR, FAR, WHOLE, WHOLE),
        scratch_shapes=[
            pltpu.VMEM((rows, deep), jnp.bfloat16), pltpu.VMEM((cols, deep), jnp.bfloat16),
            pltpu.VMEM((rows, thin), jnp.bfloat16), pltpu.VMEM((cols, thin), jnp.bfloat16),
            pltpu.VMEM((rows, cols), F32), pltpu.VMEM((rows, cols), F32),
            pltpu.VMEM((2, rows, LANES), F32), pltpu.VMEM((3, rows, LANES), F32),
            pltpu.VMEM((2, 8, cols), F32), pltpu.VMEM((3, 8, cols), F32),
            pltpu.SemaphoreType.DMA((16,)),
        ],
        compiler_params=pltpu.CompilerParams(vmem_limit_bytes=STATS_LIMIT),
        cost_estimate=cost(2 * rows * cols * (deep + thin), 8 * rows * cols, 4 * rows * cols),
    )(*(
        pltpu.with_memory_space_constraint(x, pltpu.HBM)
        for x in (teacher_img, teacher_txt, student_img, student_txt)
    ))


def joined(parts):
    teach, learn, gap = ([part[8 * q : 8 * q + 8, :] for part in parts] for q in range(3))
    teach_peak = functools.reduce(jnp.maximum, teach)
    learn_peak = functools.reduce(jnp.maximum, learn)
    weights = [jnp.exp2(part - teach_peak) for part in teach]
    mass = sum(weights[1:], weights[0])
    shares = [jnp.exp2(part - learn_peak) for part in learn]
    gaps = [weight * part for weight, part in zip(weights, gap)]
    return (
        teach_peak + jnp.log2(mass),
        learn_peak + jnp.log2(sum(shares[1:], shares[0])),
        sum(gaps[1:], gaps[0]) / mass,
    )


def join_kernel(groups, *refs):
    sources, outs = refs[: len(refs) - len(groups)], refs[len(refs) - len(groups) :]
    for group, out in zip(groups, outs):
        for q, value in enumerate(joined([sources[k][...] for k in group])):
            out[8 * q : 8 * q + 8, :] = value


def join(groups, *parts):
    return pl.pallas_call(
        functools.partial(join_kernel, groups),
        name="joined_statistics",
        out_shape=[jax.ShapeDtypeStruct(parts[group[0]].shape, F32) for group in groups],
        in_specs=[WHOLE] * len(parts),
        out_specs=[WHOLE] * len(groups),
        compiler_params=pltpu.CompilerParams(vmem_limit_bytes=1 * MIB),
        cost_estimate=cost(parts[0].size * 20, parts[0].size * 4 * len(parts), parts[0].size * 4),
    )(*parts)


def delta_kernel(scale, *refs):
    row_parts = refs[:2]
    col_stats, t_far, s_far, st_far, si_far, delta, img_out, si, row_note = refs[2:11]
    row_norms, col_norms, t, s, st, img_block, sems = refs[11:]
    tall = 256
    arrivals = []
    for n in range(t.shape[0] // tall):
        down = pl.ds(n * tall, tall)
        arrivals.append([
            pltpu.make_async_copy(far.at[down, :], near.at[down, :], sems.at[2 + 2 * n + k])
            for k, (far, near) in enumerate(((t_far, t), (s_far, s)))
        ])
        for copy in arrivals[-1]:
            copy.start()
    loads = [
        pltpu.make_async_copy(src, dst, sems.at[k])
        for k, (src, dst) in enumerate(((st_far, st), (si_far, si)))
    ]
    for load in loads:
        load.start()
    rows, cols = t.shape
    thin = st.shape[1]
    row_teach, row_learn, row_mean = joined([part[...] for part in row_parts])
    col_teach, col_learn, col_mean = joined(
        [col_stats[k] for k in range(col_stats.shape[0])]
    )
    row_total = jnp.sum(row_mean + row_learn - row_teach)
    col_total = jnp.sum(col_mean + col_learn - col_teach)
    row_note[...] = jnp.full(row_note.shape, row_total, F32)
    for which, (down, across) in enumerate(((row_teach, col_teach), (row_learn, col_learn))):
        turned = jnp.concatenate([down - 3.0] * (LANES // 8), axis=0).T
        for b in range(8):
            row_norms[which, b * LANES : (b + 1) * LANES, :] = jnp.broadcast_to(
                turned[:, b : b + 1], (LANES, LANES)
            )
            col_norms[which, :, b * LANES : (b + 1) * LANES] = jnp.broadcast_to(
                across[b : b + 1, :] - 3.0, (16, LANES)
            )

    def strip(r, carry):
        down = pl.ds(pl.multiple_of(r * 16, 16), 16)
        row_t, row_s = row_norms[0, down, :], row_norms[1, down, :]
        for k in range(cols // LANES):
            across = slice(k * LANES, (k + 1) * LANES)
            tv, sv = t[down, across], s[down, across]
            value = (
                jnp.exp2(sv - row_s) - jnp.exp2(tv - row_t)
                + jnp.exp2(sv - col_norms[1, :, across]) - jnp.exp2(tv - col_norms[0, :, across])
            )
            delta[down, across] = value.astype(jnp.bfloat16)
        return carry

    for n, copies in enumerate(arrivals):
        for copy in copies:
            copy.wait()
        lax.fori_loop(n * tall // 16, (n + 1) * tall // 16, strip, 0, unroll=2)
    for load in loads:
        load.wait()

    pieces, lines, _ = img_block.shape
    own = rows // pieces
    some = 4
    for k in range(pieces):
        img_block[k, lines - NOTE :, :] = jnp.full((NOTE, LANES), col_total, F32)
    saves = []
    for n in range(pieces // some):
        grad = scale * jnp.dot(
            delta[n * some * own : (n + 1) * some * own, :], st[...], preferred_element_type=F32
        )
        for k in range(some):
            for b in range(thin // LANES):
                img_block[n * some + k, b * own : (b + 1) * own, :] = grad[
                    k * own : (k + 1) * own, b * LANES : (b + 1) * LANES
                ]
        save = pltpu.make_async_copy(
            img_block.at[pl.ds(n * some, some)], img_out.at[pl.ds(n * some, some)], sems.at[10 + n]
        )
        save.start()
        saves.append(save)

    for save in saves:
        save.wait()


def text_kernel(scale, delta, si, row_note, theirs_out, mine, theirs, sem):
    cols = delta.shape[1]
    thin = si.shape[1]
    place, core = lax.axis_index("img_0"), lax.axis_index("img_1")
    chips = lax.axis_size("img_0")
    tall = cols // chips
    half = tall // 2
    full_note = row_note[...]

    def text_block(out, top, far, part, note):
        size = tall if part is None else half
        at = lax.rem(place + far + chips, chips) * tall
        across = pl.ds(pl.multiple_of(at, tall), tall)
        grad = scale * lax.dot_general(
            delta[:, across], si[...], (((0,), (0,)), ((), ())), preferred_element_type=F32
        )
        if part is not None:
            grad = jnp.where(part == 0, grad[:half], grad[half:])
        out[top : top + size, :] = grad
        out[top + size : top + size + NOTE, :] = note

    for out, flow in ((theirs, 1 - core), (mine, core)):
        sign = 1 - 2 * flow
        top = 0
        for far, part, note in (
            (2 * sign, None, full_note), (3 * sign, None, full_note), (sign, None, full_note),
            (chips // 2, flow, 0.5 * full_note), (0, flow, full_note),
        ):
            text_block(out, top, far, part, note)
            top += (tall if part is None else half) + NOTE
        if out is theirs:
            save = pltpu.make_async_copy(theirs, theirs_out, sem)
            save.start()

    save.wait()


def flow_rows(tall):
    full, part = tall + NOTE, tall // 2 + NOTE
    return (full, full, full, part, part)


def delta_and_image(row_parts, col_stats, t, s, student_txt, student_img, pieces):
    rows, cols = t.shape
    thin = student_txt.shape[1]
    shape = (pieces, rows // pieces * thin // LANES + NOTE, LANES)
    return pl.pallas_call(
        functools.partial(delta_kernel, 3.0 / math.sqrt(thin)),
        name="delta_and_image_gradient",
        out_shape=(
            pltpu.VMEM((rows, cols), jnp.bfloat16), pltpu.HBM(shape, F32),
            pltpu.VMEM(student_img.shape, jnp.bfloat16),
            jax.ShapeDtypeStruct((NOTE, thin), F32),
        ),
        in_specs=[WHOLE] * (len(row_parts) + 1) + [FAR] * 4,
        out_specs=(WHOLE, FAR, WHOLE, WHOLE),
        scratch_shapes=[
            pltpu.VMEM((2, rows, LANES), F32), pltpu.VMEM((2, 16, cols), F32),
            pltpu.VMEM((rows, cols), F32), pltpu.VMEM((rows, cols), F32),
            pltpu.VMEM(student_txt.shape, jnp.bfloat16), pltpu.VMEM(shape, F32),
            pltpu.SemaphoreType.DMA((10 + pieces // 4,)),
        ],
        compiler_params=pltpu.CompilerParams(vmem_limit_bytes=VMEM_LIMIT),
        cost_estimate=cost(2 * rows * cols * thin, 8 * rows * cols, 4 * rows * cols),
    )(
        *row_parts, col_stats,
        *(
            pltpu.with_memory_space_constraint(x, pltpu.HBM)
            for x in (t, s, student_txt, student_img)
        ),
    )


def text_gradient(delta, student_img, row_note, chips):
    rows, cols = delta.shape
    thin = student_img.shape[1]
    flow = (sum(flow_rows(cols // chips)), thin)
    return pl.pallas_call(
        functools.partial(text_kernel, 3.0 / math.sqrt(thin)),
        name="text_gradient",
        out_shape=(pltpu.HBM(flow, F32), jax.ShapeDtypeStruct(flow, F32)),
        in_specs=[WHOLE] * 3,
        out_specs=(FAR, WHOLE),
        scratch_shapes=[pltpu.VMEM(flow, F32), pltpu.SemaphoreType.DMA],
        compiler_params=pltpu.CompilerParams(vmem_limit_bytes=16 * MIB),
        cost_estimate=cost(2 * rows * cols * thin, 4 * rows * thin + 2 * rows * cols),
    )(delta, student_img, row_note)


def add_kernel(mine, theirs, *outs):
    top = 0
    for out in outs:
        down = slice(top, top + out.shape[0])
        out[...] = mine[down, :] + theirs[down, :]
        top += out.shape[0]


def added(mine, theirs, chips):
    thin = mine.shape[1]
    sizes = flow_rows(2 * (mine.shape[0] - 5 * NOTE) // chips)
    return pl.pallas_call(
        add_kernel,
        name="both_cores_text_terms",
        out_shape=[jax.ShapeDtypeStruct((size, thin), F32) for size in sizes],
        in_specs=[WHOLE] * 2,
        out_specs=[WHOLE] * len(sizes),
        compiler_params=pltpu.CompilerParams(vmem_limit_bytes=8 * MIB),
        cost_estimate=cost(mine.size, 12 * mine.size),
    )(mine, theirs)


def relay_kernel(near, full, *refs):
    out = refs[-1]
    out[...] = near[...] + full[...]
    if len(refs) > 1:
        part = refs[0]
        size = out.shape[0] - NOTE
        half = size // 2
        down = pl.ds(pl.multiple_of(lax.axis_index("img_1") * half, half), half)
        out[down, :] = out[down, :] + part[:half, :]
        out[size:, :] = out[size:, :] + part[half:, :]


def relayed(*parts):
    return pl.pallas_call(
        relay_kernel,
        name="relayed_text_terms",
        out_shape=jax.ShapeDtypeStruct(parts[0].shape, F32),
        in_specs=[WHOLE] * len(parts),
        out_specs=WHOLE,
        compiler_params=pltpu.CompilerParams(vmem_limit_bytes=4 * MIB),
        cost_estimate=cost(parts[0].size * 3, 12 * parts[0].size),
    )(*parts)


def finish_kernel(flow, other, own, out, note):
    half = out.shape[0]
    down = pl.ds(pl.multiple_of(lax.axis_index("img_1") * half, half), half)
    out[...] = flow[down, :] + other[down, :] + own[:half, :]
    note[...] = flow[2 * half :, :LANES] + other[2 * half :, :LANES] + own[half:, :LANES]


def finished(flow, other, own):
    thin = flow.shape[1]
    return pl.pallas_call(
        finish_kernel,
        name="text_gradient_total",
        out_shape=(
            jax.ShapeDtypeStruct((own.shape[0] - NOTE, thin), F32),
            jax.ShapeDtypeStruct((NOTE, LANES), F32),
        ),
        in_specs=[WHOLE] * 3,
        out_specs=(WHOLE, WHOLE),
        compiler_params=pltpu.CompilerParams(vmem_limit_bytes=4 * MIB),
        cost_estimate=cost(own.size * 3, 16 * own.size),
    )(flow, other, own)


def sum_kernel(row_share, col_share, parts, row_note, out, loss):
    own = out.shape[0]

    def total(down):
        return functools.reduce(jnp.add, [parts[k, down, :] for k in range(parts.shape[0])])

    for b in range(out.shape[1] // LANES):
        out[:, b * LANES : (b + 1) * LANES] = total(slice(b * own, (b + 1) * own))
    col_note = total(slice(parts.shape[1] - NOTE, parts.shape[1]))
    both = (0.5 * LN2) * (row_note[...] * row_share + col_note * col_share)
    loss[0, 0] = both[0, 0]


def summed(row_share, col_share, parts, row_note, thin):
    own = (parts.shape[1] - NOTE) * LANES // thin
    return pl.pallas_call(
        functools.partial(sum_kernel, row_share, col_share),
        name="sum_of_image_parts_and_loss",
        out_shape=(jax.ShapeDtypeStruct((own, thin), F32), jax.ShapeDtypeStruct((1, 1), F32)),
        in_specs=[WHOLE] * 2,
        out_specs=(WHOLE, pl.BlockSpec(memory_space=pltpu.SMEM)),
        compiler_params=pltpu.CompilerParams(vmem_limit_bytes=4 * MIB),
        cost_estimate=cost(parts.size, 4 * parts.size),
    )(parts, row_note)


def turn(size, step):
    return [(k, (k + step) % size) for k in range(size)]


def body(teacher_img, teacher_txt, student_img, student_txt):
    rows = student_img.shape[0]
    cols, thin = student_txt.shape
    chips, cores = lax.axis_size("img_0"), lax.axis_size("img_1")
    img_count, txt_count = chips * cores, lax.axis_size(TXT)
    side = lax.axis_size("txt_0")

    t, s, row, col = local_stats(
        teacher_img, teacher_txt, student_img, student_txt, img_count
    )
    col = lax.all_to_all(col, IMG, 0, 0, tiled=True)
    row = row[0]
    for axis in TXT:
        for first in (0, 1):
            pairs = [(k, (k + 1 - 2 * ((k + first) % 2)) % side) for k in range(side)]
            other = lax.ppermute(row, axis, pairs)
            if (axis, first) != (TXT[1], 1):
                (row,) = join(((0, 1),), row, other)
    swap = turn(cores, 1)

    delta, to_img, near_img, row_note = delta_and_image(
        (row, other), col, t, s, student_txt, student_img, txt_count
    )
    got_img = lax.all_to_all(to_img, TXT, 0, 0, tiled=True)
    theirs, mine = text_gradient(delta, near_img, row_note, chips)
    theirs = lax.ppermute(theirs, "img_1", swap)
    two, three, one, four, own = added(mine, theirs, chips)

    def outward(value, step):
        pairs = [
            (cores * z + c, cores * ((z + step * (1 - 2 * c)) % chips) + c)
            for z in range(chips) for c in range(cores)
        ]
        return lax.ppermute(value, IMG, pairs)

    four = outward(four, 2)
    flow = relayed(two, outward(three, 1), four)
    flow = relayed(one, outward(flow, 1))
    flow = outward(flow, 1)
    across = lax.ppermute(flow, "img_1", swap)
    grad_txt, row_total = finished(flow, across, own)
    grad_img, loss = summed(
        1.0 / (rows * img_count), 1.0 / (cols * txt_count), got_img, row_total, thin
    )
    return (loss.reshape(()), grad_img, grad_txt)


def solution(mesh):
    torus = Mesh(mesh.devices.reshape(8, 2, 4, 4), ("img_0", "img_1", "txt_0", "txt_1"))
    in_specs = (P(IMG, None), P(TXT, None), P(IMG, None), P(TXT, None))
    out_specs = (P(), P(IMG_TXT, None), P(TXT_IMG, None))
    return jax.shard_map(body, mesh=torus, in_specs=in_specs, out_specs=out_specs, check_vma=False)
```

```python
import functools
import math

import jax
import jax.numpy as jnp
from jax import lax
from jax.experimental import pallas as pl
from jax.experimental.pallas import tpu as pltpu
from jax.sharding import Mesh
from jax.sharding import PartitionSpec as P

IMG = ("img_0", "img_1")
TXT = ("txt_0", "txt_1")
IMG_TXT = ("img_0", "img_1", "txt_0", "txt_1")
TXT_IMG = ("txt_0", "txt_1", "img_0", "img_1")
LANES = 128
NOTE = 8
VMEM_LIMIT = 28 * 1024 * 1024
STATS_LIMIT = 32 * 1024 * 1024
LN2 = math.log(2.0)
F32 = jnp.float32
MIB = 1024 * 1024
WHOLE = pl.BlockSpec(memory_space=pltpu.VMEM)
FAR = pl.BlockSpec(memory_space=pltpu.HBM)


def cost(flops, size, transcendentals=0):
    return pl.CostEstimate(flops=flops, bytes_accessed=size, transcendentals=transcendentals)


def stats_kernel(scale_teach, scale_learn, ti_hbm, tt_hbm, si_hbm, st_hbm, t_hbm, s_hbm,
                 row_out, col_out, ti, tt, si, st, t, s, peaks, sums, col_peaks, col_sums, sems):
    rows, cols = t.shape
    tall = 256
    chunks = rows // tall

    def load(src, dst, at, size, which):
        copy = pltpu.make_async_copy(
            src.at[pl.ds(at, size), :], dst.at[pl.ds(at, size), :], sems.at[which]
        )
        copy.start()
        return copy

    st_load = load(st_hbm, st, 0, cols, 1 + chunks)
    si_load = load(si_hbm, si, 0, rows, 2 + chunks)
    tt_load = load(tt_hbm, tt, 0, cols, 0)

    saves = []

    def logits(left, right, out, far, scale, which, arrivals):
        for n in range(chunks):
            if arrivals:
                arrivals[n].wait()
            down = slice(n * tall, (n + 1) * tall)
            block = scale * lax.dot_general(
                left[down, :], right[...], (((1,), (1,)), ((), ())), preferred_element_type=F32
            )
            out[down, :] = block
            saves.append(load(out, far, n * tall, tall, sems.shape[0] - 1 - len(saves)))
            top = jnp.max(block.reshape(tall // 8, 8, cols), axis=0)
            col_peaks[which] = jnp.maximum(col_peaks[which], top) if n else top
            side = block[:, :LANES]
            for k in range(1, cols // LANES):
                side = jnp.maximum(side, block[:, k * LANES : (k + 1) * LANES])
            peaks[which, down, :] = jnp.broadcast_to(
                jnp.max(side, axis=1, keepdims=True), (tall, LANES)
            )
        col_peaks[which] = jnp.broadcast_to(
            jnp.max(col_peaks[which], axis=0, keepdims=True), (8, cols)
        )

    st_load.wait()
    si_load.wait()
    ti_loads = [load(ti_hbm, ti, n * tall, tall, 1 + n) for n in range(chunks)]
    logits(si, st, s, s_hbm, scale_learn, 1, None)
    tt_load.wait()
    logits(ti, tt, t, t_hbm, scale_teach, 0, ti_loads)

    group = 4 * LANES
    for h in range(cols // group):
        def strip(r, carry):
            at = pl.multiple_of(r * 8, 8)
            down = pl.ds(at, 8)
            row_peak_t, row_peak_s = peaks[0, down, :], peaks[1, down, :]
            row_t = row_s = row_g = None
            new = []
            for k in range(group // LANES):
                across = slice(h * group + k * LANES, h * group + (k + 1) * LANES)
                tv, sv = t[down, across], s[down, across]
                gap = tv - sv
                wr = jnp.exp2(tv - row_peak_t)
                vr = jnp.exp2(sv - row_peak_s)
                wc = jnp.exp2(tv - col_peaks[0, :, across])
                vc = jnp.exp2(sv - col_peaks[1, :, across])
                row_t = wr if row_t is None else row_t + wr
                row_s = vr if row_s is None else row_s + vr
                row_g = wr * gap if row_g is None else row_g + wr * gap
                ct, cs, cg = carry[3 * k : 3 * k + 3]
                new += [ct + wc, cs + vc, cg + wc * gap]
            for q, value in enumerate((row_t, row_s, row_g)):
                sums[q, down, :] = value + sums[q, down, :] if h else value
            return tuple(new)

        zeros = tuple(jnp.zeros((8, LANES), F32) for _ in range(3 * group // LANES))
        found = lax.fori_loop(0, rows // 8, strip, zeros, unroll=8)
        for k in range(group // LANES):
            across = slice(h * group + k * LANES, h * group + (k + 1) * LANES)
            for q in range(3):
                col_sums[q, :, across] = found[3 * k + q]

    def publish(out, peak_t, peak_s, mass_t, mass_s, gap):
        found = (peak_t + jnp.log2(mass_t), peak_s + jnp.log2(mass_s), gap / mass_t)
        for q, value in enumerate(found):
            for k in range(out.shape[0]):
                out[k, 8 * q : 8 * q + 8, :] = value

    def stacked(lines):
        return jnp.concatenate(lines, axis=0)

    def by_column(value):
        return stacked([value[:, b * LANES : (b + 1) * LANES] for b in range(cols // LANES)])

    publish(
        col_out, by_column(col_peaks[0, :1, :]), by_column(col_peaks[1, :1, :]),
        *(by_column(jnp.sum(col_sums[q], axis=0, keepdims=True)) for q in range(3)),
    )
    lane = lax.broadcasted_iota(jnp.int32, (rows, LANES), 1)
    packed = jnp.where(lane == 0, peaks[0], peaks[1])
    for q in range(3):
        packed = jnp.where(lane == 2 + q, jnp.sum(sums[q], axis=1, keepdims=True), packed)
    turned = [packed[b * LANES : (b + 1) * LANES, :].T for b in range(rows // LANES)]
    publish(row_out, *(stacked([block[q : q + 1, :] for block in turned]) for q in range(5)))
    for save in saves:
        save.wait()


def local_stats(teacher_img, teacher_txt, student_img, student_txt, copies):
    rows, deep = teacher_img.shape
    cols, thin = student_txt.shape
    kernel = functools.partial(
        stats_kernel, 3.0 / math.sqrt(deep) / LN2, 3.0 / math.sqrt(thin) / LN2
    )
    return pl.pallas_call(
        kernel,
        name="logits_and_statistics",
        out_shape=(
            pltpu.HBM((rows, cols), F32), pltpu.HBM((rows, cols), F32),
            jax.ShapeDtypeStruct((1, 3 * rows // LANES, LANES), F32),
            jax.ShapeDtypeStruct((copies, 3 * cols // LANES, LANES), F32),
        ),
        in_specs=[FAR] * 4,
        out_specs=(FAR, FAR, WHOLE, WHOLE),
        scratch_shapes=[
            pltpu.VMEM((rows, deep), jnp.bfloat16), pltpu.VMEM((cols, deep), jnp.bfloat16),
            pltpu.VMEM((rows, thin), jnp.bfloat16), pltpu.VMEM((cols, thin), jnp.bfloat16),
            pltpu.VMEM((rows, cols), F32), pltpu.VMEM((rows, cols), F32),
            pltpu.VMEM((2, rows, LANES), F32), pltpu.VMEM((3, rows, LANES), F32),
            pltpu.VMEM((2, 8, cols), F32), pltpu.VMEM((3, 8, cols), F32),
            pltpu.SemaphoreType.DMA((16,)),
        ],
        compiler_params=pltpu.CompilerParams(vmem_limit_bytes=STATS_LIMIT),
        cost_estimate=cost(2 * rows * cols * (deep + thin), 8 * rows * cols, 4 * rows * cols),
    )(*(
        pltpu.with_memory_space_constraint(x, pltpu.HBM)
        for x in (teacher_img, teacher_txt, student_img, student_txt)
    ))


def joined(parts):
    teach, learn, gap = ([part[8 * q : 8 * q + 8, :] for part in parts] for q in range(3))
    teach_peak = functools.reduce(jnp.maximum, teach)
    learn_peak = functools.reduce(jnp.maximum, learn)
    weights = [jnp.exp2(part - teach_peak) for part in teach]
    mass = sum(weights[1:], weights[0])
    shares = [jnp.exp2(part - learn_peak) for part in learn]
    gaps = [weight * part for weight, part in zip(weights, gap)]
    return (
        teach_peak + jnp.log2(mass),
        learn_peak + jnp.log2(sum(shares[1:], shares[0])),
        sum(gaps[1:], gaps[0]) / mass,
    )


def join_kernel(groups, *refs):
    sources, outs = refs[: len(refs) - len(groups)], refs[len(refs) - len(groups) :]
    for group, out in zip(groups, outs):
        for q, value in enumerate(joined([sources[k][...] for k in group])):
            out[8 * q : 8 * q + 8, :] = value


def join(groups, *parts):
    return pl.pallas_call(
        functools.partial(join_kernel, groups),
        name="joined_statistics",
        out_shape=[jax.ShapeDtypeStruct(parts[group[0]].shape, F32) for group in groups],
        in_specs=[WHOLE] * len(parts),
        out_specs=[WHOLE] * len(groups),
        compiler_params=pltpu.CompilerParams(vmem_limit_bytes=1 * MIB),
        cost_estimate=cost(parts[0].size * 20, parts[0].size * 4 * len(parts), parts[0].size * 4),
    )(*parts)


def delta_kernel(scale, *refs):
    row_parts = refs[:2]
    col_stats, t_far, s_far, st_far, si_far, delta, theirs_out, mine, st, col_note = refs[2:12]
    row_norms, col_norms, t, s, theirs, si, grads, sems = refs[12:]
    tall = 256
    arrivals = []
    for n in range(t.shape[0] // tall):
        down = pl.ds(n * tall, tall)
        arrivals.append([
            pltpu.make_async_copy(far.at[down, :], near.at[down, :], sems.at[3 + 2 * n + k])
            for k, (far, near) in enumerate(((t_far, t), (s_far, s)))
        ])
        for copy in arrivals[-1]:
            copy.start()
    loads = [
        pltpu.make_async_copy(src, dst, sems.at[1 + k])
        for k, (src, dst) in enumerate(((st_far, st), (si_far, si)))
    ]
    for load in loads:
        load.start()
    rows, cols = t.shape
    thin = st.shape[1]
    row_teach, row_learn, row_mean = joined([part[...] for part in row_parts])
    col_teach, col_learn, col_mean = joined(
        [col_stats[k] for k in range(col_stats.shape[0])]
    )
    row_total = jnp.sum(row_mean + row_learn - row_teach)
    col_total = jnp.sum(col_mean + col_learn - col_teach)
    col_note[...] = jnp.full(col_note.shape, col_total, F32)
    for which, (down, across) in enumerate(((row_teach, col_teach), (row_learn, col_learn))):
        turned = jnp.concatenate([down - 3.0] * (LANES // 8), axis=0).T
        for b in range(8):
            row_norms[which, b * LANES : (b + 1) * LANES, :] = jnp.broadcast_to(
                turned[:, b : b + 1], (LANES, LANES)
            )
            col_norms[which, :, b * LANES : (b + 1) * LANES] = jnp.broadcast_to(
                across[b : b + 1, :] - 3.0, (16, LANES)
            )

    def strip(r, carry):
        down = pl.ds(pl.multiple_of(r * 16, 16), 16)
        row_t, row_s = row_norms[0, down, :], row_norms[1, down, :]
        for k in range(cols // LANES):
            across = slice(k * LANES, (k + 1) * LANES)
            tv, sv = t[down, across], s[down, across]
            value = (
                jnp.exp2(sv - row_s) - jnp.exp2(tv - row_t)
                + jnp.exp2(sv - col_norms[1, :, across]) - jnp.exp2(tv - col_norms[0, :, across])
            )
            delta[down, across] = value.astype(jnp.bfloat16)
        return carry

    for n, copies in enumerate(arrivals):
        for copy in copies:
            copy.wait()
        lax.fori_loop(n * tall // 16, (n + 1) * tall // 16, strip, 0, unroll=2)
    for load in loads:
        load.wait()

    place, core = lax.axis_index("img_0"), lax.axis_index("img_1")
    chips = lax.axis_size("img_0")
    tall = cols // chips
    half = tall // 2
    full_note = jnp.full((NOTE, thin), row_total, F32)

    wide = 256
    for n in range(cols // wide):
        grads[n * wide : (n + 1) * wide, :] = scale * lax.dot_general(
            delta[:, n * wide : (n + 1) * wide], si[...], (((0,), (0,)), ((), ())),
            preferred_element_type=F32,
        )

    def text_block(out, top, far, part, note):
        size = tall if part is None else half
        at = lax.rem(place + far + chips, chips) * tall
        if part is not None:
            at = at + part * half
        out[top : top + size, :] = grads[pl.ds(pl.multiple_of(at, half), size), :]
        out[top + size : top + size + NOTE, :] = note

    for out, flow in ((theirs, 1 - core), (mine, core)):
        sign = 1 - 2 * flow
        top = 0
        for far, part, note in (
            (2 * sign, None, full_note), (3 * sign, None, full_note), (sign, None, full_note),
            (chips // 2, flow, 0.5 * full_note), (0, flow, full_note),
        ):
            text_block(out, top, far, part, note)
            top += (tall if part is None else half) + NOTE
        if out is theirs:
            save = pltpu.make_async_copy(theirs, theirs_out, sems.at[0])
            save.start()

    save.wait()


def image_kernel(scale, delta, st, col_note, img_out, img_block, sems):
    rows = delta.shape[0]
    thin = st.shape[1]
    pieces, lines, _ = img_block.shape
    own = rows // pieces
    some = 4
    for k in range(pieces):
        img_block[k, lines - NOTE :, :] = col_note[...]
    saves = []
    for n in range(pieces // some):
        grad = scale * jnp.dot(
            delta[n * some * own : (n + 1) * some * own, :], st[...], preferred_element_type=F32
        )
        for k in range(some):
            for b in range(thin // LANES):
                img_block[n * some + k, b * own : (b + 1) * own, :] = grad[
                    k * own : (k + 1) * own, b * LANES : (b + 1) * LANES
                ]
        save = pltpu.make_async_copy(
            img_block.at[pl.ds(n * some, some)], img_out.at[pl.ds(n * some, some)], sems.at[n]
        )
        save.start()
        saves.append(save)

    for save in saves:
        save.wait()


def flow_rows(tall):
    full, part = tall + NOTE, tall // 2 + NOTE
    return (full, full, full, part, part)


def delta_and_text(row_parts, col_stats, t, s, student_txt, student_img, chips):
    rows, cols = t.shape
    thin = student_txt.shape[1]
    flow = (sum(flow_rows(cols // chips)), thin)
    return pl.pallas_call(
        functools.partial(delta_kernel, 3.0 / math.sqrt(thin)),
        name="delta_and_text_gradient",
        out_shape=(
            pltpu.VMEM((rows, cols), jnp.bfloat16), pltpu.HBM(flow, F32),
            jax.ShapeDtypeStruct(flow, F32), pltpu.VMEM(student_txt.shape, jnp.bfloat16),
            jax.ShapeDtypeStruct((NOTE, LANES), F32),
        ),
        in_specs=[WHOLE] * (len(row_parts) + 1) + [FAR] * 4,
        out_specs=(WHOLE, FAR, WHOLE, WHOLE, WHOLE),
        scratch_shapes=[
            pltpu.VMEM((2, rows, LANES), F32), pltpu.VMEM((2, 16, cols), F32),
            pltpu.VMEM((rows, cols), F32), pltpu.VMEM((rows, cols), F32),
            pltpu.VMEM(flow, F32), pltpu.VMEM(student_img.shape, jnp.bfloat16),
            pltpu.VMEM((cols, thin), F32), pltpu.SemaphoreType.DMA((11,)),
        ],
        compiler_params=pltpu.CompilerParams(vmem_limit_bytes=VMEM_LIMIT),
        cost_estimate=cost(2 * rows * cols * thin, 8 * rows * cols, 4 * rows * cols),
    )(
        *row_parts, col_stats,
        *(
            pltpu.with_memory_space_constraint(x, pltpu.HBM)
            for x in (t, s, student_txt, student_img)
        ),
    )


def image_gradient(delta, student_txt, col_note, pieces):
    rows, cols = delta.shape
    thin = student_txt.shape[1]
    shape = (pieces, rows // pieces * thin // LANES + NOTE, LANES)
    return pl.pallas_call(
        functools.partial(image_kernel, 3.0 / math.sqrt(thin)),
        name="image_gradient",
        out_shape=pltpu.HBM(shape, F32),
        in_specs=[WHOLE] * 3,
        out_specs=FAR,
        scratch_shapes=[pltpu.VMEM(shape, F32), pltpu.SemaphoreType.DMA((pieces // 4,))],
        compiler_params=pltpu.CompilerParams(vmem_limit_bytes=16 * MIB),
        cost_estimate=cost(2 * rows * cols * thin, 4 * rows * thin + 2 * rows * cols),
    )(delta, student_txt, col_note)


def add_kernel(mine, theirs, *outs):
    top = 0
    for out in outs:
        down = slice(top, top + out.shape[0])
        out[...] = mine[down, :] + theirs[down, :]
        top += out.shape[0]


def added(mine, theirs, chips):
    thin = mine.shape[1]
    sizes = flow_rows(2 * (mine.shape[0] - 5 * NOTE) // chips)
    return pl.pallas_call(
        add_kernel,
        name="both_cores_text_terms",
        out_shape=[jax.ShapeDtypeStruct((size, thin), F32) for size in sizes],
        in_specs=[WHOLE] * 2,
        out_specs=[WHOLE] * len(sizes),
        compiler_params=pltpu.CompilerParams(vmem_limit_bytes=8 * MIB),
        cost_estimate=cost(mine.size, 12 * mine.size),
    )(mine, theirs)


def relay_kernel(near, full, *refs):
    out = refs[-1]
    out[...] = near[...] + full[...]
    if len(refs) > 1:
        part = refs[0]
        size = out.shape[0] - NOTE
        half = size // 2
        down = pl.ds(pl.multiple_of(lax.axis_index("img_1") * half, half), half)
        out[down, :] = out[down, :] + part[:half, :]
        out[size:, :] = out[size:, :] + part[half:, :]


def relayed(*parts):
    return pl.pallas_call(
        relay_kernel,
        name="relayed_text_terms",
        out_shape=jax.ShapeDtypeStruct(parts[0].shape, F32),
        in_specs=[WHOLE] * len(parts),
        out_specs=WHOLE,
        compiler_params=pltpu.CompilerParams(vmem_limit_bytes=4 * MIB),
        cost_estimate=cost(parts[0].size * 3, 12 * parts[0].size),
    )(*parts)


def finish_kernel(flow, other, own, out, note):
    half = out.shape[0]
    down = pl.ds(pl.multiple_of(lax.axis_index("img_1") * half, half), half)
    out[...] = flow[down, :] + other[down, :] + own[:half, :]
    note[...] = flow[2 * half :, :LANES] + other[2 * half :, :LANES] + own[half:, :LANES]


def finished(flow, other, own):
    thin = flow.shape[1]
    return pl.pallas_call(
        finish_kernel,
        name="text_gradient_total",
        out_shape=(
            jax.ShapeDtypeStruct((own.shape[0] - NOTE, thin), F32),
            jax.ShapeDtypeStruct((NOTE, LANES), F32),
        ),
        in_specs=[WHOLE] * 3,
        out_specs=(WHOLE, WHOLE),
        compiler_params=pltpu.CompilerParams(vmem_limit_bytes=4 * MIB),
        cost_estimate=cost(own.size * 3, 16 * own.size),
    )(flow, other, own)


def sum_kernel(row_share, col_share, parts, row_note, out, loss):
    own = out.shape[0]

    def total(down):
        return functools.reduce(jnp.add, [parts[k, down, :] for k in range(parts.shape[0])])

    for b in range(out.shape[1] // LANES):
        out[:, b * LANES : (b + 1) * LANES] = total(slice(b * own, (b + 1) * own))
    col_note = total(slice(parts.shape[1] - NOTE, parts.shape[1]))
    both = (0.5 * LN2) * (row_note[...] * row_share + col_note * col_share)
    loss[0, 0] = both[0, 0]


def summed(row_share, col_share, parts, row_note, thin):
    own = (parts.shape[1] - NOTE) * LANES // thin
    return pl.pallas_call(
        functools.partial(sum_kernel, row_share, col_share),
        name="sum_of_image_parts_and_loss",
        out_shape=(jax.ShapeDtypeStruct((own, thin), F32), jax.ShapeDtypeStruct((1, 1), F32)),
        in_specs=[WHOLE] * 2,
        out_specs=(WHOLE, pl.BlockSpec(memory_space=pltpu.SMEM)),
        compiler_params=pltpu.CompilerParams(vmem_limit_bytes=4 * MIB),
        cost_estimate=cost(parts.size, 4 * parts.size),
    )(parts, row_note)


def turn(size, step):
    return [(k, (k + step) % size) for k in range(size)]


def body(teacher_img, teacher_txt, student_img, student_txt):
    rows = student_img.shape[0]
    cols, thin = student_txt.shape
    chips, cores = lax.axis_size("img_0"), lax.axis_size("img_1")
    img_count, txt_count = chips * cores, lax.axis_size(TXT)
    side = lax.axis_size("txt_0")

    t, s, row, col = local_stats(
        teacher_img, teacher_txt, student_img, student_txt, img_count
    )
    col = lax.all_to_all(col, IMG, 0, 0, tiled=True)
    row = row[0]
    for axis in TXT:
        for first in (0, 1):
            pairs = [(k, (k + 1 - 2 * ((k + first) % 2)) % side) for k in range(side)]
            other = lax.ppermute(row, axis, pairs)
            if (axis, first) != (TXT[1], 1):
                (row,) = join(((0, 1),), row, other)
    swap = turn(cores, 1)

    delta, theirs, mine, near_txt, col_note = delta_and_text(
        (row, other), col, t, s, student_txt, student_img, chips
    )
    theirs = lax.ppermute(theirs, "img_1", swap)
    to_img = image_gradient(delta, near_txt, col_note, txt_count)
    got_img = lax.all_to_all(to_img, TXT, 0, 0, tiled=True)
    two, three, one, four, own = added(mine, theirs, chips)

    def outward(value, step):
        pairs = [
            (cores * z + c, cores * ((z + step * (1 - 2 * c)) % chips) + c)
            for z in range(chips) for c in range(cores)
        ]
        return lax.ppermute(value, IMG, pairs)

    four = outward(four, 2)
    flow = relayed(two, outward(three, 1), four)
    flow = relayed(one, outward(flow, 1))
    flow = outward(flow, 1)
    across = lax.ppermute(flow, "img_1", swap)
    grad_txt, row_total = finished(flow, across, own)
    grad_img, loss = summed(
        1.0 / (rows * img_count), 1.0 / (cols * txt_count), got_img, row_total, thin
    )
    return (loss.reshape(()), grad_img, grad_txt)


def solution(mesh):
    torus = Mesh(mesh.devices.reshape(8, 2, 4, 4), ("img_0", "img_1", "txt_0", "txt_1"))
    in_specs = (P(IMG, None), P(TXT, None), P(IMG, None), P(TXT, None))
    out_specs = (P(), P(IMG_TXT, None), P(TXT_IMG, None))
    return jax.shard_map(body, mesh=torus, in_specs=in_specs, out_specs=out_specs, check_vma=False)
```

```python
import functools
import math

import jax
import jax.numpy as jnp
from jax import lax
from jax.experimental import pallas as pl
from jax.experimental.pallas import tpu as pltpu
from jax.sharding import Mesh
from jax.sharding import PartitionSpec as P

IMG = ("img_0", "img_1")
TXT = ("txt_0", "txt_1")
IMG_TXT = ("img_0", "img_1", "txt_0", "txt_1")
TXT_IMG = ("txt_0", "txt_1", "img_0", "img_1")
LANES = 128
NOTE = 8
VMEM_LIMIT = 32 * 1024 * 1024
STATS_LIMIT = 32 * 1024 * 1024
LN2 = math.log(2.0)
F32 = jnp.float32
MIB = 1024 * 1024
WHOLE = pl.BlockSpec(memory_space=pltpu.VMEM)
FAR = pl.BlockSpec(memory_space=pltpu.HBM)


def cost(flops, size, transcendentals=0):
    return pl.CostEstimate(flops=flops, bytes_accessed=size, transcendentals=transcendentals)


def stats_kernel(scale_teach, scale_learn, ti_hbm, tt_hbm, si_hbm, st_hbm, t_hbm, s_hbm,
                 row_out, col_out, ti, tt, si, st, t, s, peaks, sums, col_peaks, col_sums, sems):
    rows, cols = t.shape
    tall = 256
    chunks = rows // tall

    def load(src, dst, at, size, which):
        copy = pltpu.make_async_copy(
            src.at[pl.ds(at, size), :], dst.at[pl.ds(at, size), :], sems.at[which]
        )
        copy.start()
        return copy

    st_load = load(st_hbm, st, 0, cols, 1 + chunks)
    si_load = load(si_hbm, si, 0, rows, 2 + chunks)
    tt_load = load(tt_hbm, tt, 0, cols, 0)

    saves = []

    def logits(left, right, out, far, scale, which, arrivals):
        for n in range(chunks):
            if arrivals:
                arrivals[n].wait()
            down = slice(n * tall, (n + 1) * tall)
            block = scale * lax.dot_general(
                left[down, :], right[...], (((1,), (1,)), ((), ())), preferred_element_type=F32
            )
            out[down, :] = block
            saves.append(load(out, far, n * tall, tall, sems.shape[0] - 1 - len(saves)))
            top = jnp.max(block.reshape(tall // 8, 8, cols), axis=0)
            col_peaks[which] = jnp.maximum(col_peaks[which], top) if n else top
            side = block[:, :LANES]
            for k in range(1, cols // LANES):
                side = jnp.maximum(side, block[:, k * LANES : (k + 1) * LANES])
            peaks[which, down, :] = jnp.broadcast_to(
                jnp.max(side, axis=1, keepdims=True), (tall, LANES)
            )
        col_peaks[which] = jnp.broadcast_to(
            jnp.max(col_peaks[which], axis=0, keepdims=True), (8, cols)
        )

    st_load.wait()
    si_load.wait()
    ti_loads = [load(ti_hbm, ti, n * tall, tall, 1 + n) for n in range(chunks)]
    logits(si, st, s, s_hbm, scale_learn, 1, None)
    tt_load.wait()
    logits(ti, tt, t, t_hbm, scale_teach, 0, ti_loads)

    group = 4 * LANES
    for h in range(cols // group):
        def strip(r, carry):
            at = pl.multiple_of(r * 8, 8)
            down = pl.ds(at, 8)
            row_peak_t, row_peak_s = peaks[0, down, :], peaks[1, down, :]
            row_t = row_s = row_g = None
            new = []
            for k in range(group // LANES):
                across = slice(h * group + k * LANES, h * group + (k + 1) * LANES)
                tv, sv = t[down, across], s[down, across]
                gap = tv - sv
                wr = jnp.exp2(tv - row_peak_t)
                vr = jnp.exp2(sv - row_peak_s)
                wc = jnp.exp2(tv - col_peaks[0, :, across])
                vc = jnp.exp2(sv - col_peaks[1, :, across])
                row_t = wr if row_t is None else row_t + wr
                row_s = vr if row_s is None else row_s + vr
                row_g = wr * gap if row_g is None else row_g + wr * gap
                ct, cs, cg = carry[3 * k : 3 * k + 3]
                new += [ct + wc, cs + vc, cg + wc * gap]
            for q, value in enumerate((row_t, row_s, row_g)):
                sums[q, down, :] = value + sums[q, down, :] if h else value
            return tuple(new)

        zeros = tuple(jnp.zeros((8, LANES), F32) for _ in range(3 * group // LANES))
        found = lax.fori_loop(0, rows // 8, strip, zeros, unroll=8)
        for k in range(group // LANES):
            across = slice(h * group + k * LANES, h * group + (k + 1) * LANES)
            for q in range(3):
                col_sums[q, :, across] = found[3 * k + q]

    def publish(out, peak_t, peak_s, mass_t, mass_s, gap):
        found = (peak_t + jnp.log2(mass_t), peak_s + jnp.log2(mass_s), gap / mass_t)
        for q, value in enumerate(found):
            for k in range(out.shape[0]):
                out[k, 8 * q : 8 * q + 8, :] = value

    def stacked(lines):
        return jnp.concatenate(lines, axis=0)

    def by_column(value):
        return stacked([value[:, b * LANES : (b + 1) * LANES] for b in range(cols // LANES)])

    publish(
        col_out, by_column(col_peaks[0, :1, :]), by_column(col_peaks[1, :1, :]),
        *(by_column(jnp.sum(col_sums[q], axis=0, keepdims=True)) for q in range(3)),
    )
    lane = lax.broadcasted_iota(jnp.int32, (rows, LANES), 1)
    packed = jnp.where(lane == 0, peaks[0], peaks[1])
    for q in range(3):
        packed = jnp.where(lane == 2 + q, jnp.sum(sums[q], axis=1, keepdims=True), packed)
    turned = [packed[b * LANES : (b + 1) * LANES, :].T for b in range(rows // LANES)]
    publish(row_out, *(stacked([block[q : q + 1, :] for block in turned]) for q in range(5)))
    for save in saves:
        save.wait()


def local_stats(teacher_img, teacher_txt, student_img, student_txt, copies):
    rows, deep = teacher_img.shape
    cols, thin = student_txt.shape
    kernel = functools.partial(
        stats_kernel, 3.0 / math.sqrt(deep) / LN2, 3.0 / math.sqrt(thin) / LN2
    )
    return pl.pallas_call(
        kernel,
        name="logits_and_statistics",
        out_shape=(
            pltpu.HBM((rows, cols), F32), pltpu.HBM((rows, cols), F32),
            jax.ShapeDtypeStruct((1, 3 * rows // LANES, LANES), F32),
            jax.ShapeDtypeStruct((copies, 3 * cols // LANES, LANES), F32),
        ),
        in_specs=[FAR] * 4,
        out_specs=(FAR, FAR, WHOLE, WHOLE),
        scratch_shapes=[
            pltpu.VMEM((rows, deep), jnp.bfloat16), pltpu.VMEM((cols, deep), jnp.bfloat16),
            pltpu.VMEM((rows, thin), jnp.bfloat16), pltpu.VMEM((cols, thin), jnp.bfloat16),
            pltpu.VMEM((rows, cols), F32), pltpu.VMEM((rows, cols), F32),
            pltpu.VMEM((2, rows, LANES), F32), pltpu.VMEM((3, rows, LANES), F32),
            pltpu.VMEM((2, 8, cols), F32), pltpu.VMEM((3, 8, cols), F32),
            pltpu.SemaphoreType.DMA((16,)),
        ],
        compiler_params=pltpu.CompilerParams(vmem_limit_bytes=STATS_LIMIT),
        cost_estimate=cost(2 * rows * cols * (deep + thin), 8 * rows * cols, 4 * rows * cols),
    )(*(
        pltpu.with_memory_space_constraint(x, pltpu.HBM)
        for x in (teacher_img, teacher_txt, student_img, student_txt)
    ))


def joined(parts):
    teach, learn, gap = ([part[8 * q : 8 * q + 8, :] for part in parts] for q in range(3))
    teach_peak = functools.reduce(jnp.maximum, teach)
    learn_peak = functools.reduce(jnp.maximum, learn)
    weights = [jnp.exp2(part - teach_peak) for part in teach]
    mass = sum(weights[1:], weights[0])
    shares = [jnp.exp2(part - learn_peak) for part in learn]
    gaps = [weight * part for weight, part in zip(weights, gap)]
    return (
        teach_peak + jnp.log2(mass),
        learn_peak + jnp.log2(sum(shares[1:], shares[0])),
        sum(gaps[1:], gaps[0]) / mass,
    )


def join_kernel(groups, *refs):
    sources, outs = refs[: len(refs) - len(groups)], refs[len(refs) - len(groups) :]
    for group, out in zip(groups, outs):
        for q, value in enumerate(joined([sources[k][...] for k in group])):
            for k in range(out.shape[0]):
                out[k, 8 * q : 8 * q + 8, :] = value


def join(groups, copies, *parts):
    return pl.pallas_call(
        functools.partial(join_kernel, groups),
        name="joined_statistics",
        out_shape=[
            jax.ShapeDtypeStruct((count, *parts[group[0]].shape), F32)
            for group, count in zip(groups, copies)
        ],
        in_specs=[WHOLE] * len(parts),
        out_specs=[WHOLE] * len(groups),
        compiler_params=pltpu.CompilerParams(vmem_limit_bytes=1 * MIB),
        cost_estimate=cost(parts[0].size * 20, parts[0].size * 4 * len(parts), parts[0].size * 4),
    )(*parts)


def delta_kernel(scale, *refs):
    row_parts = refs[:2]
    col_stats, t_far, s_far, st_far, si_far, img_out, theirs_out, mine = refs[2:10]
    row_norms, col_norms, t, s, st, si, delta, img_block, theirs, grads, sems = refs[10:]
    tall = 256
    arrivals = []
    for n in range(t.shape[0] // tall):
        down = pl.ds(n * tall, tall)
        arrivals.append([
            pltpu.make_async_copy(far.at[down, :], near.at[down, :], sems.at[2 + 2 * n + k])
            for k, (far, near) in enumerate(((t_far, t), (s_far, s)))
        ])
        for copy in arrivals[-1]:
            copy.start()
    loads = [
        pltpu.make_async_copy(src, dst, sems.at[k])
        for k, (src, dst) in enumerate(((st_far, st), (si_far, si)))
    ]
    for load in loads:
        load.start()
    rows, cols = t.shape
    thin = st.shape[1]
    row_teach, row_learn, row_mean = joined([part[...] for part in row_parts])
    col_teach, col_learn, col_mean = joined(
        [col_stats[k] for k in range(col_stats.shape[0])]
    )
    row_total = jnp.sum(row_mean + row_learn - row_teach)
    col_total = jnp.sum(col_mean + col_learn - col_teach)
    for which, (down, across) in enumerate(((row_teach, col_teach), (row_learn, col_learn))):
        turned = jnp.concatenate([down - 3.0] * (LANES // 8), axis=0).T
        for b in range(8):
            row_norms[which, b * LANES : (b + 1) * LANES, :] = jnp.broadcast_to(
                turned[:, b : b + 1], (LANES, LANES)
            )
            col_norms[which, :, b * LANES : (b + 1) * LANES] = jnp.broadcast_to(
                across[b : b + 1, :] - 3.0, (16, LANES)
            )

    def strip(r, carry):
        down = pl.ds(pl.multiple_of(r * 16, 16), 16)
        row_t, row_s = row_norms[0, down, :], row_norms[1, down, :]
        for k in range(cols // LANES):
            across = slice(k * LANES, (k + 1) * LANES)
            tv, sv = t[down, across], s[down, across]
            value = (
                jnp.exp2(sv - row_s) - jnp.exp2(tv - row_t)
                + jnp.exp2(sv - col_norms[1, :, across]) - jnp.exp2(tv - col_norms[0, :, across])
            )
            delta[down, across] = value.astype(jnp.bfloat16)
        return carry

    for n, copies in enumerate(arrivals):
        for copy in copies:
            copy.wait()
        lax.fori_loop(n * tall // 16, (n + 1) * tall // 16, strip, 0, unroll=2)
    for load in loads:
        load.wait()

    pieces, lines, _ = img_block.shape
    own = rows // pieces
    some = 4
    for k in range(pieces):
        img_block[k, lines - NOTE :, :] = jnp.full((NOTE, LANES), col_total, F32)
    saves = []
    for n in range(pieces // some):
        grad = scale * jnp.dot(
            delta[n * some * own : (n + 1) * some * own, :], st[...], preferred_element_type=F32
        )
        for k in range(some):
            for b in range(thin // LANES):
                img_block[n * some + k, b * own : (b + 1) * own, :] = grad[
                    k * own : (k + 1) * own, b * LANES : (b + 1) * LANES
                ]
        save = pltpu.make_async_copy(
            img_block.at[pl.ds(n * some, some)], img_out.at[pl.ds(n * some, some)], sems.at[10 + n]
        )
        save.start()
        saves.append(save)

    place, core = lax.axis_index("img_0"), lax.axis_index("img_1")
    chips = lax.axis_size("img_0")
    tall = cols // chips
    half = tall // 2
    full_note = jnp.full((NOTE, thin), row_total, F32)

    wide = 256
    for n in range(cols // wide):
        grads[n * wide : (n + 1) * wide, :] = scale * lax.dot_general(
            delta[:, n * wide : (n + 1) * wide], si[...], (((0,), (0,)), ((), ())),
            preferred_element_type=F32,
        )

    def text_block(out, top, far, part, note):
        size = tall if part is None else half
        at = lax.rem(place + far + chips, chips) * tall
        if part is not None:
            at = at + part * half
        out[top : top + size, :] = grads[pl.ds(pl.multiple_of(at, half), size), :]
        out[top + size : top + size + NOTE, :] = note

    for out, flow in ((theirs, 1 - core), (mine, core)):
        sign = 1 - 2 * flow
        top = 0
        for far, part, note in (
            (2 * sign, None, full_note), (3 * sign, None, full_note), (sign, None, full_note),
            (chips // 2, flow, 0.5 * full_note), (0, flow, full_note),
        ):
            text_block(out, top, far, part, note)
            top += (tall if part is None else half) + NOTE
        if out is theirs:
            save = pltpu.make_async_copy(theirs, theirs_out, sems.at[10 + len(saves)])
            save.start()
            saves.append(save)

    for save in saves:
        save.wait()


def flow_rows(tall):
    full, part = tall + NOTE, tall // 2 + NOTE
    return (full, full, full, part, part)


def gradients(row_parts, col_stats, t, s, student_txt, student_img, pieces, chips):
    rows, cols = t.shape
    thin = student_txt.shape[1]
    shape = (pieces, rows // pieces * thin // LANES + NOTE, LANES)
    flow = (sum(flow_rows(cols // chips)), thin)
    return pl.pallas_call(
        functools.partial(delta_kernel, 3.0 / math.sqrt(thin)),
        name="delta_and_gradients",
        out_shape=(pltpu.HBM(shape, F32), pltpu.HBM(flow, F32), jax.ShapeDtypeStruct(flow, F32)),
        in_specs=[WHOLE] * (len(row_parts) + 1) + [FAR] * 4,
        out_specs=(FAR, FAR, WHOLE),
        scratch_shapes=[
            pltpu.VMEM((2, rows, LANES), F32), pltpu.VMEM((2, 16, cols), F32),
            pltpu.VMEM((rows, cols), F32), pltpu.VMEM((rows, cols), F32),
            pltpu.VMEM(student_txt.shape, jnp.bfloat16),
            pltpu.VMEM(student_img.shape, jnp.bfloat16),
            pltpu.VMEM((rows, cols), jnp.bfloat16), pltpu.VMEM(shape, F32),
            pltpu.VMEM(flow, F32), pltpu.VMEM((cols, thin), F32),
            pltpu.SemaphoreType.DMA((11 + pieces // 4,)),
        ],
        compiler_params=pltpu.CompilerParams(vmem_limit_bytes=VMEM_LIMIT),
        cost_estimate=cost(4 * rows * cols * thin, 8 * rows * cols, 4 * rows * cols),
    )(
        *row_parts, col_stats,
        *(
            pltpu.with_memory_space_constraint(x, pltpu.HBM)
            for x in (t, s, student_txt, student_img)
        ),
    )


def add_kernel(mine, theirs, *outs):
    top = 0
    for out in outs:
        down = slice(top, top + out.shape[0])
        out[...] = mine[down, :] + theirs[down, :]
        top += out.shape[0]


def added(mine, theirs, chips):
    thin = mine.shape[1]
    sizes = flow_rows(2 * (mine.shape[0] - 5 * NOTE) // chips)
    return pl.pallas_call(
        add_kernel,
        name="both_cores_text_terms",
        out_shape=[jax.ShapeDtypeStruct((size, thin), F32) for size in sizes],
        in_specs=[WHOLE] * 2,
        out_specs=[WHOLE] * len(sizes),
        compiler_params=pltpu.CompilerParams(vmem_limit_bytes=8 * MIB),
        cost_estimate=cost(mine.size, 12 * mine.size),
    )(mine, theirs)


def relay_kernel(near, full, *refs):
    out = refs[-1]
    out[...] = near[...] + full[...]
    if len(refs) > 1:
        part = refs[0]
        size = out.shape[0] - NOTE
        half = size // 2
        down = pl.ds(pl.multiple_of(lax.axis_index("img_1") * half, half), half)
        out[down, :] = out[down, :] + part[:half, :]
        out[size:, :] = out[size:, :] + part[half:, :]


def relayed(*parts):
    return pl.pallas_call(
        relay_kernel,
        name="relayed_text_terms",
        out_shape=jax.ShapeDtypeStruct(parts[0].shape, F32),
        in_specs=[WHOLE] * len(parts),
        out_specs=WHOLE,
        compiler_params=pltpu.CompilerParams(vmem_limit_bytes=4 * MIB),
        cost_estimate=cost(parts[0].size * 3, 12 * parts[0].size),
    )(*parts)


def finish_kernel(flow, other, own, out, note):
    half = out.shape[0]
    down = pl.ds(pl.multiple_of(lax.axis_index("img_1") * half, half), half)
    out[...] = flow[down, :] + other[down, :] + own[:half, :]
    note[...] = flow[2 * half :, :LANES] + other[2 * half :, :LANES] + own[half:, :LANES]


def finished(flow, other, own):
    thin = flow.shape[1]
    return pl.pallas_call(
        finish_kernel,
        name="text_gradient_total",
        out_shape=(
            jax.ShapeDtypeStruct((own.shape[0] - NOTE, thin), F32),
            jax.ShapeDtypeStruct((NOTE, LANES), F32),
        ),
        in_specs=[WHOLE] * 3,
        out_specs=(WHOLE, WHOLE),
        compiler_params=pltpu.CompilerParams(vmem_limit_bytes=4 * MIB),
        cost_estimate=cost(own.size * 3, 16 * own.size),
    )(flow, other, own)


def sum_kernel(row_share, col_share, parts, row_note, out, loss):
    own = out.shape[0]

    def total(down):
        return functools.reduce(jnp.add, [parts[k, down, :] for k in range(parts.shape[0])])

    for b in range(out.shape[1] // LANES):
        out[:, b * LANES : (b + 1) * LANES] = total(slice(b * own, (b + 1) * own))
    col_note = total(slice(parts.shape[1] - NOTE, parts.shape[1]))
    both = (0.5 * LN2) * (row_note[...] * row_share + col_note * col_share)
    loss[0, 0] = both[0, 0]


def summed(row_share, col_share, parts, row_note, thin):
    own = (parts.shape[1] - NOTE) * LANES // thin
    return pl.pallas_call(
        functools.partial(sum_kernel, row_share, col_share),
        name="sum_of_image_parts_and_loss",
        out_shape=(jax.ShapeDtypeStruct((own, thin), F32), jax.ShapeDtypeStruct((1, 1), F32)),
        in_specs=[WHOLE] * 2,
        out_specs=(WHOLE, pl.BlockSpec(memory_space=pltpu.SMEM)),
        compiler_params=pltpu.CompilerParams(vmem_limit_bytes=4 * MIB),
        cost_estimate=cost(parts.size, 4 * parts.size),
    )(parts, row_note)


def turn(size, step):
    return [(k, (k + step) % size) for k in range(size)]


def body(teacher_img, teacher_txt, student_img, student_txt):
    rows = student_img.shape[0]
    cols, thin = student_txt.shape
    chips, cores = lax.axis_size("img_0"), lax.axis_size("img_1")
    img_count, txt_count = chips * cores, lax.axis_size(TXT)
    side = lax.axis_size("txt_0")

    t, s, row, col = local_stats(
        teacher_img, teacher_txt, student_img, student_txt, 1
    )
    swap = turn(cores, 1)

    def neighbour(value, axis, first):
        pairs = [(k, (k + 1 - 2 * ((k + first) % 2)) % side) for k in range(side)]
        return lax.ppermute(value, axis, pairs)

    row, col = row[0], col[0]
    other = neighbour(row, TXT[0], 0)
    row, col = join(
        ((0, 1), (2, 3)), (1, chips), row, other, col, lax.ppermute(col, "img_1", swap)
    )
    col = lax.all_to_all(col, "img_0", 0, 0, tiled=True)
    for axis, first in ((TXT[0], 1), (TXT[1], 0)):
        row = row[0]
        (row,) = join(((0, 1),), (1,), row, neighbour(row, axis, first))
    row = row[0]
    other = neighbour(row, TXT[1], 1)

    to_img, theirs, mine = gradients(
        (row, other), col, t, s, student_txt, student_img, txt_count, chips
    )
    got_img = lax.all_to_all(to_img, TXT, 0, 0, tiled=True)
    theirs = lax.ppermute(theirs, "img_1", swap)
    two, three, one, four, own = added(mine, theirs, chips)

    def outward(value, step):
        pairs = [
            (cores * z + c, cores * ((z + step * (1 - 2 * c)) % chips) + c)
            for z in range(chips) for c in range(cores)
        ]
        return lax.ppermute(value, IMG, pairs)

    four = outward(four, 2)
    flow = relayed(two, outward(three, 1), four)
    flow = relayed(one, outward(flow, 1))
    flow = outward(flow, 1)
    across = lax.ppermute(flow, "img_1", swap)
    grad_txt, row_total = finished(flow, across, own)
    grad_img, loss = summed(
        1.0 / (rows * img_count), 1.0 / (cols * txt_count), got_img, row_total, thin
    )
    return (loss.reshape(()), grad_img, grad_txt)


def solution(mesh):
    torus = Mesh(mesh.devices.reshape(8, 2, 4, 4), ("img_0", "img_1", "txt_0", "txt_1"))
    in_specs = (P(IMG, None), P(TXT, None), P(IMG, None), P(TXT, None))
    out_specs = (P(), P(IMG_TXT, None), P(TXT_IMG, None))
    return jax.shard_map(body, mesh=torus, in_specs=in_specs, out_specs=out_specs, check_vma=False)
```

```python
import functools
import math

import jax
import jax.numpy as jnp
from jax import lax
from jax.experimental import pallas as pl
from jax.experimental.pallas import tpu as pltpu
from jax.sharding import Mesh
from jax.sharding import PartitionSpec as P

IMG = ("img_0", "img_1")
TXT = ("txt_0", "txt_1")
IMG_TXT = ("img_0", "img_1", "txt_0", "txt_1")
TXT_IMG = ("txt_0", "txt_1", "img_0", "img_1")
LANES = 128
NOTE = 8
VMEM_LIMIT = 32 * 1024 * 1024
STATS_LIMIT = 32 * 1024 * 1024
LN2 = math.log(2.0)
F32 = jnp.float32
MIB = 1024 * 1024
WHOLE = pl.BlockSpec(memory_space=pltpu.VMEM)
FAR = pl.BlockSpec(memory_space=pltpu.HBM)


def cost(flops, size, transcendentals=0):
    return pl.CostEstimate(flops=flops, bytes_accessed=size, transcendentals=transcendentals)


def stats_kernel(scale_teach, scale_learn, ti_hbm, tt_hbm, si_hbm, st_hbm, t_hbm, s_hbm,
                 row_out, col_out, ti, tt, si, st, t, s, peaks, sums, col_peaks, col_sums, sems):
    rows, cols = t.shape
    tall = 256
    chunks = rows // tall

    def load(src, dst, at, size, which):
        copy = pltpu.make_async_copy(
            src.at[pl.ds(at, size), :], dst.at[pl.ds(at, size), :], sems.at[which]
        )
        copy.start()
        return copy

    st_load = load(st_hbm, st, 0, cols, 1 + chunks)
    si_load = load(si_hbm, si, 0, rows, 2 + chunks)
    tt_load = load(tt_hbm, tt, 0, cols, 0)

    saves = []

    def logits(left, right, out, far, scale, which, arrivals):
        for n in range(chunks):
            if arrivals:
                arrivals[n].wait()
            down = slice(n * tall, (n + 1) * tall)
            block = scale * lax.dot_general(
                left[down, :], right[...], (((1,), (1,)), ((), ())), preferred_element_type=F32
            )
            out[down, :] = block
            saves.append(load(out, far, n * tall, tall, sems.shape[0] - 1 - len(saves)))
            top = jnp.max(block.reshape(tall // 8, 8, cols), axis=0)
            col_peaks[which] = jnp.maximum(col_peaks[which], top) if n else top
            side = block[:, :LANES]
            for k in range(1, cols // LANES):
                side = jnp.maximum(side, block[:, k * LANES : (k + 1) * LANES])
            peaks[which, down, :] = jnp.broadcast_to(
                jnp.max(side, axis=1, keepdims=True), (tall, LANES)
            )
        col_peaks[which] = jnp.broadcast_to(
            jnp.max(col_peaks[which], axis=0, keepdims=True), (8, cols)
        )

    st_load.wait()
    si_load.wait()
    ti_loads = [load(ti_hbm, ti, n * tall, tall, 1 + n) for n in range(chunks)]
    logits(si, st, s, s_hbm, scale_learn, 1, None)
    tt_load.wait()
    logits(ti, tt, t, t_hbm, scale_teach, 0, ti_loads)

    group = 4 * LANES
    for h in range(cols // group):
        def strip(r, carry):
            at = pl.multiple_of(r * 8, 8)
            down = pl.ds(at, 8)
            row_peak_t, row_peak_s = peaks[0, down, :], peaks[1, down, :]
            row_t = row_s = row_g = None
            new = []
            for k in range(group // LANES):
                across = slice(h * group + k * LANES, h * group + (k + 1) * LANES)
                tv, sv = t[down, across], s[down, across]
                gap = tv - sv
                wr = jnp.exp2(tv - row_peak_t)
                vr = jnp.exp2(sv - row_peak_s)
                wc = jnp.exp2(tv - col_peaks[0, :, across])
                vc = jnp.exp2(sv - col_peaks[1, :, across])
                row_t = wr if row_t is None else row_t + wr
                row_s = vr if row_s is None else row_s + vr
                row_g = wr * gap if row_g is None else row_g + wr * gap
                ct, cs, cg = carry[3 * k : 3 * k + 3]
                new += [ct + wc, cs + vc, cg + wc * gap]
            for q, value in enumerate((row_t, row_s, row_g)):
                sums[q, down, :] = value + sums[q, down, :] if h else value
            return tuple(new)

        zeros = tuple(jnp.zeros((8, LANES), F32) for _ in range(3 * group // LANES))
        found = lax.fori_loop(0, rows // 8, strip, zeros, unroll=8)
        for k in range(group // LANES):
            across = slice(h * group + k * LANES, h * group + (k + 1) * LANES)
            for q in range(3):
                col_sums[q, :, across] = found[3 * k + q]

    def publish(out, peak_t, peak_s, mass_t, mass_s, gap):
        found = (peak_t + jnp.log2(mass_t), peak_s + jnp.log2(mass_s), gap / mass_t)
        for q, value in enumerate(found):
            for k in range(out.shape[0]):
                out[k, 8 * q : 8 * q + 8, :] = value

    def stacked(lines):
        return jnp.concatenate(lines, axis=0)

    def by_column(value):
        return stacked([value[:, b * LANES : (b + 1) * LANES] for b in range(cols // LANES)])

    publish(
        col_out, by_column(col_peaks[0, :1, :]), by_column(col_peaks[1, :1, :]),
        *(by_column(jnp.sum(col_sums[q], axis=0, keepdims=True)) for q in range(3)),
    )
    lane = lax.broadcasted_iota(jnp.int32, (rows, LANES), 1)
    packed = jnp.where(lane == 0, peaks[0], peaks[1])
    for q in range(3):
        packed = jnp.where(lane == 2 + q, jnp.sum(sums[q], axis=1, keepdims=True), packed)
    turned = [packed[b * LANES : (b + 1) * LANES, :].T for b in range(rows // LANES)]
    publish(row_out, *(stacked([block[q : q + 1, :] for block in turned]) for q in range(5)))
    for save in saves:
        save.wait()


def local_stats(teacher_img, teacher_txt, student_img, student_txt, copies):
    rows, deep = teacher_img.shape
    cols, thin = student_txt.shape
    kernel = functools.partial(
        stats_kernel, 3.0 / math.sqrt(deep) / LN2, 3.0 / math.sqrt(thin) / LN2
    )
    return pl.pallas_call(
        kernel,
        name="logits_and_statistics",
        out_shape=(
            pltpu.HBM((rows, cols), F32), pltpu.HBM((rows, cols), F32),
            jax.ShapeDtypeStruct((1, 3 * rows // LANES, LANES), F32),
            jax.ShapeDtypeStruct((copies, 3 * cols // LANES, LANES), F32),
        ),
        in_specs=[FAR] * 4,
        out_specs=(FAR, FAR, WHOLE, WHOLE),
        scratch_shapes=[
            pltpu.VMEM((rows, deep), jnp.bfloat16), pltpu.VMEM((cols, deep), jnp.bfloat16),
            pltpu.VMEM((rows, thin), jnp.bfloat16), pltpu.VMEM((cols, thin), jnp.bfloat16),
            pltpu.VMEM((rows, cols), F32), pltpu.VMEM((rows, cols), F32),
            pltpu.VMEM((2, rows, LANES), F32), pltpu.VMEM((3, rows, LANES), F32),
            pltpu.VMEM((2, 8, cols), F32), pltpu.VMEM((3, 8, cols), F32),
            pltpu.SemaphoreType.DMA((16,)),
        ],
        compiler_params=pltpu.CompilerParams(vmem_limit_bytes=STATS_LIMIT),
        cost_estimate=cost(2 * rows * cols * (deep + thin), 8 * rows * cols, 4 * rows * cols),
    )(*(
        pltpu.with_memory_space_constraint(x, pltpu.HBM)
        for x in (teacher_img, teacher_txt, student_img, student_txt)
    ))


def joined(parts):
    teach, learn, gap = ([part[8 * q : 8 * q + 8, :] for part in parts] for q in range(3))
    teach_peak = functools.reduce(jnp.maximum, teach)
    learn_peak = functools.reduce(jnp.maximum, learn)
    weights = [jnp.exp2(part - teach_peak) for part in teach]
    mass = sum(weights[1:], weights[0])
    shares = [jnp.exp2(part - learn_peak) for part in learn]
    gaps = [weight * part for weight, part in zip(weights, gap)]
    return (
        teach_peak + jnp.log2(mass),
        learn_peak + jnp.log2(sum(shares[1:], shares[0])),
        sum(gaps[1:], gaps[0]) / mass,
    )


def join_kernel(groups, *refs):
    sources, outs = refs[: len(refs) - len(groups)], refs[len(refs) - len(groups) :]
    for group, out in zip(groups, outs):
        for q, value in enumerate(joined([sources[k][...] for k in group])):
            for k in range(out.shape[0]):
                out[k, 8 * q : 8 * q + 8, :] = value


def join(groups, copies, *parts):
    return pl.pallas_call(
        functools.partial(join_kernel, groups),
        name="joined_statistics",
        out_shape=[
            jax.ShapeDtypeStruct((count, *parts[group[0]].shape), F32)
            for group, count in zip(groups, copies)
        ],
        in_specs=[WHOLE] * len(parts),
        out_specs=[WHOLE] * len(groups),
        compiler_params=pltpu.CompilerParams(vmem_limit_bytes=1 * MIB),
        cost_estimate=cost(parts[0].size * 20, parts[0].size * 4 * len(parts), parts[0].size * 4),
    )(*parts)


def delta_kernel(scale, *refs):
    row_parts = refs[:2]
    col_stats, t_far, s_far, st_far, si_far, img_out, theirs_out, mine = refs[2:10]
    row_norms, col_norms, t, s, st, si, delta, img_block, theirs, grads, sems = refs[10:]
    loads = [
        pltpu.make_async_copy(src, dst, sems.at[k])
        for k, (src, dst) in enumerate(((st_far, st), (si_far, si)))
    ]
    tall = 256
    arrivals = []
    for n in range(t.shape[0] // tall):
        down = pl.ds(n * tall, tall)
        arrivals.append([
            pltpu.make_async_copy(far.at[down, :], near.at[down, :], sems.at[2 + 2 * n + k])
            for k, (far, near) in enumerate(((t_far, t), (s_far, s)))
        ])
        for copy in arrivals[-1]:
            copy.start()
        if n == 0:
            loads[0].start()
    loads[1].start()
    rows, cols = t.shape
    thin = st.shape[1]
    row_teach, row_learn, row_mean = joined([part[...] for part in row_parts])
    col_teach, col_learn, col_mean = joined(
        [col_stats[k] for k in range(col_stats.shape[0])]
    )
    row_total = jnp.sum(row_mean + row_learn - row_teach)
    col_total = jnp.sum(col_mean + col_learn - col_teach)
    for which, (down, across) in enumerate(((row_teach, col_teach), (row_learn, col_learn))):
        turned = jnp.concatenate([down - 3.0] * (LANES // 8), axis=0).T
        for b in range(8):
            row_norms[which, b * LANES : (b + 1) * LANES, :] = jnp.broadcast_to(
                turned[:, b : b + 1], (LANES, LANES)
            )
            col_norms[which, :, b * LANES : (b + 1) * LANES] = jnp.broadcast_to(
                across[b : b + 1, :] - 3.0, (16, LANES)
            )

    def strip(r, carry):
        down = pl.ds(pl.multiple_of(r * 16, 16), 16)
        row_t, row_s = row_norms[0, down, :], row_norms[1, down, :]
        for k in range(cols // LANES):
            across = slice(k * LANES, (k + 1) * LANES)
            tv, sv = t[down, across], s[down, across]
            value = (
                jnp.exp2(sv - row_s) - jnp.exp2(tv - row_t)
                + jnp.exp2(sv - col_norms[1, :, across]) - jnp.exp2(tv - col_norms[0, :, across])
            )
            delta[down, across] = value.astype(jnp.bfloat16)
        return carry

    pieces, lines, _ = img_block.shape
    own = rows // pieces
    some = tall // own
    for k in range(pieces):
        img_block[k, lines - NOTE :, :] = jnp.full((NOTE, LANES), col_total, F32)
    saves = []
    for n, copies in enumerate(arrivals):
        for copy in copies:
            copy.wait()
        lax.fori_loop(n * tall // 16, (n + 1) * tall // 16, strip, 0, unroll=2)
        if n == 0:
            loads[0].wait()
        grad = scale * jnp.dot(
            delta[n * tall : (n + 1) * tall, :], st[...], preferred_element_type=F32
        )
        for k in range(some):
            for b in range(thin // LANES):
                img_block[n * some + k, b * own : (b + 1) * own, :] = grad[
                    k * own : (k + 1) * own, b * LANES : (b + 1) * LANES
                ]
        save = pltpu.make_async_copy(
            img_block.at[pl.ds(n * some, some)], img_out.at[pl.ds(n * some, some)], sems.at[10 + n]
        )
        save.start()
        saves.append(save)
    loads[1].wait()

    place, core = lax.axis_index("img_0"), lax.axis_index("img_1")
    chips = lax.axis_size("img_0")
    tall = cols // chips
    half = tall // 2
    full_note = jnp.full((NOTE, thin), row_total, F32)

    wide = 256
    for n in range(cols // wide):
        grads[n * wide : (n + 1) * wide, :] = scale * lax.dot_general(
            delta[:, n * wide : (n + 1) * wide], si[...], (((0,), (0,)), ((), ())),
            preferred_element_type=F32,
        )

    def text_block(out, top, far, part, note):
        size = tall if part is None else half
        at = lax.rem(place + far + chips, chips) * tall
        if part is not None:
            at = at + part * half
        out[top : top + size, :] = grads[pl.ds(pl.multiple_of(at, half), size), :]
        out[top + size : top + size + NOTE, :] = note

    for out, flow in ((theirs, 1 - core), (mine, core)):
        sign = 1 - 2 * flow
        top = 0
        for far, part, note in (
            (2 * sign, None, full_note), (3 * sign, None, full_note), (sign, None, full_note),
            (chips // 2, flow, 0.5 * full_note), (0, flow, full_note),
        ):
            text_block(out, top, far, part, note)
            top += (tall if part is None else half) + NOTE
        if out is theirs:
            save = pltpu.make_async_copy(theirs, theirs_out, sems.at[10 + len(saves)])
            save.start()
            saves.append(save)

    for save in saves:
        save.wait()


def flow_rows(tall):
    full, part = tall + NOTE, tall // 2 + NOTE
    return (full, full, full, part, part)


def gradients(row_parts, col_stats, t, s, student_txt, student_img, pieces, chips):
    rows, cols = t.shape
    thin = student_txt.shape[1]
    shape = (pieces, rows // pieces * thin // LANES + NOTE, LANES)
    flow = (sum(flow_rows(cols // chips)), thin)
    return pl.pallas_call(
        functools.partial(delta_kernel, 3.0 / math.sqrt(thin)),
        name="delta_and_gradients",
        out_shape=(pltpu.HBM(shape, F32), pltpu.HBM(flow, F32), jax.ShapeDtypeStruct(flow, F32)),
        in_specs=[WHOLE] * (len(row_parts) + 1) + [FAR] * 4,
        out_specs=(FAR, FAR, WHOLE),
        scratch_shapes=[
            pltpu.VMEM((2, rows, LANES), F32), pltpu.VMEM((2, 16, cols), F32),
            pltpu.VMEM((rows, cols), F32), pltpu.VMEM((rows, cols), F32),
            pltpu.VMEM(student_txt.shape, jnp.bfloat16),
            pltpu.VMEM(student_img.shape, jnp.bfloat16),
            pltpu.VMEM((rows, cols), jnp.bfloat16), pltpu.VMEM(shape, F32),
            pltpu.VMEM(flow, F32), pltpu.VMEM((cols, thin), F32),
            pltpu.SemaphoreType.DMA((11 + pieces // 4,)),
        ],
        compiler_params=pltpu.CompilerParams(vmem_limit_bytes=VMEM_LIMIT),
        cost_estimate=cost(4 * rows * cols * thin, 8 * rows * cols, 4 * rows * cols),
    )(
        *row_parts, col_stats,
        *(
            pltpu.with_memory_space_constraint(x, pltpu.HBM)
            for x in (t, s, student_txt, student_img)
        ),
    )


def add_kernel(tops, mine, theirs, *refs):
    outs, near, sems = refs[: len(tops)], refs[len(tops) : -1], refs[-1]
    copies = []
    for k, (top, out) in enumerate(zip(tops, outs)):
        down = pl.ds(top, out.shape[0])
        copies.append(pltpu.make_async_copy(theirs.at[down, :], near[k], sems.at[k]))
        copies[-1].start()
    for k, (top, out) in enumerate(zip(tops, outs)):
        copies[k].wait()
        out[...] = mine[top : top + out.shape[0], :] + near[k][...]


def added(slots, mine, theirs, chips):
    thin = mine.shape[1]
    sizes = flow_rows(2 * (mine.shape[0] - 5 * NOTE) // chips)
    tops = [sum(sizes[:k]) for k in slots]
    return pl.pallas_call(
        functools.partial(add_kernel, tops),
        name="both_cores_text_terms",
        out_shape=[jax.ShapeDtypeStruct((sizes[k], thin), F32) for k in slots],
        in_specs=[WHOLE, FAR],
        out_specs=[WHOLE] * len(slots),
        scratch_shapes=[pltpu.VMEM((sizes[k], thin), F32) for k in slots]
        + [pltpu.SemaphoreType.DMA((len(slots),))],
        compiler_params=pltpu.CompilerParams(vmem_limit_bytes=8 * MIB),
        cost_estimate=cost(mine.size, 6 * mine.size),
    )(mine, pltpu.with_memory_space_constraint(theirs, pltpu.HBM))


def relay_kernel(near, full, *refs):
    out = refs[-1]
    out[...] = near[...] + full[...]
    if len(refs) > 1:
        part = refs[0]
        size = out.shape[0] - NOTE
        half = size // 2
        down = pl.ds(pl.multiple_of(lax.axis_index("img_1") * half, half), half)
        out[down, :] = out[down, :] + part[:half, :]
        out[size:, :] = out[size:, :] + part[half:, :]


def relayed(*parts):
    return pl.pallas_call(
        relay_kernel,
        name="relayed_text_terms",
        out_shape=jax.ShapeDtypeStruct(parts[0].shape, F32),
        in_specs=[WHOLE] * len(parts),
        out_specs=WHOLE,
        compiler_params=pltpu.CompilerParams(vmem_limit_bytes=4 * MIB),
        cost_estimate=cost(parts[0].size * 3, 12 * parts[0].size),
    )(*parts)


def finish_kernel(flow, other, own, out, note):
    half = out.shape[0]
    down = pl.ds(pl.multiple_of(lax.axis_index("img_1") * half, half), half)
    out[...] = flow[down, :] + other[down, :] + own[:half, :]
    note[...] = flow[2 * half :, :LANES] + other[2 * half :, :LANES] + own[half:, :LANES]


def finished(flow, other, own):
    thin = flow.shape[1]
    return pl.pallas_call(
        finish_kernel,
        name="text_gradient_total",
        out_shape=(
            jax.ShapeDtypeStruct((own.shape[0] - NOTE, thin), F32),
            jax.ShapeDtypeStruct((NOTE, LANES), F32),
        ),
        in_specs=[WHOLE] * 3,
        out_specs=(WHOLE, WHOLE),
        compiler_params=pltpu.CompilerParams(vmem_limit_bytes=4 * MIB),
        cost_estimate=cost(own.size * 3, 16 * own.size),
    )(flow, other, own)


def sum_kernel(row_share, col_share, parts, row_note, out, loss):
    own = out.shape[0]

    def total(down):
        return functools.reduce(jnp.add, [parts[k, down, :] for k in range(parts.shape[0])])

    for b in range(out.shape[1] // LANES):
        out[:, b * LANES : (b + 1) * LANES] = total(slice(b * own, (b + 1) * own))
    col_note = total(slice(parts.shape[1] - NOTE, parts.shape[1]))
    both = (0.5 * LN2) * (row_note[...] * row_share + col_note * col_share)
    loss[0, 0] = both[0, 0]


def summed(row_share, col_share, parts, row_note, thin):
    own = (parts.shape[1] - NOTE) * LANES // thin
    return pl.pallas_call(
        functools.partial(sum_kernel, row_share, col_share),
        name="sum_of_image_parts_and_loss",
        out_shape=(jax.ShapeDtypeStruct((own, thin), F32), jax.ShapeDtypeStruct((1, 1), F32)),
        in_specs=[WHOLE] * 2,
        out_specs=(WHOLE, pl.BlockSpec(memory_space=pltpu.SMEM)),
        compiler_params=pltpu.CompilerParams(vmem_limit_bytes=4 * MIB),
        cost_estimate=cost(parts.size, 4 * parts.size),
    )(parts, row_note)


def turn(size, step):
    return [(k, (k + step) % size) for k in range(size)]


def body(teacher_img, teacher_txt, student_img, student_txt):
    rows = student_img.shape[0]
    cols, thin = student_txt.shape
    chips, cores = lax.axis_size("img_0"), lax.axis_size("img_1")
    img_count, txt_count = chips * cores, lax.axis_size(TXT)
    side = lax.axis_size("txt_0")

    t, s, row, col = local_stats(
        teacher_img, teacher_txt, student_img, student_txt, 1
    )
    swap = turn(cores, 1)

    def neighbour(value, axis, first):
        pairs = [(k, (k + 1 - 2 * ((k + first) % 2)) % side) for k in range(side)]
        return lax.ppermute(value, axis, pairs)

    row, col = row[0], col[0]
    other = neighbour(row, TXT[0], 0)
    row, col = join(
        ((0, 1), (2, 3)), (1, chips), row, other, col, lax.ppermute(col, "img_1", swap)
    )
    col = lax.all_to_all(col, "img_0", 0, 0, tiled=True)
    for axis, first in ((TXT[0], 1), (TXT[1], 0)):
        row = row[0]
        (row,) = join(((0, 1),), (1,), row, neighbour(row, axis, first))
    row = row[0]
    other = neighbour(row, TXT[1], 1)

    to_img, theirs, mine = gradients(
        (row, other), col, t, s, student_txt, student_img, txt_count, chips
    )
    got_img = lax.all_to_all(to_img, TXT, 0, 0, tiled=True)
    theirs = lax.ppermute(theirs, "img_1", swap)
    three, four = added((1, 3), mine, theirs, chips)
    two, one, own = added((0, 2, 4), mine, theirs, chips)

    def outward(value, step):
        pairs = [
            (cores * z + c, cores * ((z + step * (1 - 2 * c)) % chips) + c)
            for z in range(chips) for c in range(cores)
        ]
        return lax.ppermute(value, IMG, pairs)

    four = outward(four, 2)
    flow = relayed(two, outward(three, 1), four)
    flow = relayed(one, outward(flow, 1))
    flow = outward(flow, 1)
    across = lax.ppermute(flow, "img_1", swap)
    grad_txt, row_total = finished(flow, across, own)
    grad_img, loss = summed(
        1.0 / (rows * img_count), 1.0 / (cols * txt_count), got_img, row_total, thin
    )
    return (loss.reshape(()), grad_img, grad_txt)


def solution(mesh):
    torus = Mesh(mesh.devices.reshape(8, 2, 4, 4), ("img_0", "img_1", "txt_0", "txt_1"))
    in_specs = (P(IMG, None), P(TXT, None), P(IMG, None), P(TXT, None))
    out_specs = (P(), P(IMG_TXT, None), P(TXT_IMG, None))
    return jax.shard_map(body, mesh=torus, in_specs=in_specs, out_specs=out_specs, check_vma=False)
```

```python
import functools
import math

import jax
import jax.numpy as jnp
from jax import lax
from jax.experimental import pallas as pl
from jax.experimental.pallas import tpu as pltpu
from jax.sharding import Mesh
from jax.sharding import PartitionSpec as P

IMG = ("img_0", "img_1")
TXT = ("txt_0", "txt_1")
IMG_TXT = ("img_0", "img_1", "txt_0", "txt_1")
TXT_IMG = ("txt_0", "txt_1", "img_0", "img_1")
LANES = 128
NOTE = 8
VMEM_LIMIT = 32 * 1024 * 1024
STATS_LIMIT = 32 * 1024 * 1024
LN2 = math.log(2.0)
F32 = jnp.float32
MIB = 1024 * 1024
WHOLE = pl.BlockSpec(memory_space=pltpu.VMEM)
FAR = pl.BlockSpec(memory_space=pltpu.HBM)


def cost(flops, size, transcendentals=0):
    return pl.CostEstimate(flops=flops, bytes_accessed=size, transcendentals=transcendentals)


def stats_kernel(scale_teach, scale_learn, ti_hbm, tt_hbm, si_hbm, st_hbm, t_hbm, s_hbm,
                 row_out, col_out, ti, tt, si, st, t, s, peaks, sums, col_peaks, col_sums, sems):
    rows, cols = t.shape
    tall = 256
    chunks = rows // tall

    def load(src, dst, at, size, which):
        copy = pltpu.make_async_copy(
            src.at[pl.ds(at, size), :], dst.at[pl.ds(at, size), :], sems.at[which]
        )
        copy.start()
        return copy

    st_load = load(st_hbm, st, 0, cols, 1 + chunks)
    si_load = load(si_hbm, si, 0, rows, 2 + chunks)
    tt_load = load(tt_hbm, tt, 0, cols, 0)

    saves = []

    def logits(left, right, out, far, scale, which, arrivals):
        for n in range(chunks):
            if arrivals:
                arrivals[n].wait()
            down = slice(n * tall, (n + 1) * tall)
            block = scale * lax.dot_general(
                left[down, :], right[...], (((1,), (1,)), ((), ())), preferred_element_type=F32
            )
            out[down, :] = block
            saves.append(load(out, far, n * tall, tall, sems.shape[0] - 1 - len(saves)))
            top = jnp.max(block.reshape(tall // 8, 8, cols), axis=0)
            col_peaks[which] = jnp.maximum(col_peaks[which], top) if n else top
            side = block[:, :LANES]
            for k in range(1, cols // LANES):
                side = jnp.maximum(side, block[:, k * LANES : (k + 1) * LANES])
            peaks[which, down, :] = jnp.broadcast_to(
                jnp.max(side, axis=1, keepdims=True), (tall, LANES)
            )
        col_peaks[which] = jnp.broadcast_to(
            jnp.max(col_peaks[which], axis=0, keepdims=True), (8, cols)
        )

    st_load.wait()
    si_load.wait()
    ti_loads = [load(ti_hbm, ti, n * tall, tall, 1 + n) for n in range(chunks)]
    logits(si, st, s, s_hbm, scale_learn, 1, None)
    tt_load.wait()
    logits(ti, tt, t, t_hbm, scale_teach, 0, ti_loads)

    group = 4 * LANES
    for h in range(cols // group):
        def strip(r, carry):
            at = pl.multiple_of(r * 8, 8)
            down = pl.ds(at, 8)
            row_peak_t, row_peak_s = peaks[0, down, :], peaks[1, down, :]
            row_t = row_s = row_g = None
            new = []
            for k in range(group // LANES):
                across = slice(h * group + k * LANES, h * group + (k + 1) * LANES)
                tv, sv = t[down, across], s[down, across]
                gap = tv - sv
                wr = jnp.exp2(tv - row_peak_t)
                vr = jnp.exp2(sv - row_peak_s)
                wc = jnp.exp2(tv - col_peaks[0, :, across])
                vc = jnp.exp2(sv - col_peaks[1, :, across])
                row_t = wr if row_t is None else row_t + wr
                row_s = vr if row_s is None else row_s + vr
                row_g = wr * gap if row_g is None else row_g + wr * gap
                ct, cs, cg = carry[3 * k : 3 * k + 3]
                new += [ct + wc, cs + vc, cg + wc * gap]
            for q, value in enumerate((row_t, row_s, row_g)):
                sums[q, down, :] = value + sums[q, down, :] if h else value
            return tuple(new)

        zeros = tuple(jnp.zeros((8, LANES), F32) for _ in range(3 * group // LANES))
        found = lax.fori_loop(0, rows // 8, strip, zeros, unroll=8)
        for k in range(group // LANES):
            across = slice(h * group + k * LANES, h * group + (k + 1) * LANES)
            for q in range(3):
                col_sums[q, :, across] = found[3 * k + q]

    def publish(out, peak_t, peak_s, mass_t, mass_s, gap):
        found = (peak_t + jnp.log2(mass_t), peak_s + jnp.log2(mass_s), gap / mass_t)
        for q, value in enumerate(found):
            for k in range(out.shape[0]):
                out[k, 8 * q : 8 * q + 8, :] = value

    def stacked(lines):
        return jnp.concatenate(lines, axis=0)

    def by_column(value):
        return stacked([value[:, b * LANES : (b + 1) * LANES] for b in range(cols // LANES)])

    publish(
        col_out, by_column(col_peaks[0, :1, :]), by_column(col_peaks[1, :1, :]),
        *(by_column(jnp.sum(col_sums[q], axis=0, keepdims=True)) for q in range(3)),
    )
    lane = lax.broadcasted_iota(jnp.int32, (rows, LANES), 1)
    packed = jnp.where(lane == 0, peaks[0], peaks[1])
    for q in range(3):
        packed = jnp.where(lane == 2 + q, jnp.sum(sums[q], axis=1, keepdims=True), packed)
    turned = [packed[b * LANES : (b + 1) * LANES, :].T for b in range(rows // LANES)]
    publish(row_out, *(stacked([block[q : q + 1, :] for block in turned]) for q in range(5)))
    for save in saves:
        save.wait()


def local_stats(teacher_img, teacher_txt, student_img, student_txt, copies):
    rows, deep = teacher_img.shape
    cols, thin = student_txt.shape
    kernel = functools.partial(
        stats_kernel, 3.0 / math.sqrt(deep) / LN2, 3.0 / math.sqrt(thin) / LN2
    )
    return pl.pallas_call(
        kernel,
        name="logits_and_statistics",
        out_shape=(
            pltpu.HBM((rows, cols), F32), pltpu.HBM((rows, cols), F32),
            jax.ShapeDtypeStruct((1, 3 * rows // LANES, LANES), F32),
            jax.ShapeDtypeStruct((copies, 3 * cols // LANES, LANES), F32),
        ),
        in_specs=[FAR] * 4,
        out_specs=(FAR, FAR, WHOLE, WHOLE),
        scratch_shapes=[
            pltpu.VMEM((rows, deep), jnp.bfloat16), pltpu.VMEM((cols, deep), jnp.bfloat16),
            pltpu.VMEM((rows, thin), jnp.bfloat16), pltpu.VMEM((cols, thin), jnp.bfloat16),
            pltpu.VMEM((rows, cols), F32), pltpu.VMEM((rows, cols), F32),
            pltpu.VMEM((2, rows, LANES), F32), pltpu.VMEM((3, rows, LANES), F32),
            pltpu.VMEM((2, 8, cols), F32), pltpu.VMEM((3, 8, cols), F32),
            pltpu.SemaphoreType.DMA((16,)),
        ],
        compiler_params=pltpu.CompilerParams(vmem_limit_bytes=STATS_LIMIT),
        cost_estimate=cost(2 * rows * cols * (deep + thin), 8 * rows * cols, 4 * rows * cols),
    )(*(
        pltpu.with_memory_space_constraint(x, pltpu.HBM)
        for x in (teacher_img, teacher_txt, student_img, student_txt)
    ))


def joined(parts):
    teach, learn, gap = ([part[8 * q : 8 * q + 8, :] for part in parts] for q in range(3))
    teach_peak = functools.reduce(jnp.maximum, teach)
    learn_peak = functools.reduce(jnp.maximum, learn)
    weights = [jnp.exp2(part - teach_peak) for part in teach]
    mass = sum(weights[1:], weights[0])
    shares = [jnp.exp2(part - learn_peak) for part in learn]
    gaps = [weight * part for weight, part in zip(weights, gap)]
    return (
        teach_peak + jnp.log2(mass),
        learn_peak + jnp.log2(sum(shares[1:], shares[0])),
        sum(gaps[1:], gaps[0]) / mass,
    )


def join_kernel(groups, *refs):
    sources, outs = refs[: len(refs) - len(groups)], refs[len(refs) - len(groups) :]
    for group, out in zip(groups, outs):
        for q, value in enumerate(joined([sources[k][...] for k in group])):
            for k in range(out.shape[0]):
                out[k, 8 * q : 8 * q + 8, :] = value


def join(groups, copies, *parts):
    return pl.pallas_call(
        functools.partial(join_kernel, groups),
        name="joined_statistics",
        out_shape=[
            jax.ShapeDtypeStruct((count, *parts[group[0]].shape), F32)
            for group, count in zip(groups, copies)
        ],
        in_specs=[WHOLE] * len(parts),
        out_specs=[WHOLE] * len(groups),
        compiler_params=pltpu.CompilerParams(vmem_limit_bytes=1 * MIB),
        cost_estimate=cost(parts[0].size * 20, parts[0].size * 4 * len(parts), parts[0].size * 4),
    )(*parts)


def delta_kernel(scale, *refs):
    row_parts = refs[:2]
    col_stats, t_far, s_far, st_far, si_far, img_out, theirs_out, mine = refs[2:10]
    row_norms, col_norms, t, s, st, si, delta, img_block, theirs, grads, sems = refs[10:]
    tall = 256
    arrivals = []
    for n in range(t.shape[0] // tall):
        down = pl.ds(n * tall, tall)
        arrivals.append([
            pltpu.make_async_copy(far.at[down, :], near.at[down, :], sems.at[2 + 2 * n + k])
            for k, (far, near) in enumerate(((t_far, t), (s_far, s)))
        ])
        for copy in arrivals[-1]:
            copy.start()
    loads = [
        pltpu.make_async_copy(src, dst, sems.at[k])
        for k, (src, dst) in enumerate(((st_far, st), (si_far, si)))
    ]
    for load in loads:
        load.start()
    rows, cols = t.shape
    thin = st.shape[1]
    row_teach, row_learn, row_mean = joined([part[...] for part in row_parts])
    col_teach, col_learn, col_mean = joined(
        [col_stats[k] for k in range(col_stats.shape[0])]
    )
    row_total = jnp.sum(row_mean + row_learn - row_teach)
    col_total = jnp.sum(col_mean + col_learn - col_teach)
    for which, (down, across) in enumerate(((row_teach, col_teach), (row_learn, col_learn))):
        turned = jnp.concatenate([down - 3.0] * (LANES // 8), axis=0).T
        for b in range(8):
            row_norms[which, b * LANES : (b + 1) * LANES, :] = jnp.broadcast_to(
                turned[:, b : b + 1], (LANES, LANES)
            )
            col_norms[which, :, b * LANES : (b + 1) * LANES] = jnp.broadcast_to(
                across[b : b + 1, :] - 3.0, (16, LANES)
            )

    def strip(r, carry):
        down = pl.ds(pl.multiple_of(r * 16, 16), 16)
        row_t, row_s = row_norms[0, down, :], row_norms[1, down, :]
        for k in range(cols // LANES):
            across = slice(k * LANES, (k + 1) * LANES)
            tv, sv = t[down, across], s[down, across]
            value = (
                jnp.exp2(sv - row_s) - jnp.exp2(tv - row_t)
                + jnp.exp2(sv - col_norms[1, :, across]) - jnp.exp2(tv - col_norms[0, :, across])
            )
            delta[down, across] = value.astype(jnp.bfloat16)
        return carry

    for n, copies in enumerate(arrivals):
        for copy in copies:
            copy.wait()
        lax.fori_loop(n * tall // 16, (n + 1) * tall // 16, strip, 0, unroll=2)
    for load in loads:
        load.wait()

    pieces, lines, _ = img_block.shape
    own = rows // pieces
    some = 4
    for k in range(pieces):
        img_block[k, lines - NOTE :, :] = jnp.full((NOTE, LANES), col_total, F32)
    saves = []
    for n in range(pieces // some):
        grad = scale * jnp.dot(
            delta[n * some * own : (n + 1) * some * own, :], st[...], preferred_element_type=F32
        )
        for k in range(some):
            for b in range(thin // LANES):
                img_block[n * some + k, b * own : (b + 1) * own, :] = grad[
                    k * own : (k + 1) * own, b * LANES : (b + 1) * LANES
                ]
        save = pltpu.make_async_copy(
            img_block.at[pl.ds(n * some, some)], img_out.at[pl.ds(n * some, some)], sems.at[10 + n]
        )
        save.start()
        saves.append(save)

    place, core = lax.axis_index("img_0"), lax.axis_index("img_1")
    chips = lax.axis_size("img_0")
    tall = cols // chips
    half = tall // 2
    full_note = jnp.full((NOTE, thin), row_total, F32)

    wide = 256
    for n in range(cols // wide):
        grads[n * wide : (n + 1) * wide, :] = scale * lax.dot_general(
            delta[:, n * wide : (n + 1) * wide], si[...], (((0,), (0,)), ((), ())),
            preferred_element_type=F32,
        )

    def text_block(out, top, far, part, note):
        size = tall if part is None else half
        at = lax.rem(place + far + chips, chips) * tall
        if part is not None:
            at = at + part * half
        out[top : top + size, :] = grads[pl.ds(pl.multiple_of(at, half), size), :]
        out[top + size : top + size + NOTE, :] = note

    for out, flow in ((theirs, 1 - core), (mine, core)):
        sign = 1 - 2 * flow
        top = 0
        for far, part, note in (
            (2 * sign, None, full_note), (3 * sign, None, full_note), (sign, None, full_note),
            (chips // 2, flow, 0.5 * full_note), (0, flow, full_note),
        ):
            text_block(out, top, far, part, note)
            top += (tall if part is None else half) + NOTE
        if out is theirs:
            save = pltpu.make_async_copy(theirs, theirs_out, sems.at[10 + len(saves)])
            save.start()
            saves.append(save)

    for save in saves:
        save.wait()


def flow_rows(tall):
    full, part = tall + NOTE, tall // 2 + NOTE
    return (full, full, full, part, part)


def gradients(row_parts, col_stats, t, s, student_txt, student_img, pieces, chips):
    rows, cols = t.shape
    thin = student_txt.shape[1]
    shape = (pieces, rows // pieces * thin // LANES + NOTE, LANES)
    flow = (sum(flow_rows(cols // chips)), thin)
    return pl.pallas_call(
        functools.partial(delta_kernel, 3.0 / math.sqrt(thin)),
        name="delta_and_gradients",
        out_shape=(pltpu.HBM(shape, F32), pltpu.HBM(flow, F32), jax.ShapeDtypeStruct(flow, F32)),
        in_specs=[WHOLE] * (len(row_parts) + 1) + [FAR] * 4,
        out_specs=(FAR, FAR, WHOLE),
        scratch_shapes=[
            pltpu.VMEM((2, rows, LANES), F32), pltpu.VMEM((2, 16, cols), F32),
            pltpu.VMEM((rows, cols), F32), pltpu.VMEM((rows, cols), F32),
            pltpu.VMEM(student_txt.shape, jnp.bfloat16),
            pltpu.VMEM(student_img.shape, jnp.bfloat16),
            pltpu.VMEM((rows, cols), jnp.bfloat16), pltpu.VMEM(shape, F32),
            pltpu.VMEM(flow, F32), pltpu.VMEM((cols, thin), F32),
            pltpu.SemaphoreType.DMA((11 + pieces // 4,)),
        ],
        compiler_params=pltpu.CompilerParams(vmem_limit_bytes=VMEM_LIMIT),
        cost_estimate=cost(4 * rows * cols * thin, 8 * rows * cols, 4 * rows * cols),
    )(
        *row_parts, col_stats,
        *(
            pltpu.with_memory_space_constraint(x, pltpu.HBM)
            for x in (t, s, student_txt, student_img)
        ),
    )


def add_kernel(mine, theirs, *outs):
    top = 0
    for out in outs:
        down = slice(top, top + out.shape[0])
        out[...] = mine[down, :] + theirs[down, :]
        top += out.shape[0]


def added(mine, theirs, chips):
    thin = mine.shape[1]
    sizes = flow_rows(2 * (mine.shape[0] - 5 * NOTE) // chips)
    return pl.pallas_call(
        add_kernel,
        name="both_cores_text_terms",
        out_shape=[jax.ShapeDtypeStruct((size, thin), F32) for size in sizes],
        in_specs=[WHOLE] * 2,
        out_specs=[WHOLE] * len(sizes),
        compiler_params=pltpu.CompilerParams(vmem_limit_bytes=8 * MIB),
        cost_estimate=cost(mine.size, 12 * mine.size),
    )(mine, theirs)


def relay_kernel(near, full, *refs):
    out = refs[-1]
    out[...] = near[...] + full[...]
    if len(refs) > 1:
        part = refs[0]
        size = out.shape[0] - NOTE
        half = size // 2
        down = pl.ds(pl.multiple_of(lax.axis_index("img_1") * half, half), half)
        out[down, :] = out[down, :] + part[:half, :]
        out[size:, :] = out[size:, :] + part[half:, :]


def relayed(*parts):
    return pl.pallas_call(
        relay_kernel,
        name="relayed_text_terms",
        out_shape=jax.ShapeDtypeStruct(parts[0].shape, F32),
        in_specs=[WHOLE] * len(parts),
        out_specs=WHOLE,
        compiler_params=pltpu.CompilerParams(vmem_limit_bytes=4 * MIB),
        cost_estimate=cost(parts[0].size * 3, 12 * parts[0].size),
    )(*parts)


def finish_kernel(one, two, own, out, note):
    half = out.shape[0]
    total = one[...] + two[...] + own[...]
    out[...] = total[:half, :]
    note[...] = total[half:, :LANES]


def finished(one, two, own):
    thin = own.shape[1]
    return pl.pallas_call(
        finish_kernel,
        name="text_gradient_total",
        out_shape=(
            jax.ShapeDtypeStruct((own.shape[0] - NOTE, thin), F32),
            jax.ShapeDtypeStruct((NOTE, LANES), F32),
        ),
        in_specs=[WHOLE] * 3,
        out_specs=(WHOLE, WHOLE),
        compiler_params=pltpu.CompilerParams(vmem_limit_bytes=4 * MIB),
        cost_estimate=cost(own.size * 3, 16 * own.size),
    )(one, two, own)


def part_kernel(near, full, same, cross):
    half = same.shape[0] - NOTE
    core = lax.axis_index("img_1")
    note = slice(2 * half, 2 * half + NOTE)
    for out, which in ((same, core), (cross, 1 - core)):
        down = pl.ds(pl.multiple_of(which * half, half), half)
        out[:half, :] = near[down, :] + full[down, :]
        out[half:, :] = near[note, :] + full[note, :]


def parted(near, full):
    part = jax.ShapeDtypeStruct(((near.shape[0] + NOTE) // 2, near.shape[1]), F32)
    return pl.pallas_call(
        part_kernel,
        name="parted_text_terms",
        out_shape=(part, part),
        in_specs=[WHOLE] * 2,
        out_specs=(WHOLE, WHOLE),
        compiler_params=pltpu.CompilerParams(vmem_limit_bytes=4 * MIB),
        cost_estimate=cost(near.size, 12 * near.size),
    )(near, full)


def sum_kernel(row_share, col_share, parts, row_note, out, loss):
    own = out.shape[0]

    def total(down):
        return functools.reduce(jnp.add, [parts[k, down, :] for k in range(parts.shape[0])])

    for b in range(out.shape[1] // LANES):
        out[:, b * LANES : (b + 1) * LANES] = total(slice(b * own, (b + 1) * own))
    col_note = total(slice(parts.shape[1] - NOTE, parts.shape[1]))
    both = (0.5 * LN2) * (row_note[...] * row_share + col_note * col_share)
    loss[0, 0] = both[0, 0]


def summed(row_share, col_share, parts, row_note, thin):
    own = (parts.shape[1] - NOTE) * LANES // thin
    return pl.pallas_call(
        functools.partial(sum_kernel, row_share, col_share),
        name="sum_of_image_parts_and_loss",
        out_shape=(jax.ShapeDtypeStruct((own, thin), F32), jax.ShapeDtypeStruct((1, 1), F32)),
        in_specs=[WHOLE] * 2,
        out_specs=(WHOLE, pl.BlockSpec(memory_space=pltpu.SMEM)),
        compiler_params=pltpu.CompilerParams(vmem_limit_bytes=4 * MIB),
        cost_estimate=cost(parts.size, 4 * parts.size),
    )(parts, row_note)


def turn(size, step):
    return [(k, (k + step) % size) for k in range(size)]


def body(teacher_img, teacher_txt, student_img, student_txt):
    rows = student_img.shape[0]
    cols, thin = student_txt.shape
    chips, cores = lax.axis_size("img_0"), lax.axis_size("img_1")
    img_count, txt_count = chips * cores, lax.axis_size(TXT)
    side = lax.axis_size("txt_0")

    t, s, row, col = local_stats(
        teacher_img, teacher_txt, student_img, student_txt, 1
    )
    swap = turn(cores, 1)

    def neighbour(value, axis, first):
        pairs = [(k, (k + 1 - 2 * ((k + first) % 2)) % side) for k in range(side)]
        return lax.ppermute(value, axis, pairs)

    row, col = row[0], col[0]
    other = neighbour(row, TXT[0], 0)
    row, col = join(
        ((0, 1), (2, 3)), (1, chips), row, other, col, lax.ppermute(col, "img_1", swap)
    )
    col = lax.all_to_all(col, "img_0", 0, 0, tiled=True)
    for axis, first in ((TXT[0], 1), (TXT[1], 0)):
        row = row[0]
        (row,) = join(((0, 1),), (1,), row, neighbour(row, axis, first))
    row = row[0]
    other = neighbour(row, TXT[1], 1)

    to_img, theirs, mine = gradients(
        (row, other), col, t, s, student_txt, student_img, txt_count, chips
    )
    got_img = lax.all_to_all(to_img, TXT, 0, 0, tiled=True)
    theirs = lax.ppermute(theirs, "img_1", swap)
    two, three, one, four, own = added(mine, theirs, chips)

    def outward(value, step, cross=0):
        pairs = [
            (cores * z + c, cores * ((z + step * (1 - 2 * c)) % chips) + (c + cross) % cores)
            for z in range(chips) for c in range(cores)
        ]
        return lax.ppermute(value, IMG, pairs)

    four = outward(four, 2)
    flow = relayed(two, outward(three, 1), four)
    same, cross = parted(one, outward(flow, 1))
    grad_txt, row_total = finished(outward(same, 1), outward(cross, 1, 1), own)
    grad_img, loss = summed(
        1.0 / (rows * img_count), 1.0 / (cols * txt_count), got_img, row_total, thin
    )
    return (loss.reshape(()), grad_img, grad_txt)


def solution(mesh):
    torus = Mesh(mesh.devices.reshape(8, 2, 4, 4), ("img_0", "img_1", "txt_0", "txt_1"))
    in_specs = (P(IMG, None), P(TXT, None), P(IMG, None), P(TXT, None))
    out_specs = (P(), P(IMG_TXT, None), P(TXT_IMG, None))
    return jax.shard_map(body, mesh=torus, in_specs=in_specs, out_specs=out_specs, check_vma=False)
```

```python
import functools
import math

import jax
import jax.numpy as jnp
from jax import lax
from jax.experimental import pallas as pl
from jax.experimental.pallas import tpu as pltpu
from jax.sharding import Mesh
from jax.sharding import PartitionSpec as P

IMG = ("img_0", "img_1")
TXT = ("txt_0", "txt_1")
IMG_TXT = ("img_0", "img_1", "txt_0", "txt_1")
TXT_IMG = ("txt_0", "txt_1", "img_0", "img_1")
LANES = 128
NOTE = 8
VMEM_LIMIT = 32 * 1024 * 1024
STATS_LIMIT = 32 * 1024 * 1024
LN2 = math.log(2.0)
F32 = jnp.float32
MIB = 1024 * 1024
WHOLE = pl.BlockSpec(memory_space=pltpu.VMEM)
FAR = pl.BlockSpec(memory_space=pltpu.HBM)


def cost(flops, size, transcendentals=0):
    return pl.CostEstimate(flops=flops, bytes_accessed=size, transcendentals=transcendentals)


def stats_kernel(scale_teach, scale_learn, ti_hbm, tt_hbm, si_hbm, st_hbm, t_hbm, s_hbm,
                 row_out, col_out, ti, tt, si, st, t, s, peaks, sums, col_peaks, col_sums, sems):
    rows, cols = t.shape
    tall = 256
    chunks = rows // tall

    def load(src, dst, at, size, which):
        copy = pltpu.make_async_copy(
            src.at[pl.ds(at, size), :], dst.at[pl.ds(at, size), :], sems.at[which]
        )
        copy.start()
        return copy

    st_load = load(st_hbm, st, 0, cols, 1 + chunks)
    si_load = load(si_hbm, si, 0, rows, 2 + chunks)
    tt_load = load(tt_hbm, tt, 0, cols, 0)

    saves = []

    def logits(left, right, out, far, scale, which, arrivals):
        for n in range(chunks):
            if arrivals:
                arrivals[n].wait()
            down = slice(n * tall, (n + 1) * tall)
            block = scale * lax.dot_general(
                left[down, :], right[...], (((1,), (1,)), ((), ())), preferred_element_type=F32
            )
            out[down, :] = block
            saves.append(load(out, far, n * tall, tall, sems.shape[0] - 1 - len(saves)))
            top = jnp.max(block.reshape(tall // 8, 8, cols), axis=0)
            col_peaks[which] = jnp.maximum(col_peaks[which], top) if n else top
            side = block[:, :LANES]
            for k in range(1, cols // LANES):
                side = jnp.maximum(side, block[:, k * LANES : (k + 1) * LANES])
            peaks[which, down, :] = jnp.broadcast_to(
                jnp.max(side, axis=1, keepdims=True), (tall, LANES)
            )
        col_peaks[which] = jnp.broadcast_to(
            jnp.max(col_peaks[which], axis=0, keepdims=True), (8, cols)
        )

    st_load.wait()
    si_load.wait()
    ti_loads = [load(ti_hbm, ti, n * tall, tall, 1 + n) for n in range(chunks)]
    logits(si, st, s, s_hbm, scale_learn, 1, None)
    tt_load.wait()
    logits(ti, tt, t, t_hbm, scale_teach, 0, ti_loads)

    group = 4 * LANES
    for h in range(cols // group):
        def strip(r, carry):
            at = pl.multiple_of(r * 8, 8)
            down = pl.ds(at, 8)
            row_peak_t, row_peak_s = peaks[0, down, :], peaks[1, down, :]
            row_t = row_s = row_g = None
            new = []
            for k in range(group // LANES):
                across = slice(h * group + k * LANES, h * group + (k + 1) * LANES)
                tv, sv = t[down, across], s[down, across]
                gap = tv - sv
                wr = jnp.exp2(tv - row_peak_t)
                vr = jnp.exp2(sv - row_peak_s)
                wc = jnp.exp2(tv - col_peaks[0, :, across])
                vc = jnp.exp2(sv - col_peaks[1, :, across])
                row_t = wr if row_t is None else row_t + wr
                row_s = vr if row_s is None else row_s + vr
                row_g = wr * gap if row_g is None else row_g + wr * gap
                ct, cs, cg = carry[3 * k : 3 * k + 3]
                new += [ct + wc, cs + vc, cg + wc * gap]
            for q, value in enumerate((row_t, row_s, row_g)):
                sums[q, down, :] = value + sums[q, down, :] if h else value
            return tuple(new)

        zeros = tuple(jnp.zeros((8, LANES), F32) for _ in range(3 * group // LANES))
        found = lax.fori_loop(0, rows // 8, strip, zeros, unroll=8)
        for k in range(group // LANES):
            across = slice(h * group + k * LANES, h * group + (k + 1) * LANES)
            for q in range(3):
                col_sums[q, :, across] = found[3 * k + q]

    def publish(out, peak_t, peak_s, mass_t, mass_s, gap):
        found = (peak_t + jnp.log2(mass_t), peak_s + jnp.log2(mass_s), gap / mass_t)
        for q, value in enumerate(found):
            for k in range(out.shape[0]):
                out[k, 8 * q : 8 * q + 8, :] = value

    def stacked(lines):
        return jnp.concatenate(lines, axis=0)

    def by_column(value):
        return stacked([value[:, b * LANES : (b + 1) * LANES] for b in range(cols // LANES)])

    publish(
        col_out, by_column(col_peaks[0, :1, :]), by_column(col_peaks[1, :1, :]),
        *(by_column(jnp.sum(col_sums[q], axis=0, keepdims=True)) for q in range(3)),
    )
    lane = lax.broadcasted_iota(jnp.int32, (rows, LANES), 1)
    packed = jnp.where(lane == 0, peaks[0], peaks[1])
    for q in range(3):
        packed = jnp.where(lane == 2 + q, jnp.sum(sums[q], axis=1, keepdims=True), packed)
    turned = [packed[b * LANES : (b + 1) * LANES, :].T for b in range(rows // LANES)]
    publish(row_out, *(stacked([block[q : q + 1, :] for block in turned]) for q in range(5)))
    for save in saves:
        save.wait()


def local_stats(teacher_img, teacher_txt, student_img, student_txt, copies):
    rows, deep = teacher_img.shape
    cols, thin = student_txt.shape
    kernel = functools.partial(
        stats_kernel, 3.0 / math.sqrt(deep) / LN2, 3.0 / math.sqrt(thin) / LN2
    )
    return pl.pallas_call(
        kernel,
        name="logits_and_statistics",
        out_shape=(
            pltpu.HBM((rows, cols), F32), pltpu.HBM((rows, cols), F32),
            jax.ShapeDtypeStruct((1, 3 * rows // LANES, LANES), F32),
            jax.ShapeDtypeStruct((copies, 3 * cols // LANES, LANES), F32),
        ),
        in_specs=[FAR] * 4,
        out_specs=(FAR, FAR, WHOLE, WHOLE),
        scratch_shapes=[
            pltpu.VMEM((rows, deep), jnp.bfloat16), pltpu.VMEM((cols, deep), jnp.bfloat16),
            pltpu.VMEM((rows, thin), jnp.bfloat16), pltpu.VMEM((cols, thin), jnp.bfloat16),
            pltpu.VMEM((rows, cols), F32), pltpu.VMEM((rows, cols), F32),
            pltpu.VMEM((2, rows, LANES), F32), pltpu.VMEM((3, rows, LANES), F32),
            pltpu.VMEM((2, 8, cols), F32), pltpu.VMEM((3, 8, cols), F32),
            pltpu.SemaphoreType.DMA((16,)),
        ],
        compiler_params=pltpu.CompilerParams(vmem_limit_bytes=STATS_LIMIT),
        cost_estimate=cost(2 * rows * cols * (deep + thin), 8 * rows * cols, 4 * rows * cols),
    )(*(
        pltpu.with_memory_space_constraint(x, pltpu.HBM)
        for x in (teacher_img, teacher_txt, student_img, student_txt)
    ))


def joined(parts):
    teach, learn, gap = ([part[8 * q : 8 * q + 8, :] for part in parts] for q in range(3))
    teach_peak = functools.reduce(jnp.maximum, teach)
    learn_peak = functools.reduce(jnp.maximum, learn)
    weights = [jnp.exp2(part - teach_peak) for part in teach]
    mass = sum(weights[1:], weights[0])
    shares = [jnp.exp2(part - learn_peak) for part in learn]
    gaps = [weight * part for weight, part in zip(weights, gap)]
    return (
        teach_peak + jnp.log2(mass),
        learn_peak + jnp.log2(sum(shares[1:], shares[0])),
        sum(gaps[1:], gaps[0]) / mass,
    )


def join_kernel(groups, *refs):
    sources, outs = refs[: len(refs) - len(groups)], refs[len(refs) - len(groups) :]
    for group, out in zip(groups, outs):
        for q, value in enumerate(joined([sources[k][...] for k in group])):
            for k in range(out.shape[0]):
                out[k, 8 * q : 8 * q + 8, :] = value


def join(groups, copies, *parts):
    return pl.pallas_call(
        functools.partial(join_kernel, groups),
        name="joined_statistics",
        out_shape=[
            jax.ShapeDtypeStruct((count, *parts[group[0]].shape), F32)
            for group, count in zip(groups, copies)
        ],
        in_specs=[WHOLE] * len(parts),
        out_specs=[WHOLE] * len(groups),
        compiler_params=pltpu.CompilerParams(vmem_limit_bytes=1 * MIB),
        cost_estimate=cost(parts[0].size * 20, parts[0].size * 4 * len(parts), parts[0].size * 4),
    )(*parts)


def delta_kernel(scale, *refs):
    row_parts = refs[:2]
    col_stats, t_far, s_far, st_far, si_far, img_out, theirs_out, mine = refs[2:10]
    row_norms, col_norms, t, s, st, si, delta, img_block, theirs, grads, sems = refs[10:]
    tall = 256
    arrivals = []
    for n in range(t.shape[0] // tall):
        down = pl.ds(n * tall, tall)
        arrivals.append([
            pltpu.make_async_copy(far.at[down, :], near.at[down, :], sems.at[2 + 2 * n + k])
            for k, (far, near) in enumerate(((t_far, t), (s_far, s)))
        ])
        for copy in arrivals[-1]:
            copy.start()
    loads = [
        pltpu.make_async_copy(src, dst, sems.at[k])
        for k, (src, dst) in enumerate(((st_far, st), (si_far, si)))
    ]
    for load in loads:
        load.start()
    rows, cols = t.shape
    thin = st.shape[1]
    row_teach, row_learn, row_mean = joined([part[...] for part in row_parts])
    col_teach, col_learn, col_mean = joined(
        [col_stats[k] for k in range(col_stats.shape[0])]
    )
    row_total = jnp.sum(row_mean + row_learn - row_teach)
    col_total = jnp.sum(col_mean + col_learn - col_teach)
    for which, (down, across) in enumerate(((row_teach, col_teach), (row_learn, col_learn))):
        turned = jnp.concatenate([down - 3.0] * (LANES // 8), axis=0).T
        for b in range(8):
            row_norms[which, b * LANES : (b + 1) * LANES, :] = jnp.broadcast_to(
                turned[:, b : b + 1], (LANES, LANES)
            )
            col_norms[which, :, b * LANES : (b + 1) * LANES] = jnp.broadcast_to(
                across[b : b + 1, :] - 3.0, (16, LANES)
            )

    def strip(r, carry):
        down = pl.ds(pl.multiple_of(r * 16, 16), 16)
        row_t, row_s = row_norms[0, down, :], row_norms[1, down, :]
        for k in range(cols // LANES):
            across = slice(k * LANES, (k + 1) * LANES)
            tv, sv = t[down, across], s[down, across]
            value = (
                jnp.exp2(sv - row_s) - jnp.exp2(tv - row_t)
                + jnp.exp2(sv - col_norms[1, :, across]) - jnp.exp2(tv - col_norms[0, :, across])
            )
            delta[down, across] = value.astype(jnp.bfloat16)
        return carry

    for n, copies in enumerate(arrivals):
        for copy in copies:
            copy.wait()
        lax.fori_loop(n * tall // 16, (n + 1) * tall // 16, strip, 0, unroll=2)
    for load in loads:
        load.wait()

    pieces, lines, _ = img_block.shape
    own = rows // pieces
    some = 4
    for k in range(pieces):
        img_block[k, lines - NOTE :, :] = jnp.full((NOTE, LANES), col_total, F32)
    saves = []
    for n in range(pieces // some):
        grad = scale * jnp.dot(
            delta[n * some * own : (n + 1) * some * own, :], st[...], preferred_element_type=F32
        )
        for k in range(some):
            for b in range(thin // LANES):
                img_block[n * some + k, b * own : (b + 1) * own, :] = grad[
                    k * own : (k + 1) * own, b * LANES : (b + 1) * LANES
                ]
        save = pltpu.make_async_copy(
            img_block.at[pl.ds(n * some, some)], img_out.at[pl.ds(n * some, some)], sems.at[10 + n]
        )
        save.start()
        saves.append(save)

    place, core = lax.axis_index("img_0"), lax.axis_index("img_1")
    chips = lax.axis_size("img_0")
    tall = cols // chips
    half = tall // 2
    full_note = jnp.full((NOTE, thin), row_total, F32)

    wide = 256
    for n in range(cols // wide):
        grads[n * wide : (n + 1) * wide, :] = scale * lax.dot_general(
            delta[:, n * wide : (n + 1) * wide], si[...], (((0,), (0,)), ((), ())),
            preferred_element_type=F32,
        )

    def text_block(out, top, far, part, note):
        size = tall if part is None else half
        at = lax.rem(place + far + chips, chips) * tall
        if part is not None:
            at = at + part * half
        out[top : top + size, :] = grads[pl.ds(pl.multiple_of(at, half), size), :]
        out[top + size : top + size + NOTE, :] = note

    for out, flow in ((theirs, 1 - core), (mine, core)):
        sign = 1 - 2 * flow
        top = 0
        for far, part, note in (
            (2 * sign, None, full_note), (3 * sign, None, full_note), (sign, None, full_note),
            (chips // 2, flow, 0.5 * full_note), (0, flow, full_note),
        ):
            text_block(out, top, far, part, note)
            top += (tall if part is None else half) + NOTE
        if out is theirs:
            save = pltpu.make_async_copy(theirs, theirs_out, sems.at[10 + len(saves)])
            save.start()
            saves.append(save)

    for save in saves:
        save.wait()


def flow_rows(tall):
    full, part = tall + NOTE, tall // 2 + NOTE
    return (full, full, full, part, part)


def gradients(row_parts, col_stats, t, s, student_txt, student_img, pieces, chips):
    rows, cols = t.shape
    thin = student_txt.shape[1]
    shape = (pieces, rows // pieces * thin // LANES + NOTE, LANES)
    flow = (sum(flow_rows(cols // chips)), thin)
    return pl.pallas_call(
        functools.partial(delta_kernel, 3.0 / math.sqrt(thin)),
        name="delta_and_gradients",
        out_shape=(pltpu.HBM(shape, F32), pltpu.HBM(flow, F32), jax.ShapeDtypeStruct(flow, F32)),
        in_specs=[WHOLE] * (len(row_parts) + 1) + [FAR] * 4,
        out_specs=(FAR, FAR, WHOLE),
        scratch_shapes=[
            pltpu.VMEM((2, rows, LANES), F32), pltpu.VMEM((2, 16, cols), F32),
            pltpu.VMEM((rows, cols), F32), pltpu.VMEM((rows, cols), F32),
            pltpu.VMEM(student_txt.shape, jnp.bfloat16),
            pltpu.VMEM(student_img.shape, jnp.bfloat16),
            pltpu.VMEM((rows, cols), jnp.bfloat16), pltpu.VMEM(shape, F32),
            pltpu.VMEM(flow, F32), pltpu.VMEM((cols, thin), F32),
            pltpu.SemaphoreType.DMA((11 + pieces // 4,)),
        ],
        compiler_params=pltpu.CompilerParams(vmem_limit_bytes=VMEM_LIMIT),
        cost_estimate=cost(4 * rows * cols * thin, 8 * rows * cols, 4 * rows * cols),
    )(
        *row_parts, col_stats,
        *(
            pltpu.with_memory_space_constraint(x, pltpu.HBM)
            for x in (t, s, student_txt, student_img)
        ),
    )


def add_kernel(mine, theirs, *outs):
    top = 0
    for out in outs:
        down = slice(top, top + out.shape[0])
        out[...] = mine[down, :] + theirs[down, :]
        top += out.shape[0]


def added(mine, theirs, chips):
    thin = mine.shape[1]
    sizes = flow_rows(2 * (mine.shape[0] - 5 * NOTE) // chips)
    return pl.pallas_call(
        add_kernel,
        name="both_cores_text_terms",
        out_shape=[jax.ShapeDtypeStruct((size, thin), F32) for size in sizes],
        in_specs=[WHOLE] * 2,
        out_specs=[WHOLE] * len(sizes),
        compiler_params=pltpu.CompilerParams(vmem_limit_bytes=8 * MIB),
        cost_estimate=cost(mine.size, 12 * mine.size),
    )(mine, theirs)


def relay_kernel(near, full, *refs):
    out = refs[-1]
    out[...] = near[...] + full[...]
    if len(refs) > 1:
        part = refs[0]
        size = out.shape[0] - NOTE
        half = size // 2
        down = pl.ds(pl.multiple_of(lax.axis_index("img_1") * half, half), half)
        out[down, :] = out[down, :] + part[:half, :]
        out[size:, :] = out[size:, :] + part[half:, :]


def relayed(*parts):
    return pl.pallas_call(
        relay_kernel,
        name="relayed_text_terms",
        out_shape=jax.ShapeDtypeStruct(parts[0].shape, F32),
        in_specs=[WHOLE] * len(parts),
        out_specs=WHOLE,
        compiler_params=pltpu.CompilerParams(vmem_limit_bytes=4 * MIB),
        cost_estimate=cost(parts[0].size * 3, 12 * parts[0].size),
    )(*parts)


def part_kernel(near, full, same, cross):
    half = same.shape[0] - NOTE
    core = lax.axis_index("img_1")
    note = slice(2 * half, 2 * half + NOTE)
    for out, which in ((same, core), (cross, 1 - core)):
        down = pl.ds(pl.multiple_of(which * half, half), half)
        out[:half, :] = near[down, :] + full[down, :]
        out[half:, :] = near[note, :] + full[note, :]


def parted(near, full):
    part = jax.ShapeDtypeStruct(((near.shape[0] + NOTE) // 2, near.shape[1]), F32)
    return pl.pallas_call(
        part_kernel,
        name="parted_text_terms",
        out_shape=(part, part),
        in_specs=[WHOLE] * 2,
        out_specs=(WHOLE, WHOLE),
        compiler_params=pltpu.CompilerParams(vmem_limit_bytes=4 * MIB),
        cost_estimate=cost(near.size, 12 * near.size),
    )(near, full)


def totals_kernel(row_share, col_share, one, two, own, parts, txt_out, img_out, loss):
    half = txt_out.shape[0]
    text = one[...] + two[...] + own[...]
    txt_out[...] = text[:half, :]
    size = img_out.shape[0]

    def total(down):
        return functools.reduce(jnp.add, [parts[k, down, :] for k in range(parts.shape[0])])

    for b in range(img_out.shape[1] // LANES):
        img_out[:, b * LANES : (b + 1) * LANES] = total(slice(b * size, (b + 1) * size))
    col_note = total(slice(parts.shape[1] - NOTE, parts.shape[1]))
    both = (0.5 * LN2) * (text[half:, :LANES] * row_share + col_note * col_share)
    loss[0, 0] = both[0, 0]


def totals(row_share, col_share, one, two, own, parts):
    thin = own.shape[1]
    size = (parts.shape[1] - NOTE) * LANES // thin
    return pl.pallas_call(
        functools.partial(totals_kernel, row_share, col_share),
        name="gradient_totals_and_loss",
        out_shape=(
            jax.ShapeDtypeStruct((own.shape[0] - NOTE, thin), F32),
            jax.ShapeDtypeStruct((size, thin), F32),
            jax.ShapeDtypeStruct((1, 1), F32),
        ),
        in_specs=[WHOLE] * 4,
        out_specs=(WHOLE, WHOLE, pl.BlockSpec(memory_space=pltpu.SMEM)),
        compiler_params=pltpu.CompilerParams(vmem_limit_bytes=5 * MIB),
        cost_estimate=cost(parts.size + own.size * 3, 4 * parts.size + 16 * own.size),
    )(one, two, own, parts)


def turn(size, step):
    return [(k, (k + step) % size) for k in range(size)]


def body(teacher_img, teacher_txt, student_img, student_txt):
    rows = student_img.shape[0]
    cols, thin = student_txt.shape
    chips, cores = lax.axis_size("img_0"), lax.axis_size("img_1")
    img_count, txt_count = chips * cores, lax.axis_size(TXT)
    side = lax.axis_size("txt_0")

    t, s, row, col = local_stats(
        teacher_img, teacher_txt, student_img, student_txt, 1
    )
    swap = turn(cores, 1)

    def neighbour(value, axis, first):
        pairs = [(k, (k + 1 - 2 * ((k + first) % 2)) % side) for k in range(side)]
        return lax.ppermute(value, axis, pairs)

    row, col = row[0], col[0]
    other = neighbour(row, TXT[0], 0)
    row, col = join(
        ((0, 1), (2, 3)), (1, chips), row, other, col, lax.ppermute(col, "img_1", swap)
    )
    col = lax.all_to_all(col, "img_0", 0, 0, tiled=True)
    for axis, first in ((TXT[0], 1), (TXT[1], 0)):
        row = row[0]
        (row,) = join(((0, 1),), (1,), row, neighbour(row, axis, first))
    row = row[0]
    other = neighbour(row, TXT[1], 1)

    to_img, theirs, mine = gradients(
        (row, other), col, t, s, student_txt, student_img, txt_count, chips
    )
    got_img = lax.all_to_all(to_img, TXT, 0, 0, tiled=True)
    theirs = lax.ppermute(theirs, "img_1", swap)
    two, three, one, four, own = added(mine, theirs, chips)

    def outward(value, step, cross=0):
        pairs = [
            (cores * z + c, cores * ((z + step * (1 - 2 * c)) % chips) + (c + cross) % cores)
            for z in range(chips) for c in range(cores)
        ]
        return lax.ppermute(value, IMG, pairs)

    four = outward(four, 2)
    flow = relayed(two, outward(three, 1), four)
    same, cross = parted(one, outward(flow, 1))
    grad_txt, grad_img, loss = totals(
        1.0 / (rows * img_count), 1.0 / (cols * txt_count),
        outward(same, 1), outward(cross, 1, 1), own, got_img,
    )
    return (loss.reshape(()), grad_img, grad_txt)


def solution(mesh):
    torus = Mesh(mesh.devices.reshape(8, 2, 4, 4), ("img_0", "img_1", "txt_0", "txt_1"))
    in_specs = (P(IMG, None), P(TXT, None), P(IMG, None), P(TXT, None))
    out_specs = (P(), P(IMG_TXT, None), P(TXT_IMG, None))
    return jax.shard_map(body, mesh=torus, in_specs=in_specs, out_specs=out_specs, check_vma=False)
```
